32 devices in a mesh: modes: 8 (over z, y), grid: 4 (over x, core).
Axes of the slice: x: 2, y: 2, z: 4, core: 2. Of those that a mesh axis runs over, the one named last changes fastest.
Arguments:
- u_modes: float32 [8, 2, 64, 1024], P('modes', None, 'grid'), may hold values from -5 to 5
- v_modes: float32 [8, 2, 64, 1024], P('modes', None, 'grid'), may hold values from -0.85 to 0.85
- potential: float32 [64, 1024], P('grid'), may hold values from -1.5 to 0
- pairing: float32 [2, 64, 1024], P(None, 'grid'), may hold values from -1 to 1
Outputs:
- u_next: float32 [8, 2, 64, 1024], P('modes', None, 'grid')
- v_next: float32 [8, 2, 64, 1024], P('modes', None, 'grid')
- fields: float32 [4, 64, 1024], P(None, 'grid')
The draws below stay inside these ranges and needn't reach their ends.
All inputs are finite; a program needn't handle non-finite values.
Results may differ from the reference program's by a relative error of at most 0.00035.
Values sent between devices are 32-bit elements; how exact they have to be, the bound alone decides.
No kernel may reach another device: no remote copies, remote signals or barrier semaphores. Data moves between devices by JAX's collectives and lax.ppermute only.
A program may use at most 64 MiB of HBM per device.

```python
import jax
import jax.numpy as jnp
from jax import lax

MODE_DEV = 1
NX = 32
NY = 32
NZ = 64
NXY = 1024
MODES = 8
N_MODES = 8


def mode_pair(key):
    base_key = jax.random.fold_in(key, 11)
    first_key, mixing_key, jitter_key = jax.random.split(base_key, 3)
    full_shape = (MODES, 2, NZ, NX * NY)
    upper = jax.random.truncated_normal(first_key, -5.0, 5.0, full_shape, jnp.float32)
    mixing = jax.random.uniform(mixing_key, full_shape, jnp.float32, 0.02, 0.06)
    jitter = 0.1 * jax.random.truncated_normal(jitter_key, -5.0, 5.0, full_shape, jnp.float32)
    return (upper, mixing * upper + jitter)


def draw_u_modes(key, part):
    return mode_pair(key)[0]


def draw_v_modes(key, part):
    return mode_pair(key)[1]


def level_of(key, extent, pieces, smallest, largest):
    factor_of, own = 1.0, jax.random.fold_in(key, 6)
    for dim, blocks in pieces:
        steps = jnp.exp(jax.random.uniform(jax.random.fold_in(own, dim), (blocks,), jnp.float32, smallest / len(pieces), largest / len(pieces)))
        factor_of = factor_of * jnp.repeat(steps, extent[dim] // blocks).reshape([-1 if axis == dim else 1 for axis in range(len(extent))])
    return factor_of


def setup_inputs(seed: int = 0) -> dict:
    keys = jax.random.split(jax.random.key(seed), 5)
    return {
        "u_modes": draw_u_modes(jax.random.fold_in(keys[4], 71), 0),
        "v_modes": draw_v_modes(jax.random.fold_in(keys[4], 71), 0),
        "potential": jnp.clip(-1.5 + 1.5 * jax.random.uniform(keys[2], (NZ, NXY), jnp.float32) ** level_of(keys[2], (NZ, NXY), ((0, 4),), -0.2, 0.2), -1.5, 0.0),
        "pairing": jnp.clip(jax.random.uniform(keys[3], (2, NZ, NXY), jnp.float32, -1.0, 1.0) * level_of(keys[3], (2, NZ, NXY), ((1, 4),), -0.4, 0.0), -1.0, 1.0),
    }


stencil_coef = (-205.0 / 72.0, 8.0 / 5.0, -1.0 / 5.0, 8.0 / 315.0, -1.0 / 560.0)
alpha_coef = 1.14
beta_coef = -0.553
gamma_coef = -11.11
time_step = 0.18
epsilon = 1e-6


def laplace_ref(states):
    shaped = states.reshape(states.shape[:3] + (NY, NX))
    total = 3.0 * stencil_coef[0] * shaped
    for offset in range(1, 5):
        for axis_num in (2, 3, 4):
            total = total + stencil_coef[offset] * (jnp.roll(shaped, offset, axis_num) + jnp.roll(shaped, -offset, axis_num))
    return total.reshape(states.shape)


def slopes(states, laplace, field_pot, pair_re, pair_im):
    kinetic = -0.5 * alpha_coef * laplace + field_pot * states
    upper_re = kinetic[:, 0] + pair_re * states[:, 2] - pair_im * states[:, 3]
    upper_im = kinetic[:, 1] + pair_re * states[:, 3] + pair_im * states[:, 2]
    lower_re = pair_re * states[:, 0] + pair_im * states[:, 1] - kinetic[:, 2]
    lower_im = pair_re * states[:, 1] - pair_im * states[:, 0] - kinetic[:, 3]
    return jnp.stack([upper_im, -upper_re, lower_im, -lower_re], axis=1)


def potentials(raw_sums, modes_total):
    density = 2.0 * raw_sums[0] / modes_total
    kinetic = -2.0 * raw_sums[1] / modes_total
    anomal_re = raw_sums[2] / modes_total
    anomal_im = raw_sums[3] / modes_total
    dense_safe = density + epsilon
    fermi = 0.5 * jnp.power(3.0 * jnp.pi ** 2 * dense_safe, 2.0 / 3.0)
    anomal_sq = anomal_re * anomal_re + anomal_im * anomal_im
    third_root = jnp.power(dense_safe, -1.0 / 3.0)
    field_pot = beta_coef * fermi - (gamma_coef / 3.0) * anomal_sq * third_root / dense_safe
    pair_re = -gamma_coef * anomal_re * third_root
    pair_im = -gamma_coef * anomal_im * third_root
    energy = alpha_coef * kinetic / 2.0 + 0.6 * beta_coef * dense_safe * fermi + gamma_coef * anomal_sq * third_root
    return jnp.stack([field_pot, pair_re, pair_im, energy], axis=0)


def reference(u_modes, v_modes, potential, pairing):
    u_blocks = u_modes.reshape((N_MODES, MODE_DEV) + u_modes.shape[1:])
    v_blocks = v_modes.reshape((N_MODES, MODE_DEV) + v_modes.shape[1:])

    def evolve(pair_in):
        start_state = jnp.concatenate([pair_in[0], pair_in[1]], axis=1)

        def slope_at(states):
            return slopes(states, laplace_ref(states), potential, pairing[0], pairing[1])

        slope_one = slope_at(start_state)
        slope_two = slope_at(start_state + 0.5 * time_step * slope_one)
        slope_three = slope_at(start_state + 0.5 * time_step * slope_two)
        slope_four = slope_at(start_state + time_step * slope_three)
        return start_state + (time_step / 6.0) * (slope_one + 2.0 * slope_two + 2.0 * slope_three + slope_four)

    stepped_all = lax.map(evolve, (u_blocks, v_blocks))

    def add_sums(running, stepped):
        lap_step = laplace_ref(stepped)
        partial_value = jnp.stack([
            jnp.sum(stepped[:, 2] * stepped[:, 2] + stepped[:, 3] * stepped[:, 3], axis=0),
            jnp.sum(stepped[:, 2] * lap_step[:, 2] + stepped[:, 3] * lap_step[:, 3], axis=0),
            jnp.sum(stepped[:, 0] * stepped[:, 2] + stepped[:, 1] * stepped[:, 3], axis=0),
            jnp.sum(stepped[:, 1] * stepped[:, 2] - stepped[:, 0] * stepped[:, 3], axis=0),
        ], axis=0)
        return running + partial_value, None

    zero_sums = jnp.zeros((4,) + potential.shape, jnp.float32)
    raw_sums, unused = lax.scan(add_sums, zero_sums, stepped_all)
    fields = potentials(raw_sums, float(MODES))

    def advance(stepped):
        lap_step = laplace_ref(stepped)
        next_one = slopes(stepped, lap_step, fields[0], fields[1], fields[2])
        middle = stepped + 0.5 * time_step * next_one
        next_two = slopes(middle, laplace_ref(middle), fields[0], fields[1], fields[2])
        return stepped + (time_step / 6.0) * (next_one + 2.0 * next_two)

    result = lax.map(advance, stepped_all)
    result = result.reshape((MODES,) + result.shape[2:])
    return result[:, 0:2], result[:, 2:4], fields
```

```python
import functools

import jax
import jax.numpy as jnp
import numpy as np
from jax import lax
from jax.experimental import pallas as pl
from jax.experimental.pallas import tpu as pltpu
from jax.sharding import PartitionSpec as P

NX = 32
NY = 32

stencil_coef = (-205.0 / 72.0, 8.0 / 5.0, -1.0 / 5.0, 8.0 / 315.0, -1.0 / 560.0)
alpha_coef = 1.14
beta_coef = -0.553
gamma_coef = -11.11
time_step = 0.18
epsilon = 1e-06

REACH = 4
LANES = 128
BLOCK = 256
WINDOW = BLOCK + 2 * LANES


def in_plane_matrix():
    rows_out = BLOCK // NX
    mat = np.zeros((WINDOW, BLOCK), np.float64)
    for y in range(rows_out):
        for x in range(NX):
            out = y * NX + x
            for k in range(1, REACH + 1):
                for sign in (-1, 1):
                    mat[(y + REACH) * NX + (x + sign * k) % NX, out] += stencil_coef[k]
                    mat[(y + REACH + sign * k) * NX + x, out] += stencil_coef[k]
    mat = mat.astype(np.float32)
    high = mat.astype(jnp.bfloat16)
    low = (mat - high.astype(np.float32)).astype(jnp.bfloat16)
    return np.concatenate([high, high, low], axis=0)


def up16(n):
    return -(-n // 16) * 16


def laplace_in_plane(read, rows, w_ref, hi_ref, lo_ref, xy_ref):
    for c in range(4):
        for j in range(8):
            value = read(c, j)
            high = value.astype(jnp.bfloat16)
            low = (value - high.astype(jnp.float32)).astype(jnp.bfloat16)
            if j % 2 == 0:
                places = ((j // 2, 1), ((j // 2 + 3) % 4, 3))
            else:
                places = ((j // 2, 2), ((j // 2 + 1) % 4, 0))
            for big, part in places:
                hi_ref[big, c, :rows, part * LANES : (part + 1) * LANES] = high
                lo_ref[big, c, :rows, part * LANES : (part + 1) * LANES] = low
    high = hi_ref[:, :, :rows, :].reshape(16 * rows, WINDOW)
    low = lo_ref[:, :, :rows, :].reshape(16 * rows, WINDOW)
    total = jnp.dot(
        jnp.concatenate([high, low, high], axis=1),
        w_ref[...],
        preferred_element_type=jnp.float32,
    )
    xy_ref[:, :, :rows, :] = total.reshape(4, 4, rows, BLOCK)


def z_part(ref, c, j, start, count):
    centre = ref[c, j, pl.ds(start, count), :]
    total = (3.0 * stencil_coef[0]) * centre
    for k in range(1, REACH + 1):
        total = total + stencil_coef[k] * (
            ref[c, j, pl.ds(start + k, count), :] + ref[c, j, pl.ds(start - k, count), :]
        )
    return centre, total


def slope(f, lap, pot, pr, pi):
    kin = [-0.5 * alpha_coef * lap[c] + pot * f[c] for c in range(4)]
    upper_re = kin[0] + pr * f[2] - pi * f[3]
    upper_im = kin[1] + pr * f[3] + pi * f[2]
    lower_re = pr * f[0] + pi * f[1] - kin[2]
    lower_im = pr * f[1] - pi * f[0] - kin[3]
    return upper_im, -upper_re, lower_im, -lower_re


def chunks(rows, size=16):
    return [(r, min(size, rows - r)) for r in range(0, rows, size)]


def stages_kernel(pieces, planes, low_bits, *refs):
    n = len(pieces)
    parts = refs[:n]
    w_ref = refs[n]
    psi1_ref, lap1_ref, sums_ref = refs[n + 1 : n + 4]
    b0, b1, b2, b3, b4, pd, hi, lo, xy = refs[n + 4 :]
    odd = lax.rem(lax.axis_index("grid"), 2)
    quarter = lax.rem(lax.axis_index("modes"), low_bits)

    for ref, (channels, moves) in zip(parts, pieces):
        for src, count, dst_even, dst_odd in moves:
            if dst_even == dst_odd:
                dst = dst_even
                dst_pd = dst_even - 8
            else:
                dst = pl.multiple_of(dst_even + odd * (dst_odd - dst_even), 8)
                dst_pd = pl.multiple_of(dst - 8, 8)
            for c in range(channels):
                for j in range(8):
                    value = ref[c, src : src + count, j * LANES : (j + 1) * LANES]
                    if c < 4:
                        b0[c, j, pl.ds(dst, count), :] = value
                    else:
                        pd[c - 4, j, pl.ds(dst_pd, count), :] = value

    def run(src, start, rows, store):
        tall = up16(rows)
        laplace_in_plane(
            lambda c, j: src[c, j, pl.ds(start, tall), :], tall, w_ref, hi, lo, xy
        )
        margin = (planes + 32 - rows) // 2

        def body(big, carry):
            for half in range(2):
                j = big * 2 + half
                for r, count in chunks(rows):
                    centre, lap = [], []
                    for c in range(4):
                        f, z = z_part(src, c, j, start + r, count)
                        centre.append(f)
                        lap.append(
                            z + xy[big, c, pl.ds(r, count), half * LANES : (half + 1) * LANES]
                        )
                    store(big, half, j, r, count, margin + r, centre, lap)
            return carry

        lax.fori_loop(0, 4, body, 0)

    def fields_at(j, row, count):
        return [pd[i, j, pl.ds(row, count), :] for i in range(3)]

    def stage(dst, factor):
        def store(big, half, j, r, count, row, centre, lap):
            k = slope(centre, lap, *fields_at(j, row, count))
            for c in range(4):
                dst[c, j, pl.ds(r, count), :] = b0[c, j, pl.ds(row + 8, count), :] + factor * k[c]

        return store

    run(b0, 8, planes + 32, stage(b1, 0.5 * time_step))
    run(b1, 4, planes + 24, stage(b2, 0.5 * time_step))
    run(b2, 4, planes + 16, stage(b3, time_step))

    def last(big, half, j, r, count, row, centre, lap):
        k = slope(centre, lap, *fields_at(j, row, count))
        for c in range(4):
            early = (
                b1[c, j, pl.ds(r + 12, count), :]
                - b0[c, j, pl.ds(r + 20, count), :]
                + 2.0 * b2[c, j, pl.ds(r + 8, count), :]
                + centre[c]
            )
            b4[c, j, pl.ds(r, count), :] = early * (1.0 / 3.0) + (time_step / 6.0) * k[c]

    run(b3, 4, planes + 8, last)

    def finish(big, half, j, r, count, row, f, lap):
        for c in range(4):
            psi1_ref[c, j, pl.ds(r, count), :] = f[c]
            lap1_ref[c, j, pl.ds(r, count), :] = lap[c]
        sums = (
            f[2] * f[2] + f[3] * f[3],
            f[2] * lap[2] + f[3] * lap[3],
            f[0] * f[2] + f[1] * f[3],
            f[1] * f[2] - f[0] * f[3],
        )
        place = lax.bitwise_xor(big, quarter) if low_bits == 4 else big
        for s in range(4):
            sums_ref[place, half, s, pl.ds(r, count), :] = sums[s]

    run(b4, 4, planes, finish)


def field_reader(parts, low_bits):
    stack, = parts

    def read(big, half, i):
        return stack[big, half, i]

    return read


def middle_kernel(paired, planes, low_bits, *refs):
    count = len(refs) - 6 - 2
    pieces = refs[:low_bits]
    psi1, lap1 = refs[low_bits : low_bits + 2]
    mid, first_send, second_send, fields_out, fields_flat = refs[low_bits + 2 :]
    even = lax.rem(lax.axis_index("grid"), 2) == 0
    quarter = lax.rem(lax.axis_index("modes"), low_bits)
    per = 4 // low_bits
    for k in range(low_bits):
        for t in range(per):
            place = lax.bitwise_xor(quarter, k) * per + t
            for half in range(2):
                for i in range(4):
                    fields_flat[place, half, i] = pieces[k][t, half, i]

    for j in range(8):
        big, half = j // 2, j % 2
        now = [fields_flat[big, half, i] for i in range(4)]
        for i in range(4):
            fields_out[i, :, j * LANES : (j + 1) * LANES] = now[i]
        f = [psi1[c, j] for c in range(4)]
        q = slope(f, [lap1[c, j] for c in range(4)], now[0], now[1], now[2])
        for c in range(4):
            m = f[c] + (0.5 * time_step) * q[c]
            mid[c, j] = m
            top, bottom = m[:REACH], m[planes - REACH :]
            if paired:
                a, b = jnp.where(even, top, bottom), jnp.where(even, bottom, top)
            else:
                a, b = top, bottom
            first_send[j, c * REACH : (c + 1) * REACH, :] = a
            second_send[j, c * REACH : (c + 1) * REACH, :] = b


def inner_kernel(planes, *refs):
    psi1, lap1, mid, fields_flat, w_ref, part_ref, pad, hi, lo, xy = refs
    tall = up16(planes)
    zero = jnp.zeros((8, LANES), jnp.float32)
    for c in range(4):
        for j in range(8):
            pad[c, j, 0:8, :] = zero
            pad[c, j, 8 : 8 + planes, :] = mid[c, j]
            for r in range(8 + planes, pad.shape[2], 8):
                pad[c, j, r : r + 8, :] = zero
    laplace_in_plane(lambda c, j: pad[c, j, 8 : 8 + tall, :], tall, w_ref, hi, lo, xy)

    def body(big, carry):
        for half in range(2):
            j = big * 2 + half
            for r, count in chunks(planes):
                field = [fields_flat[big, half, i, pl.ds(r, count), :] for i in range(3)]
                f = [psi1[c, j, pl.ds(r, count), :] for c in range(4)]
                q1 = slope(f, [lap1[c, j, pl.ds(r, count), :] for c in range(4)], *field)
                m, lap = [], []
                for c in range(4):
                    centre, z = z_part(pad, c, j, 8 + r, count)
                    m.append(centre)
                    lap.append(z + xy[big, c, pl.ds(r, count), half * LANES : (half + 1) * LANES])
                q2 = slope(m, lap, *field)
                for c in range(4):
                    part_ref[c, j, pl.ds(r, count), :] = f[c] + (time_step / 6.0) * (
                        q1[c] + 2.0 * q2[c]
                    )
        return carry

    lax.fori_loop(0, 4, body, 0)


def edge_kernel(paired, planes, *refs):
    part, first, second, u_ref, v_ref = refs
    even = lax.rem(lax.axis_index("grid"), 2) == 0
    scale = -0.5 * alpha_coef * 2.0 * time_step / 6.0
    terms = ((0, 1, 1.0), (1, 0, -1.0), (2, 3, -1.0), (3, 2, 1.0))
    for j in range(8):
        a, b = first[j], second[j]
        if paired:
            before, after = jnp.where(even, a, b), jnp.where(even, b, a)
        else:
            before, after = b, a
        for out, src, sign in terms:
            lo_rows = before[src * REACH : (src + 1) * REACH]
            hi_rows = after[src * REACH : (src + 1) * REACH]
            lead, tail = [], []
            for r in range(REACH):
                lead.append(
                    sum(
                        stencil_coef[k] * lo_rows[r - k + REACH : r - k + REACH + 1]
                        for k in range(r + 1, REACH + 1)
                    )
                )
                tail.append(
                    sum(
                        stencil_coef[k] * hi_rows[r + k - REACH : r + k - REACH + 1]
                        for k in range(REACH - r, REACH + 1)
                    )
                )
            value = part[out, j]
            parts = [value[:REACH] + (sign * scale) * jnp.concatenate(lead, axis=0)]
            if planes > 2 * REACH:
                parts.append(value[REACH : planes - REACH])
            parts.append(value[planes - REACH :] + (sign * scale) * jnp.concatenate(tail, axis=0))
            ref = u_ref if out < 2 else v_ref
            ref[0, out % 2, :, j * LANES : (j + 1) * LANES] = jnp.concatenate(parts, axis=0)


def potentials(raw, modes_total):
    density = 2.0 * raw[:, :, 0] / modes_total
    kinetic = -2.0 * raw[:, :, 1] / modes_total
    anomal_re = raw[:, :, 2] / modes_total
    anomal_im = raw[:, :, 3] / modes_total
    dense_safe = density + epsilon
    fermi = 0.5 * jnp.power(3.0 * jnp.pi**2 * dense_safe, 2.0 / 3.0)
    anomal_sq = anomal_re * anomal_re + anomal_im * anomal_im
    third_root = jnp.power(dense_safe, -1.0 / 3.0)
    field_pot = beta_coef * fermi - gamma_coef / 3.0 * anomal_sq * third_root / dense_safe
    pair_re = -gamma_coef * anomal_re * third_root
    pair_im = -gamma_coef * anomal_im * third_root
    energy = (
        alpha_coef * kinetic / 2.0
        + 0.6 * beta_coef * dense_safe * fermi
        + gamma_coef * anomal_sq * third_root
    )
    return jnp.stack([field_pot, pair_re, pair_im, energy], axis=2)


def call(kernel, outs, scratch, args, name):
    vmem = pl.BlockSpec(memory_space=pltpu.VMEM)
    flops = 2 * sum(int(np.prod(s)) for s in outs)
    return pl.pallas_call(
        kernel,
        out_shape=tuple(jax.ShapeDtypeStruct(s, jnp.float32) for s in outs),
        in_specs=[vmem] * len(args),
        out_specs=tuple([vmem] * len(outs)),
        scratch_shapes=[pltpu.VMEM(s, d) for s, d in scratch],
        compiler_params=pltpu.CompilerParams(vmem_limit_bytes=48 << 20),
        cost_estimate=pl.CostEstimate(flops=1000 * flops, bytes_accessed=4 * flops, transcendentals=0),
        name=name,
    )(*args)


def exchange_xor(x, axis, bits, count):
    return lax.ppermute(x, axis, [(i, i ^ bits) for i in range(count)])


def local(u_modes, v_modes, potential, pairing):
    planes = u_modes.shape[2]
    slabs = lax.axis_size("grid")
    modes = lax.axis_size("modes")
    paired = slabs == 4 and planes == 16
    f32, bf16 = jnp.float32, jnp.bfloat16
    weights = jnp.asarray(in_plane_matrix())
    own = jnp.concatenate([u_modes[0], v_modes[0], potential[None], pairing], axis=0)

    cross = [(i, (i - 1 if i % 2 == 0 else i + 1) % slabs) for i in range(slabs)]
    up = [(i, (i + 1) % slabs) for i in range(slabs)]
    down = [(j, i) for i, j in up]
    base = 24
    pieces, arrays = [(7, [(0, planes, base, base)])], [own]
    if paired:
        far_slab = lax.ppermute(own, "grid", cross)
        near_slab = exchange_xor(own, "grid", 1, slabs)
        both = jnp.concatenate([far_slab[:4, :REACH], far_slab[:4, planes - REACH :]], axis=1)
        relayed = exchange_xor(both, "grid", 1, slabs)
        pieces += [
            (7, [(0, planes, base - planes, base + planes)]),
            (7, [(0, planes, base + planes, base - planes)]),
            (4, [(0, REACH, base + 2 * planes, base + 2 * planes), (REACH, REACH, base - planes - REACH, base - planes - REACH)]),
        ]
        arrays += [far_slab, near_slab, relayed]
    else:
        reach, step = 0, 0
        while reach < 5 * REACH:
            step += 1
            count = min(planes, 5 * REACH - reach)
            wide = 7 if reach < 4 * REACH else 4
            before = lax.ppermute(
                own[:wide, planes - count :], "grid", [(i, (i + step) % slabs) for i in range(slabs)]
            )
            after = lax.ppermute(
                own[:wide, :count], "grid", [((i + step) % slabs, i) for i in range(slabs)]
            )
            lead, tail = base - reach - count, base + planes + reach
            pieces += [(wide, [(0, count, lead, lead)]), (wide, [(0, count, tail, tail)])]
            arrays += [before, after]
            reach += count

    low_bits = 4 if modes % 4 == 0 else 1
    tall = up16(planes + 32)
    state = (4, 8, planes, LANES)
    psi1, lap1, sums = call(
        functools.partial(stages_kernel, pieces, planes, low_bits),
        [state, state, (4, 2, 4, planes, LANES)],
        [
            ((4, 8, tall + 24, LANES), f32),
            ((4, 8, tall + 8, LANES), f32),
            ((4, 8, tall + 8, LANES), f32),
            ((4, 8, tall + 8, LANES), f32),
            ((4, 8, tall + 8, LANES), f32),
            ((3, 8, tall + 8, LANES), f32),
            ((4, 4, tall, WINDOW), bf16),
            ((4, 4, tall, WINDOW), bf16),
            ((4, 4, tall, BLOCK), f32),
        ],
        arrays + [weights],
        "stages",
    )

    if low_bits == 4:
        total = sums[0:1]
        for k in (1, 2, 3):
            total = total + exchange_xor(sums[k : k + 1], "modes", k, modes)
    else:
        total = sums
    bits = low_bits
    while bits < modes:
        total = total + exchange_xor(total, "modes", bits, modes)
        bits *= 2
    quarter = potentials(total, float(u_modes.shape[0] * modes))
    got = [quarter] + [exchange_xor(quarter, "modes", k, modes) for k in range(1, low_bits)]

    edge = (8, 4 * REACH, LANES)
    mid, first, second, fields, fields_flat = call(
        functools.partial(middle_kernel, paired, planes, low_bits),
        [state, edge, edge, (4, planes, NX * NY), (4, 2, 4, planes, LANES)],
        [],
        got + [psi1, lap1],
        "middle",
    )
    if paired:
        first = lax.ppermute(first, "grid", cross)
        second = exchange_xor(second, "grid", 1, slabs)
    else:
        first = lax.ppermute(first, "grid", down)
        second = lax.ppermute(second, "grid", up)
    flat = up16(planes)
    (part,) = call(
        functools.partial(inner_kernel, planes),
        [state],
        [
            ((4, 8, flat + 16, LANES), f32),
            ((4, 4, flat, WINDOW), bf16),
            ((4, 4, flat, WINDOW), bf16),
            ((4, 4, flat, BLOCK), f32),
        ],
        [psi1, lap1, mid, fields_flat, weights],
        "inner",
    )
    u_next, v_next = call(
        functools.partial(edge_kernel, paired, planes),
        [u_modes.shape, v_modes.shape],
        [],
        [part, first, second],
        "edges",
    )
    return u_next, v_next, fields


def solution(mesh):
    wide = P("modes", None, "grid", None)
    return jax.shard_map(
        local,
        mesh=mesh,
        in_specs=(wide, wide, P("grid", None), P(None, "grid", None)),
        out_specs=(wide, wide, P(None, "grid", None)),
        check_vma=False,
    )
```

```python
import functools

import jax
import jax.numpy as jnp
import numpy as np
from jax import lax
from jax.experimental import pallas as pl
from jax.experimental.pallas import tpu as pltpu
from jax.sharding import PartitionSpec as P

NX = 32
NY = 32

stencil_coef = (-205.0 / 72.0, 8.0 / 5.0, -1.0 / 5.0, 8.0 / 315.0, -1.0 / 560.0)
alpha_coef = 1.14
beta_coef = -0.553
gamma_coef = -11.11
time_step = 0.18
epsilon = 1e-06

REACH = 4
LANES = 128
BLOCK = 256
WINDOW = BLOCK + 2 * LANES
kinetic_coef = -0.5 * alpha_coef
unit = stencil_coef[1]
near_coef = tuple(c / unit for c in stencil_coef)
unit_coef = kinetic_coef * unit
centre_coef = 3.0 * kinetic_coef * stencil_coef[0]


def in_plane_matrix():
    rows_out = BLOCK // NX
    mat = np.zeros((WINDOW, BLOCK), np.float64)
    for y in range(rows_out):
        for x in range(NX):
            out = y * NX + x
            for k in range(1, REACH + 1):
                for sign in (-1, 1):
                    mat[(y + REACH) * NX + (x + sign * k) % NX, out] += near_coef[k]
                    mat[(y + REACH + sign * k) * NX + x, out] += near_coef[k]
    mat = mat.astype(jnp.bfloat16)
    return np.concatenate([mat, mat], axis=0)


def up16(n):
    return -(-n // 16) * 16


def put_split(value, c, j, row, hi_ref, lo_ref):
    count = value.shape[0]
    high = value.astype(jnp.bfloat16)
    low = (value - high.astype(jnp.float32)).astype(jnp.bfloat16)
    if j % 2 == 0:
        places = ((j // 2, 1), ((j // 2 + 3) % 4, 3))
    else:
        places = ((j // 2, 2), ((j // 2 + 1) % 4, 0))
    for big, part in places:
        hi_ref[big, c, pl.ds(row, count), part * LANES : (part + 1) * LANES] = high
        lo_ref[big, c, pl.ds(row, count), part * LANES : (part + 1) * LANES] = low


GROUP = 2


def in_plane(group, rows, w_ref, hi_ref, lo_ref, xy_ref):
    span = slice(group * GROUP, (group + 1) * GROUP)
    high = hi_ref[span, :, :rows, :].reshape(GROUP * 4 * rows, WINDOW)
    low = lo_ref[span, :, :rows, :].reshape(GROUP * 4 * rows, WINDOW)
    total = jnp.dot(
        jnp.concatenate([high, low], axis=1), w_ref[...], preferred_element_type=jnp.float32
    )
    for half in range(2):
        xy_ref[span, :, half, :rows, :] = total[:, half * LANES : (half + 1) * LANES].reshape(
            GROUP, 4, rows, LANES
        )


def in_plane_steps(rows, w_ref, hi_ref, lo_ref, xy_ref):
    groups = 4 // GROUP
    in_plane(0, rows, w_ref, hi_ref, lo_ref, xy_ref)
    for group in range(groups):
        if group + 1 < groups:
            in_plane(group + 1, rows, w_ref, hi_ref, lo_ref, xy_ref)
        for j in range(group * GROUP * 2, (group + 1) * GROUP * 2):
            yield j


def neighbours(ref, xy, c, j, start, xy_start, count):
    total = xy[j // 2, c, j % 2, pl.ds(xy_start, count), :]
    for k in range(1, REACH + 1):
        pair = ref[c, j, pl.ds(start + k, count), :] + ref[c, j, pl.ds(start - k, count), :]
        total = total + (pair if k == 1 else near_coef[k] * pair)
    return total


def slope(f, kin, pr, pi):
    upper_re = kin[0] + pr * f[2] - pi * f[3]
    upper_im = kin[1] + pr * f[3] + pi * f[2]
    lower_re = pr * f[0] + pi * f[1] - kin[2]
    lower_im = pr * f[1] - pi * f[0] - kin[3]
    return upper_im, upper_re, lower_im, lower_re


signs = (1.0, -1.0, 1.0, -1.0)


def chunks(rows, size=16):
    return [(r, min(size, rows - r)) for r in range(0, rows, size)]


def stages_kernel(pieces, planes, low_bits, *refs):
    n = len(pieces)
    parts = refs[:n]
    w_ref = refs[n]
    psi1_ref, kin1_ref, sums_ref = refs[n + 1 : n + 4]
    b0, b1, b2, b3, b4, pd, hi_a, lo_a, hi_b, lo_b, xy = refs[n + 4 :]
    odd = lax.rem(lax.axis_index("grid"), 2)
    quarter = lax.rem(lax.axis_index("modes"), low_bits)

    for ref, (channels, moves) in zip(parts, pieces):
        for src, count, dst_even, dst_odd in moves:
            if dst_even == dst_odd:
                dst = dst_even
                dst_pd = dst_even - 8
            else:
                step = pl.multiple_of(odd * (dst_odd - dst_even), 16)
                dst = pl.multiple_of(dst_even + step, 8)
                dst_pd = pl.multiple_of(dst_even - 8 + step, 16 if (dst_even - 8) % 16 == 0 else 8)
            for c in range(channels):
                for j in range(8):
                    value = ref[c, src : src + count, j * LANES : (j + 1) * LANES]
                    if c < 4:
                        b0[c, j, pl.ds(dst, count), :] = value
                        if channels > 4:
                            put_split(value, c, j, dst_pd, hi_a, lo_a)
                    else:
                        if c == 4:
                            value = value + centre_coef
                        pd[c - 4, j, pl.ds(dst_pd, count), :] = value

    def run(src, start, xy_start, rows, hi, lo, store):
        tall = up16(rows + 2 * xy_start)
        margin = (planes + 32 - rows) // 2
        for j in in_plane_steps(tall, w_ref, hi, lo, xy):
            for r, count in chunks(rows):
                f = [src[c, j, pl.ds(start + r, count), :] for c in range(4)]
                near = [
                    neighbours(src, xy, c, j, start + r, xy_start + r, count) for c in range(4)
                ]
                store(j, r, count, margin + r, f, near)

    def derivative(j, row, count, f, near):
        pot, pr, pi = [pd[i, j, pl.ds(row, count), :] for i in range(3)]
        return slope(f, [unit_coef * near[c] + pot * f[c] for c in range(4)], pr, pi)

    def stage(dst, factor, hi, lo):
        def store(j, r, count, row, f, near):
            k = derivative(j, row, count, f, near)
            for c in range(4):
                value = b0[c, j, pl.ds(row + 8, count), :] + (signs[c] * factor) * k[c]
                dst[c, j, pl.ds(r, count), :] = value
                put_split(value, c, j, r, hi, lo)

        return store

    run(b0, 8, 0, planes + 32, hi_a, lo_a, stage(b1, 0.5 * time_step, hi_b, lo_b))
    run(b1, 4, 4, planes + 24, hi_b, lo_b, stage(b2, 0.5 * time_step, hi_a, lo_a))
    run(b2, 4, 4, planes + 16, hi_a, lo_a, stage(b3, time_step, hi_b, lo_b))

    def last(j, r, count, row, f, near):
        k = derivative(j, row, count, f, near)
        for c in range(4):
            early = (
                b1[c, j, pl.ds(r + 12, count), :]
                - b0[c, j, pl.ds(r + 20, count), :]
                + 2.0 * b2[c, j, pl.ds(r + 8, count), :]
                + f[c]
            )
            value = early * (1.0 / 3.0) + (signs[c] * time_step / 6.0) * k[c]
            b4[c, j, pl.ds(r, count), :] = value
            put_split(value, c, j, r, hi_a, lo_a)

    run(b3, 4, 4, planes + 8, hi_b, lo_b, last)

    def finish(j, r, count, row, f, near):
        full = [unit_coef * near[c] + centre_coef * f[c] for c in range(4)]
        for c in range(4):
            psi1_ref[c, j, pl.ds(r, count), :] = f[c]
            kin1_ref[c, j, pl.ds(r, count), :] = full[c]
        sums = (
            f[2] * f[2] + f[3] * f[3],
            f[2] * full[2] + f[3] * full[3],
            f[0] * f[2] + f[1] * f[3],
            f[1] * f[2] - f[0] * f[3],
        )
        place = lax.bitwise_xor(jnp.int32(j // 2), quarter) if low_bits == 4 else j // 2
        for s in range(4):
            sums_ref[place, j % 2, s, pl.ds(r, count), :] = sums[s]

    run(b4, 4, 4, planes, hi_a, lo_a, finish)


def middle_kernel(paired, planes, low_bits, *refs):
    pieces = refs[:low_bits]
    psi1, kin1 = refs[low_bits : low_bits + 2]
    mid, first_send, second_send, fields_out, fields_flat = refs[low_bits + 2 :]
    even = lax.rem(lax.axis_index("grid"), 2) == 0
    quarter = lax.rem(lax.axis_index("modes"), low_bits)
    per = 4 // low_bits
    for k in range(low_bits):
        for t in range(per):
            place = lax.bitwise_xor(quarter, k) * per + t
            for half in range(2):
                for i in range(4):
                    fields_flat[place, half, i] = pieces[k][t, half, i]

    for j in range(8):
        big, half = j // 2, j % 2
        now = [fields_flat[big, half, i] for i in range(4)]
        for i in range(4):
            fields_out[i, :, j * LANES : (j + 1) * LANES] = now[i]
        f = [psi1[c, j] for c in range(4)]
        q = slope(f, [kin1[c, j] + now[0] * f[c] for c in range(4)], now[1], now[2])
        for c in range(4):
            m = f[c] + (signs[c] * 0.5 * time_step) * q[c]
            mid[c, j] = m
            top, bottom = m[:REACH], m[planes - REACH :]
            if paired:
                a, b = jnp.where(even, top, bottom), jnp.where(even, bottom, top)
            else:
                a, b = top, bottom
            first_send[j, c * REACH : (c + 1) * REACH, :] = a
            second_send[j, c * REACH : (c + 1) * REACH, :] = b


def inner_kernel(planes, *refs):
    psi1, kin1, mid, fields_flat, w_ref, part_ref, pad, hi, lo, xy = refs
    tall = up16(planes)
    zero = jnp.zeros((8, LANES), jnp.float32)
    for c in range(4):
        for j in range(8):
            value = mid[c, j]
            pad[c, j, 0:8, :] = zero
            pad[c, j, 8 : 8 + planes, :] = value
            pad[c, j, 8 + planes : 16 + planes, :] = zero
            put_split(value, c, j, 0, hi, lo)

    for j in in_plane_steps(tall, w_ref, hi, lo, xy):
        for r, count in chunks(planes):
            pot, pr, pi = [fields_flat[j // 2, j % 2, i, pl.ds(r, count), :] for i in range(3)]
            f = [psi1[c, j, pl.ds(r, count), :] for c in range(4)]
            q1 = slope(f, [kin1[c, j, pl.ds(r, count), :] + pot * f[c] for c in range(4)], pr, pi)
            m = [pad[c, j, pl.ds(8 + r, count), :] for c in range(4)]
            pot = pot + centre_coef
            near = [neighbours(pad, xy, c, j, 8 + r, r, count) for c in range(4)]
            q2 = slope(m, [unit_coef * near[c] + pot * m[c] for c in range(4)], pr, pi)
            for c in range(4):
                part_ref[c, j, pl.ds(r, count), :] = f[c] + (signs[c] * time_step / 6.0) * (
                    q1[c] + 2.0 * q2[c]
                )


def edge_kernel(paired, planes, *refs):
    part, first, second, u_ref, v_ref = refs
    even = lax.rem(lax.axis_index("grid"), 2) == 0
    scale = -0.5 * alpha_coef * 2.0 * time_step / 6.0
    terms = ((0, 1, 1.0), (1, 0, -1.0), (2, 3, -1.0), (3, 2, 1.0))
    for j in range(8):
        a, b = first[j], second[j]
        if paired:
            before, after = jnp.where(even, a, b), jnp.where(even, b, a)
        else:
            before, after = b, a
        for out, src, sign in terms:
            lo_rows = before[src * REACH : (src + 1) * REACH]
            hi_rows = after[src * REACH : (src + 1) * REACH]
            lead, tail = [], []
            for r in range(REACH):
                lead.append(
                    sum(
                        stencil_coef[k] * lo_rows[r - k + REACH : r - k + REACH + 1]
                        for k in range(r + 1, REACH + 1)
                    )
                )
                tail.append(
                    sum(
                        stencil_coef[k] * hi_rows[r + k - REACH : r + k - REACH + 1]
                        for k in range(REACH - r, REACH + 1)
                    )
                )
            value = part[out, j]
            parts = [value[:REACH] + (sign * scale) * jnp.concatenate(lead, axis=0)]
            if planes > 2 * REACH:
                parts.append(value[REACH : planes - REACH])
            parts.append(value[planes - REACH :] + (sign * scale) * jnp.concatenate(tail, axis=0))
            ref = u_ref if out < 2 else v_ref
            ref[0, out % 2, :, j * LANES : (j + 1) * LANES] = jnp.concatenate(parts, axis=0)


def potentials(raw, modes_total):
    density = 2.0 * raw[:, :, 0] / modes_total
    kinetic = (-2.0 / kinetic_coef) * raw[:, :, 1] / modes_total
    anomal_re = raw[:, :, 2] / modes_total
    anomal_im = raw[:, :, 3] / modes_total
    dense_safe = density + epsilon
    fermi = 0.5 * jnp.power(3.0 * jnp.pi**2 * dense_safe, 2.0 / 3.0)
    anomal_sq = anomal_re * anomal_re + anomal_im * anomal_im
    third_root = jnp.power(dense_safe, -1.0 / 3.0)
    field_pot = beta_coef * fermi - gamma_coef / 3.0 * anomal_sq * third_root / dense_safe
    pair_re = -gamma_coef * anomal_re * third_root
    pair_im = -gamma_coef * anomal_im * third_root
    energy = (
        alpha_coef * kinetic / 2.0
        + 0.6 * beta_coef * dense_safe * fermi
        + gamma_coef * anomal_sq * third_root
    )
    return jnp.stack([field_pot, pair_re, pair_im, energy], axis=2)


def call(kernel, outs, scratch, args, name):
    vmem = pl.BlockSpec(memory_space=pltpu.VMEM)
    flops = 2 * sum(int(np.prod(s)) for s in outs)
    return pl.pallas_call(
        kernel,
        out_shape=tuple(jax.ShapeDtypeStruct(s, jnp.float32) for s in outs),
        in_specs=[vmem] * len(args),
        out_specs=tuple([vmem] * len(outs)),
        scratch_shapes=[pltpu.VMEM(s, d) for s, d in scratch],
        compiler_params=pltpu.CompilerParams(vmem_limit_bytes=48 << 20),
        cost_estimate=pl.CostEstimate(flops=1000 * flops, bytes_accessed=4 * flops, transcendentals=0),
        name=name,
    )(*args)


def exchange_xor(x, axis, bits, count):
    return lax.ppermute(x, axis, [(i, i ^ bits) for i in range(count)])


def local(u_modes, v_modes, potential, pairing):
    planes = u_modes.shape[2]
    slabs = lax.axis_size("grid")
    modes = lax.axis_size("modes")
    paired = slabs == 4 and planes == 16
    f32, bf16 = jnp.float32, jnp.bfloat16
    weights = jnp.asarray(in_plane_matrix())
    own = jnp.concatenate([u_modes[0], v_modes[0], potential[None], pairing], axis=0)

    cross = [(i, (i - 1 if i % 2 == 0 else i + 1) % slabs) for i in range(slabs)]
    up = [(i, (i + 1) % slabs) for i in range(slabs)]
    down = [(j, i) for i, j in up]
    base = 24
    pieces, arrays = [(7, [(0, planes, base, base)])], [own]
    if paired:
        far_slab = lax.ppermute(own, "grid", cross)
        near_slab = exchange_xor(own, "grid", 1, slabs)
        both = jnp.concatenate([far_slab[:4, :REACH], far_slab[:4, planes - REACH :]], axis=1)
        relayed = exchange_xor(both, "grid", 1, slabs)
        pieces += [
            (7, [(0, planes, base - planes, base + planes)]),
            (7, [(0, planes, base + planes, base - planes)]),
            (4, [(0, REACH, base + 2 * planes, base + 2 * planes), (REACH, REACH, base - planes - REACH, base - planes - REACH)]),
        ]
        arrays += [far_slab, near_slab, relayed]
    else:
        reach, step = 0, 0
        while reach < 5 * REACH:
            step += 1
            count = min(planes, 5 * REACH - reach)
            wide = 7 if reach < 4 * REACH else 4
            before = lax.ppermute(
                own[:wide, planes - count :], "grid", [(i, (i + step) % slabs) for i in range(slabs)]
            )
            after = lax.ppermute(
                own[:wide, :count], "grid", [((i + step) % slabs, i) for i in range(slabs)]
            )
            lead, tail = base - reach - count, base + planes + reach
            pieces += [(wide, [(0, count, lead, lead)]), (wide, [(0, count, tail, tail)])]
            arrays += [before, after]
            reach += count

    low_bits = 4 if modes % 4 == 0 else 1
    tall = up16(planes + 32)
    state = (4, 8, planes, LANES)
    psi1, kin1, sums = call(
        functools.partial(stages_kernel, pieces, planes, low_bits),
        [state, state, (4, 2, 4, planes, LANES)],
        [
            ((4, 8, tall + 24, LANES), f32),
            ((4, 8, tall + 8, LANES), f32),
            ((4, 8, tall + 8, LANES), f32),
            ((4, 8, tall + 8, LANES), f32),
            ((4, 8, tall + 8, LANES), f32),
            ((3, 8, tall + 8, LANES), f32),
            ((4, 4, tall, WINDOW), bf16),
            ((4, 4, tall, WINDOW), bf16),
            ((4, 4, tall, WINDOW), bf16),
            ((4, 4, tall, WINDOW), bf16),
            ((4, 4, 2, tall, LANES), f32),
        ],
        arrays + [weights],
        "stages",
    )

    if low_bits == 4:
        total = sums[0:1]
        for k in (1, 2, 3):
            total = total + exchange_xor(sums[k : k + 1], "modes", k, modes)
    else:
        total = sums
    bits = low_bits
    while bits < modes:
        total = total + exchange_xor(total, "modes", bits, modes)
        bits *= 2
    quarter = potentials(total, float(u_modes.shape[0] * modes))
    got = [quarter] + [exchange_xor(quarter, "modes", k, modes) for k in range(1, low_bits)]

    edge = (8, 4 * REACH, LANES)
    mid, first, second, fields, fields_flat = call(
        functools.partial(middle_kernel, paired, planes, low_bits),
        [state, edge, edge, (4, planes, NX * NY), (4, 2, 4, planes, LANES)],
        [],
        got + [psi1, kin1],
        "middle",
    )
    if paired:
        first = lax.ppermute(first, "grid", cross)
        second = exchange_xor(second, "grid", 1, slabs)
    else:
        first = lax.ppermute(first, "grid", down)
        second = lax.ppermute(second, "grid", up)
    flat = up16(planes)
    (part,) = call(
        functools.partial(inner_kernel, planes),
        [state],
        [
            ((4, 8, flat + 16, LANES), f32),
            ((4, 4, flat, WINDOW), bf16),
            ((4, 4, flat, WINDOW), bf16),
            ((4, 4, 2, flat, LANES), f32),
        ],
        [psi1, kin1, mid, fields_flat, weights],
        "inner",
    )
    u_next, v_next = call(
        functools.partial(edge_kernel, paired, planes),
        [u_modes.shape, v_modes.shape],
        [],
        [part, first, second],
        "edges",
    )
    return u_next, v_next, fields


def solution(mesh):
    wide = P("modes", None, "grid", None)
    return jax.shard_map(
        local,
        mesh=mesh,
        in_specs=(wide, wide, P("grid", None), P(None, "grid", None)),
        out_specs=(wide, wide, P(None, "grid", None)),
        check_vma=False,
    )
```

```python
import functools

import jax
import jax.numpy as jnp
import numpy as np
from jax import lax
from jax.experimental import pallas as pl
from jax.experimental.pallas import tpu as pltpu
from jax.sharding import PartitionSpec as P

NX = 32
NY = 32

stencil_coef = (-205.0 / 72.0, 8.0 / 5.0, -1.0 / 5.0, 8.0 / 315.0, -1.0 / 560.0)
alpha_coef = 1.14
beta_coef = -0.553
gamma_coef = -11.11
time_step = 0.18
epsilon = 1e-06

REACH = 4
LANES = 128
BLOCK = 256
WINDOW = BLOCK + 2 * LANES
kinetic_coef = -0.5 * alpha_coef
unit = stencil_coef[1]
near_coef = tuple(c / unit for c in stencil_coef)
unit_coef = kinetic_coef * unit
centre_coef = 3.0 * kinetic_coef * stencil_coef[0]


def in_plane_matrix():
    rows_out = BLOCK // NX
    mat = np.zeros((WINDOW, BLOCK), np.float64)
    for y in range(rows_out):
        for x in range(NX):
            out = y * NX + x
            for k in range(1, REACH + 1):
                for sign in (-1, 1):
                    mat[(y + REACH) * NX + (x + sign * k) % NX, out] += near_coef[k]
                    mat[(y + REACH + sign * k) * NX + x, out] += near_coef[k]
    mat = mat.astype(jnp.bfloat16)
    return np.concatenate([mat, mat], axis=0)


def up16(n):
    return -(-n // 16) * 16


def put_split(value, c, j, row, hi_ref, lo_ref):
    count = value.shape[0]
    high = value.astype(jnp.bfloat16)
    low = (value - high.astype(jnp.float32)).astype(jnp.bfloat16)
    if j % 2 == 0:
        places = ((j // 2, 1), ((j // 2 + 3) % 4, 3))
    else:
        places = ((j // 2, 2), ((j // 2 + 1) % 4, 0))
    for big, part in places:
        hi_ref[big, c, pl.ds(row, count), part * LANES : (part + 1) * LANES] = high
        lo_ref[big, c, pl.ds(row, count), part * LANES : (part + 1) * LANES] = low


GROUP = 2


def in_plane(group, rows, w_ref, hi_ref, lo_ref, xy_ref):
    span = slice(group * GROUP, (group + 1) * GROUP)
    high = hi_ref[span, :, :rows, :].reshape(GROUP * 4 * rows, WINDOW)
    low = lo_ref[span, :, :rows, :].reshape(GROUP * 4 * rows, WINDOW)
    total = jnp.dot(
        jnp.concatenate([high, low], axis=1), w_ref[...], preferred_element_type=jnp.float32
    )
    for half in range(2):
        xy_ref[span, :, half, :rows, :] = total[:, half * LANES : (half + 1) * LANES].reshape(
            GROUP, 4, rows, LANES
        )


def in_plane_steps(rows, w_ref, hi_ref, lo_ref, xy_ref):
    groups = 4 // GROUP
    in_plane(0, rows, w_ref, hi_ref, lo_ref, xy_ref)
    for group in range(groups):
        if group + 1 < groups:
            in_plane(group + 1, rows, w_ref, hi_ref, lo_ref, xy_ref)
        for j in range(group * GROUP * 2, (group + 1) * GROUP * 2):
            yield j


def neighbours(ref, xy, c, j, start, xy_start, count):
    total = xy[j // 2, c, j % 2, pl.ds(xy_start, count), :]
    for k in range(1, REACH + 1):
        pair = ref[c, j, pl.ds(start + k, count), :] + ref[c, j, pl.ds(start - k, count), :]
        total = total + (pair if k == 1 else near_coef[k] * pair)
    return total


def slope(f, kin, pr, pi):
    upper_re = kin[0] + pr * f[2] - pi * f[3]
    upper_im = kin[1] + pr * f[3] + pi * f[2]
    lower_re = pr * f[0] + pi * f[1] - kin[2]
    lower_im = pr * f[1] - pi * f[0] - kin[3]
    return upper_im, upper_re, lower_im, lower_re


signs = (1.0, -1.0, 1.0, -1.0)


def chunks(rows, size=16):
    return [(r, min(size, rows - r)) for r in range(0, rows, size)]


def laplace_rows(src, start, xy_start, rows, planes, refs, store):
    w_ref, hi, lo, xy = refs
    tall = up16(rows + 2 * xy_start)
    margin = (planes + 32 - rows) // 2
    for j in in_plane_steps(tall, w_ref, hi, lo, xy):
        for r, count in chunks(rows):
            f = [src[c, j, pl.ds(start + r, count), :] for c in range(4)]
            near = [neighbours(src, xy, c, j, start + r, xy_start + r, count) for c in range(4)]
            store(j, r, count, margin + r, f, near)


def derivative(pd, j, row, count, f, near):
    pot, pr, pi = [pd[i, j, pl.ds(row, count), :] for i in range(3)]
    return slope(f, [unit_coef * near[c] + pot * f[c] for c in range(4)], pr, pi)


def stage_store(b0, pd, dst, factor, hi, lo):
    def store(j, r, count, row, f, near):
        k = derivative(pd, j, row, count, f, near)
        for c in range(4):
            value = b0[c, j, pl.ds(row + 8, count), :] + (signs[c] * factor) * k[c]
            dst[c, j, pl.ds(r, count), :] = value
            put_split(value, c, j, r, hi, lo)

    return store


def first_kernel(pieces, planes, *refs):
    n = len(pieces)
    parts, w_ref = refs[:n], refs[n]
    b0, pd, b1, hi_b, lo_b, hi_a, lo_a, xy = refs[n + 1 :]
    odd = lax.rem(lax.axis_index("grid"), 2)
    half = lax.rem(lax.axis_index("modes"), 2)
    zero = jnp.zeros((8, LANES), jnp.float32)
    for c in range(4):
        for j in range(8):
            b0[c, j, 0:8, :] = zero
            b0[c, j, planes + 40 : planes + 48, :] = zero

    for ref, (first, channels, count, row_even, row_odd, flip) in zip(parts, pieces):
        row = row_even
        if row_odd != row_even:
            row = pl.multiple_of(row_even + odd * (row_odd - row_even), 16)
        if flip is not None:
            row = pl.multiple_of(row + (half if flip == 0 else 1 - half) * count, 8)
        for i in range(channels):
            c = first + i
            for j in range(8):
                value = ref[i, :, j * LANES : (j + 1) * LANES]
                if c < 4:
                    b0[c, j, pl.ds(row + 8, count), :] = value
                    put_split(value, c, j, row, hi_a, lo_a)
                else:
                    pd[c - 4, j, pl.ds(row, count), :] = value + centre_coef if c == 4 else value

    store = stage_store(b0, pd, b1, 0.5 * time_step, hi_b, lo_b)
    laplace_rows(b0, 8, 0, planes + 32, planes, (w_ref, hi_a, lo_a, xy), store)


def stages_kernel(far, planes, low_bits, *refs):
    lead_ref, tail_ref, b0, pd = refs[:4]
    w_ref = refs[7]
    psi1_ref, kin1_ref, sums_ref, b1, hi_b, lo_b = refs[8:14]
    b2, b3, b4, hi_a, lo_a, xy, past = refs[14:]
    quarter = lax.rem(lax.axis_index("modes"), low_bits)

    zero = jnp.zeros((8, LANES), jnp.float32)
    for c in range(4):
        for j in range(8):
            lanes = slice(j * LANES, (j + 1) * LANES)
            past[c, j, 4:12, :] = zero
            past[c, j, 16:24, :] = zero
            past[c, j, 0:REACH, :] = lead_ref[c, far[0] : far[0] + REACH, lanes]
            past[c, j, 24 : 24 + REACH, :] = tail_ref[c, far[1] : far[1] + REACH, lanes]
    scale = 0.5 * time_step * unit_coef
    for j in range(8):
        for row, begin, sign in ((0, 4, -1), (planes + 24, 16, 1)):
            change = []
            for c in range(4):
                total = past[c, j, pl.ds(begin + sign, 8), :]
                for k in range(2, REACH + 1):
                    total = total + near_coef[k] * past[c, j, pl.ds(begin + sign * k, 8), :]
                change.append(scale * total)
            for c, delta in enumerate((change[1], -change[0], -change[3], change[2])):
                value = b1[c, j, row : row + 8, :] + delta
                b1[c, j, row : row + 8, :] = value
                put_split(value, c, j, row, hi_b, lo_b)

    def run(src, start, xy_start, rows, hi, lo, store):
        laplace_rows(src, start, xy_start, rows, planes, (w_ref, hi, lo, xy), store)

    store = stage_store(b0, pd, b2, 0.5 * time_step, hi_a, lo_a)
    run(b1, 4, 4, planes + 24, hi_b, lo_b, store)
    store = stage_store(b0, pd, b3, time_step, hi_b, lo_b)
    run(b2, 4, 4, planes + 16, hi_a, lo_a, store)

    def last(j, r, count, row, f, near):
        k = derivative(pd, j, row, count, f, near)
        for c in range(4):
            early = (
                b1[c, j, pl.ds(r + 12, count), :]
                - b0[c, j, pl.ds(r + 20, count), :]
                + 2.0 * b2[c, j, pl.ds(r + 8, count), :]
                + f[c]
            )
            value = early * (1.0 / 3.0) + (signs[c] * time_step / 6.0) * k[c]
            b4[c, j, pl.ds(r, count), :] = value
            put_split(value, c, j, r, hi_a, lo_a)

    run(b3, 4, 4, planes + 8, hi_b, lo_b, last)

    def finish(j, r, count, row, f, near):
        full = [unit_coef * near[c] + centre_coef * f[c] for c in range(4)]
        for c in range(4):
            psi1_ref[c, j, pl.ds(r, count), :] = f[c]
            kin1_ref[c, j, pl.ds(r, count), :] = full[c]
        sums = (
            f[2] * f[2] + f[3] * f[3],
            f[2] * full[2] + f[3] * full[3],
            f[0] * f[2] + f[1] * f[3],
            f[1] * f[2] - f[0] * f[3],
        )
        place = lax.bitwise_xor(jnp.int32(j // 2), quarter) if low_bits == 4 else j // 2
        for s in range(4):
            sums_ref[place, j % 2, s, pl.ds(r, count), :] = sums[s]

    run(b4, 4, 4, planes, hi_a, lo_a, finish)


def middle_kernel(paired, planes, low_bits, *refs):
    pieces = refs[:low_bits]
    psi1, kin1 = refs[low_bits : low_bits + 2]
    mid, first_send, second_send, fields_out, fields_flat = refs[low_bits + 2 :]
    even = lax.rem(lax.axis_index("grid"), 2) == 0
    quarter = lax.rem(lax.axis_index("modes"), low_bits)
    per = 4 // low_bits
    for k in range(low_bits):
        for t in range(per):
            place = lax.bitwise_xor(quarter, k) * per + t
            for half in range(2):
                for i in range(4):
                    fields_flat[place, half, i] = pieces[k][t, half, i]

    for j in range(8):
        big, half = j // 2, j % 2
        now = [fields_flat[big, half, i] for i in range(4)]
        for i in range(4):
            fields_out[i, :, j * LANES : (j + 1) * LANES] = now[i]
        f = [psi1[c, j] for c in range(4)]
        q = slope(f, [kin1[c, j] + now[0] * f[c] for c in range(4)], now[1], now[2])
        for c in range(4):
            m = f[c] + (signs[c] * 0.5 * time_step) * q[c]
            mid[c, j] = m
            top, bottom = m[:REACH], m[planes - REACH :]
            if paired:
                a, b = jnp.where(even, top, bottom), jnp.where(even, bottom, top)
            else:
                a, b = top, bottom
            first_send[j, c * REACH : (c + 1) * REACH, :] = a
            second_send[j, c * REACH : (c + 1) * REACH, :] = b


def inner_kernel(planes, *refs):
    psi1, kin1, mid, fields_flat, w_ref, part_ref, pad, hi, lo, xy = refs
    tall = up16(planes)
    zero = jnp.zeros((8, LANES), jnp.float32)
    for c in range(4):
        for j in range(8):
            value = mid[c, j]
            pad[c, j, 0:8, :] = zero
            pad[c, j, 8 : 8 + planes, :] = value
            pad[c, j, 8 + planes : 16 + planes, :] = zero
            put_split(value, c, j, 0, hi, lo)

    for j in in_plane_steps(tall, w_ref, hi, lo, xy):
        for r, count in chunks(planes):
            pot, pr, pi = [fields_flat[j // 2, j % 2, i, pl.ds(r, count), :] for i in range(3)]
            f = [psi1[c, j, pl.ds(r, count), :] for c in range(4)]
            q1 = slope(f, [kin1[c, j, pl.ds(r, count), :] + pot * f[c] for c in range(4)], pr, pi)
            m = [pad[c, j, pl.ds(8 + r, count), :] for c in range(4)]
            pot = pot + centre_coef
            near = [neighbours(pad, xy, c, j, 8 + r, r, count) for c in range(4)]
            q2 = slope(m, [unit_coef * near[c] + pot * m[c] for c in range(4)], pr, pi)
            for c in range(4):
                part_ref[c, j, pl.ds(r, count), :] = f[c] + (signs[c] * time_step / 6.0) * (
                    q1[c] + 2.0 * q2[c]
                )


def edge_kernel(paired, planes, *refs):
    part, first, second, u_ref, v_ref = refs
    even = lax.rem(lax.axis_index("grid"), 2) == 0
    scale = -0.5 * alpha_coef * 2.0 * time_step / 6.0
    terms = ((0, 1, 1.0), (1, 0, -1.0), (2, 3, -1.0), (3, 2, 1.0))
    for j in range(8):
        a, b = first[j], second[j]
        if paired:
            before, after = jnp.where(even, a, b), jnp.where(even, b, a)
        else:
            before, after = b, a
        for out, src, sign in terms:
            lo_rows = before[src * REACH : (src + 1) * REACH]
            hi_rows = after[src * REACH : (src + 1) * REACH]
            lead, tail = [], []
            for r in range(REACH):
                lead.append(
                    sum(
                        stencil_coef[k] * lo_rows[r - k + REACH : r - k + REACH + 1]
                        for k in range(r + 1, REACH + 1)
                    )
                )
                tail.append(
                    sum(
                        stencil_coef[k] * hi_rows[r + k - REACH : r + k - REACH + 1]
                        for k in range(REACH - r, REACH + 1)
                    )
                )
            value = part[out, j]
            parts = [value[:REACH] + (sign * scale) * jnp.concatenate(lead, axis=0)]
            if planes > 2 * REACH:
                parts.append(value[REACH : planes - REACH])
            parts.append(value[planes - REACH :] + (sign * scale) * jnp.concatenate(tail, axis=0))
            ref = u_ref if out < 2 else v_ref
            ref[0, out % 2, :, j * LANES : (j + 1) * LANES] = jnp.concatenate(parts, axis=0)


def potentials(raw, modes_total):
    density = 2.0 * raw[:, :, 0] / modes_total
    kinetic = (-2.0 / kinetic_coef) * raw[:, :, 1] / modes_total
    anomal_re = raw[:, :, 2] / modes_total
    anomal_im = raw[:, :, 3] / modes_total
    dense_safe = density + epsilon
    fermi = 0.5 * jnp.power(3.0 * jnp.pi**2 * dense_safe, 2.0 / 3.0)
    anomal_sq = anomal_re * anomal_re + anomal_im * anomal_im
    third_root = jnp.power(dense_safe, -1.0 / 3.0)
    field_pot = beta_coef * fermi - gamma_coef / 3.0 * anomal_sq * third_root / dense_safe
    pair_re = -gamma_coef * anomal_re * third_root
    pair_im = -gamma_coef * anomal_im * third_root
    energy = (
        alpha_coef * kinetic / 2.0
        + 0.6 * beta_coef * dense_safe * fermi
        + gamma_coef * anomal_sq * third_root
    )
    return jnp.stack([field_pot, pair_re, pair_im, energy], axis=2)


def call(kernel, outs, scratch, args, name, aliases=None):
    vmem = pl.BlockSpec(memory_space=pltpu.VMEM)
    shapes = [o if isinstance(o[0], tuple) else (o, jnp.float32) for o in outs]
    flops = 2 * sum(int(np.prod(s)) for s, d in shapes)
    return pl.pallas_call(
        kernel,
        out_shape=tuple(jax.ShapeDtypeStruct(s, d) for s, d in shapes),
        in_specs=[vmem] * len(args),
        out_specs=tuple([vmem] * len(outs)),
        scratch_shapes=[pltpu.VMEM(s, d) for s, d in scratch],
        input_output_aliases=aliases or {},
        compiler_params=pltpu.CompilerParams(vmem_limit_bytes=32 << 20),
        cost_estimate=pl.CostEstimate(flops=1000 * flops, bytes_accessed=4 * flops, transcendentals=0),
        name=name,
    )(*args)


def exchange_xor(x, axis, bits, count):
    return lax.ppermute(x, axis, [(i, i ^ bits) for i in range(count)])


def local(u_modes, v_modes, potential, pairing):
    planes = u_modes.shape[2]
    slabs = lax.axis_size("grid")
    modes = lax.axis_size("modes")
    low_bits = 4 if modes % 4 == 0 else 1
    paired = slabs == 4 and planes == 16 and low_bits == 4
    f32, bf16 = jnp.float32, jnp.bfloat16
    weights = jnp.asarray(in_plane_matrix())
    frozen = jnp.concatenate([potential[None], pairing], axis=0)
    psi = (u_modes[0], v_modes[0])

    cross = [(i, (i - 1 if i % 2 == 0 else i + 1) % slabs) for i in range(slabs)]
    up = [(i, (i + 1) % slabs) for i in range(slabs)]
    down = [(j, i) for i, j in up]
    pieces = [(0, 2, planes, 16, 16, None), (2, 2, planes, 16, 16, None), (4, 3, planes, 16, 16, None)]
    arrays = [*psi, frozen]
    if paired:
        part = planes // 2
        upper = lax.rem(lax.axis_index("modes"), 2) == 1
        mine = lax.ppermute(
            jnp.where(upper, frozen[:, part:], frozen[:, :part]), "grid", cross
        )
        far_u, far_v = [lax.ppermute(x, "grid", cross) for x in psi]
        near_u, near_v, near_f = [exchange_xor(x, "grid", 1, slabs) for x in (*psi, frozen)]
        other = exchange_xor(mine, "modes", 1, modes)
        lead, tail = 16 - planes, 16 + planes
        pieces += [
            (0, 2, planes, tail, lead, None),
            (2, 2, planes, tail, lead, None),
            (4, 3, planes, tail, lead, None),
            (4, 3, part, lead, tail, 0),
            (4, 3, part, lead, tail, 1),
            (0, 2, planes, lead, tail, None),
            (2, 2, planes, lead, tail, None),
        ]
        arrays += [near_u, near_v, near_f, mine, other, far_u, far_v]
        both = jnp.concatenate(
            [
                jnp.concatenate([x[:, :REACH], x[:, planes - REACH :]], axis=1)
                for x in (far_u, far_v)
            ],
            axis=0,
        )
        lead_far = tail_far = exchange_xor(both, "grid", 1, slabs)
        far = (REACH, 0)
    else:
        own = jnp.concatenate([*psi, frozen], axis=0)
        reach, step = 0, 0
        while reach < 5 * REACH:
            step += 1
            count = min(planes, 5 * REACH - reach)
            wide = 7 if reach < 4 * REACH else 4
            before = lax.ppermute(
                own[:wide, planes - count :], "grid", [(i, (i + step) % slabs) for i in range(slabs)]
            )
            after = lax.ppermute(
                own[:wide, :count], "grid", [((i + step) % slabs, i) for i in range(slabs)]
            )
            lead, tail = 16 - reach - count, 16 + planes + reach
            if wide == 7:
                pieces += [(0, 7, count, lead, lead, None), (0, 7, count, tail, tail, None)]
                arrays += [before, after]
            else:
                lead_far, tail_far, far = before, after, (0, 0)
            reach += count

    tall = up16(planes + 32)
    state = (4, 8, planes, LANES)
    split = ((4, 4, tall, WINDOW), bf16)
    b0, pd, b1, hi, lo = call(
        functools.partial(first_kernel, pieces, planes),
        [
            (4, 8, tall + 16, LANES),
            (3, 8, tall, LANES),
            (4, 8, tall + 8, LANES),
            split,
            split,
        ],
        [split, split, ((4, 4, 2, tall, LANES), f32)],
        arrays + [weights],
        "first",
    )
    inputs = [lead_far, tail_far, b0, pd, b1, hi, lo, weights]
    psi1, kin1, sums, *rest = call(
        functools.partial(stages_kernel, far, planes, low_bits),
        [state, state, (4, 2, 4, planes, LANES), b1.shape, split, split],
        [
            ((4, 8, tall + 8, LANES), f32),
            ((4, 8, tall + 8, LANES), f32),
            ((4, 8, tall + 8, LANES), f32),
            split,
            split,
            ((4, 4, 2, tall, LANES), f32),
            ((4, 8, 32, LANES), f32),
        ],
        inputs,
        "stages",
        {4: 3, 5: 4, 6: 5},
    )

    if low_bits == 4:
        total = sums[0:1]
        for k in (1, 2, 3):
            total = total + exchange_xor(sums[k : k + 1], "modes", k, modes)
    else:
        total = sums
    bits = low_bits
    while bits < modes:
        total = total + exchange_xor(total, "modes", bits, modes)
        bits *= 2
    quarter = potentials(total, float(u_modes.shape[0] * modes))
    got = [quarter] + [exchange_xor(quarter, "modes", k, modes) for k in range(1, low_bits)]

    edge = (8, 4 * REACH, LANES)
    mid, first, second, fields, fields_flat = call(
        functools.partial(middle_kernel, paired, planes, low_bits),
        [state, edge, edge, (4, planes, NX * NY), (4, 2, 4, planes, LANES)],
        [],
        got + [psi1, kin1],
        "middle",
    )
    if paired:
        first = lax.ppermute(first, "grid", cross)
        second = exchange_xor(second, "grid", 1, slabs)
    else:
        first = lax.ppermute(first, "grid", down)
        second = lax.ppermute(second, "grid", up)
    flat = up16(planes)
    (part,) = call(
        functools.partial(inner_kernel, planes),
        [state],
        [
            ((4, 8, flat + 16, LANES), f32),
            ((4, 4, flat, WINDOW), bf16),
            ((4, 4, flat, WINDOW), bf16),
            ((4, 4, 2, flat, LANES), f32),
        ],
        [psi1, kin1, mid, fields_flat, weights],
        "inner",
    )
    u_next, v_next = call(
        functools.partial(edge_kernel, paired, planes),
        [u_modes.shape, v_modes.shape],
        [],
        [part, first, second],
        "edges",
    )
    return u_next, v_next, fields


def solution(mesh):
    wide = P("modes", None, "grid", None)
    return jax.shard_map(
        local,
        mesh=mesh,
        in_specs=(wide, wide, P("grid", None), P(None, "grid", None)),
        out_specs=(wide, wide, P(None, "grid", None)),
        check_vma=False,
    )
```

```python
import functools

import jax
import jax.numpy as jnp
import numpy as np
from jax import lax
from jax.experimental import pallas as pl
from jax.experimental.pallas import tpu as pltpu
from jax.sharding import PartitionSpec as P


NX = 32
NY = 32

stencil_coef = (-205.0 / 72.0, 8.0 / 5.0, -1.0 / 5.0, 8.0 / 315.0, -1.0 / 560.0)
alpha_coef = 1.14
beta_coef = -0.553
gamma_coef = -11.11
time_step = 0.18
epsilon = 1e-06

REACH = 4
LANES = 128
BLOCK = 256
WINDOW = BLOCK + 2 * LANES
kinetic_coef = -0.5 * alpha_coef
unit = stencil_coef[1]
near_coef = tuple(c / unit for c in stencil_coef)
unit_coef = kinetic_coef * unit
centre_coef = 3.0 * kinetic_coef * stencil_coef[0]


def in_plane_matrix():
    rows_out = BLOCK // NX
    mat = np.zeros((WINDOW, BLOCK), np.float64)
    for y in range(rows_out):
        for x in range(NX):
            out = y * NX + x
            for k in range(1, REACH + 1):
                for sign in (-1, 1):
                    mat[(y + REACH) * NX + (x + sign * k) % NX, out] += near_coef[k]
                    mat[(y + REACH + sign * k) * NX + x, out] += near_coef[k]
    mat = mat.astype(jnp.bfloat16)
    return np.concatenate([mat, mat], axis=0)


def up16(n):
    return -(-n // 16) * 16


def put_split(value, c, j, row, hi_ref, lo_ref):
    count = value.shape[0]
    high = value.astype(jnp.bfloat16)
    low = (value - high.astype(jnp.float32)).astype(jnp.bfloat16)
    if j % 2 == 0:
        places = ((j // 2, 1), ((j // 2 + 3) % 4, 3))
    else:
        places = ((j // 2, 2), ((j // 2 + 1) % 4, 0))
    for big, part in places:
        hi_ref[big, c, pl.ds(row, count), part * LANES : (part + 1) * LANES] = high
        lo_ref[big, c, pl.ds(row, count), part * LANES : (part + 1) * LANES] = low


GROUP = 2


def in_plane(group, rows, w_ref, hi_ref, lo_ref, xy_ref):
    span = slice(group * GROUP, (group + 1) * GROUP)
    high = hi_ref[span, :, :rows, :].reshape(GROUP * 4 * rows, WINDOW)
    low = lo_ref[span, :, :rows, :].reshape(GROUP * 4 * rows, WINDOW)
    total = jnp.dot(
        jnp.concatenate([high, low], axis=1), w_ref[...], preferred_element_type=jnp.float32
    )
    for half in range(2):
        xy_ref[span, :, half, :rows, :] = total[:, half * LANES : (half + 1) * LANES].reshape(
            GROUP, 4, rows, LANES
        )


def in_plane_steps(rows, w_ref, hi_ref, lo_ref, xy_ref):
    groups = 4 // GROUP
    in_plane(0, rows, w_ref, hi_ref, lo_ref, xy_ref)
    for group in range(groups):
        if group + 1 < groups:
            in_plane(group + 1, rows, w_ref, hi_ref, lo_ref, xy_ref)
        for j in range(group * GROUP * 2, (group + 1) * GROUP * 2):
            yield j


def neighbours(ref, xy, c, j, start, xy_start, count):
    total = xy[j // 2, c, j % 2, pl.ds(xy_start, count), :]
    for k in range(1, REACH + 1):
        pair = ref[c, j, pl.ds(start + k, count), :] + ref[c, j, pl.ds(start - k, count), :]
        total = total + (pair if k == 1 else near_coef[k] * pair)
    return total


def slope(f, kin, pr, pi):
    upper_re = kin[0] + pr * f[2] - pi * f[3]
    upper_im = kin[1] + pr * f[3] + pi * f[2]
    lower_re = pr * f[0] + pi * f[1] - kin[2]
    lower_im = pr * f[1] - pi * f[0] - kin[3]
    return upper_im, upper_re, lower_im, lower_re


signs = (1.0, -1.0, 1.0, -1.0)


def chunks(rows, size=16):
    return [(r, min(size, rows - r)) for r in range(0, rows, size)]


def laplace_rows(src, start, xy_start, rows, planes, refs, store):
    w_ref, hi, lo, xy = refs
    tall = up16(rows + 2 * xy_start)
    margin = (planes + 32 - rows) // 2
    for j in in_plane_steps(tall, w_ref, hi, lo, xy):
        for r, count in chunks(rows):
            f = [src[c, j, pl.ds(start + r, count), :] for c in range(4)]
            near = [neighbours(src, xy, c, j, start + r, xy_start + r, count) for c in range(4)]
            store(j, r, count, margin + r, f, near)


def derivative(pd, j, row, count, f, near):
    pot, pr, pi = [pd[i, j, pl.ds(row, count), :] for i in range(3)]
    return slope(f, [unit_coef * near[c] + pot * f[c] for c in range(4)], pr, pi)


def stage_store(b0, pd, dst, factor, hi, lo):
    def store(j, r, count, row, f, near):
        k = derivative(pd, j, row, count, f, near)
        for c in range(4):
            value = b0[c, j, pl.ds(row + 8, count), :] + (signs[c] * factor) * k[c]
            dst[c, j, pl.ds(r, count), :] = value
            put_split(value, c, j, r, hi, lo)

    return store


def first_kernel(pieces, planes, *refs):
    n = len(pieces)
    parts, w_ref = refs[:n], refs[n]
    b0, pd, b1, hi_b, lo_b, hi_a, lo_a, xy = refs[n + 1 :]
    odd = lax.rem(lax.axis_index("grid"), 2)
    half = lax.rem(lax.axis_index("modes"), 2)
    zero = jnp.zeros((8, LANES), jnp.float32)
    for c in range(4):
        for j in range(8):
            b0[c, j, 0:8, :] = zero
            b0[c, j, planes + 40 : planes + 48, :] = zero

    for ref, (first, channels, count, row_even, row_odd, flip) in zip(parts, pieces):
        row = row_even
        if row_odd != row_even:
            row = pl.multiple_of(row_even + odd * (row_odd - row_even), 16)
        if flip is not None:
            row = pl.multiple_of(row + (half if flip == 0 else 1 - half) * count, 8)
        for i in range(channels):
            c = first + i
            for j in range(8):
                value = ref[i, :, j * LANES : (j + 1) * LANES]
                if c < 4:
                    b0[c, j, pl.ds(row + 8, count), :] = value
                    put_split(value, c, j, row, hi_a, lo_a)
                else:
                    pd[c - 4, j, pl.ds(row, count), :] = value + centre_coef if c == 4 else value

    store = stage_store(b0, pd, b1, 0.5 * time_step, hi_b, lo_b)
    laplace_rows(b0, 8, 0, planes + 32, planes, (w_ref, hi_a, lo_a, xy), store)


def stages_kernel(far, planes, low_bits, *refs):
    lead_ref, tail_ref, b0, pd = refs[:4]
    w_ref = refs[7]
    psi1_ref, kin1_ref, sums_ref, b1, hi_b, lo_b = refs[8:14]
    b2, b3, b4, hi_a, lo_a, xy, past = refs[14:]
    quarter = lax.rem(lax.axis_index("modes"), low_bits)

    zero = jnp.zeros((8, LANES), jnp.float32)
    for c in range(4):
        for j in range(8):
            lanes = slice(j * LANES, (j + 1) * LANES)
            past[c, j, 4:12, :] = zero
            past[c, j, 16:24, :] = zero
            past[c, j, 0:REACH, :] = lead_ref[c, far[0] : far[0] + REACH, lanes]
            past[c, j, 24 : 24 + REACH, :] = tail_ref[c, far[1] : far[1] + REACH, lanes]
    scale = 0.5 * time_step * unit_coef
    for j in range(8):
        for row, begin, sign in ((0, 4, -1), (planes + 24, 16, 1)):
            change = []
            for c in range(4):
                total = past[c, j, pl.ds(begin + sign, 8), :]
                for k in range(2, REACH + 1):
                    total = total + near_coef[k] * past[c, j, pl.ds(begin + sign * k, 8), :]
                change.append(scale * total)
            for c, delta in enumerate((change[1], -change[0], -change[3], change[2])):
                value = b1[c, j, row : row + 8, :] + delta
                b1[c, j, row : row + 8, :] = value
                put_split(value, c, j, row, hi_b, lo_b)

    def run(src, start, xy_start, rows, hi, lo, store):
        laplace_rows(src, start, xy_start, rows, planes, (w_ref, hi, lo, xy), store)

    store = stage_store(b0, pd, b2, 0.5 * time_step, hi_a, lo_a)
    run(b1, 4, 4, planes + 24, hi_b, lo_b, store)
    store = stage_store(b0, pd, b3, time_step, hi_b, lo_b)
    run(b2, 4, 4, planes + 16, hi_a, lo_a, store)

    def last(j, r, count, row, f, near):
        k = derivative(pd, j, row, count, f, near)
        for c in range(4):
            early = (
                b1[c, j, pl.ds(r + 12, count), :]
                - b0[c, j, pl.ds(r + 20, count), :]
                + 2.0 * b2[c, j, pl.ds(r + 8, count), :]
                + f[c]
            )
            value = early * (1.0 / 3.0) + (signs[c] * time_step / 6.0) * k[c]
            b4[c, j, pl.ds(r, count), :] = value
            put_split(value, c, j, r, hi_a, lo_a)

    run(b3, 4, 4, planes + 8, hi_b, lo_b, last)

    def finish(j, r, count, row, f, near):
        full = [unit_coef * near[c] + centre_coef * f[c] for c in range(4)]
        for c in range(4):
            psi1_ref[c, j, pl.ds(r, count), :] = f[c]
            kin1_ref[c, j, pl.ds(r, count), :] = full[c]
        sums = (
            f[2] * f[2] + f[3] * f[3],
            f[2] * full[2] + f[3] * full[3],
            f[0] * f[2] + f[1] * f[3],
            f[1] * f[2] - f[0] * f[3],
        )
        place = lax.bitwise_xor(jnp.int32(j // 2), quarter) if low_bits == 4 else j // 2
        for s in range(4):
            sums_ref[place, j % 2, s, pl.ds(r, count), :] = sums[s]

    run(b4, 4, 4, planes, hi_a, lo_a, finish)


def middle_kernel(paired, planes, low_bits, *refs):
    pieces = refs[:low_bits]
    psi1, kin1 = refs[low_bits : low_bits + 2]
    mid, first_send, second_send, fields_out, fields_flat = refs[low_bits + 2 :]
    even = lax.rem(lax.axis_index("grid"), 2) == 0
    quarter = lax.rem(lax.axis_index("modes"), low_bits)
    per = 4 // low_bits
    for k in range(low_bits):
        for t in range(per):
            place = lax.bitwise_xor(quarter, k) * per + t
            for half in range(2):
                for i in range(4):
                    fields_flat[place, half, i] = pieces[k][t, half, i]

    for j in range(8):
        big, half = j // 2, j % 2
        now = [fields_flat[big, half, i] for i in range(4)]
        for i in range(4):
            fields_out[i, :, j * LANES : (j + 1) * LANES] = now[i]
        f = [psi1[c, j] for c in range(4)]
        q = slope(f, [kin1[c, j] + now[0] * f[c] for c in range(4)], now[1], now[2])
        for c in range(4):
            m = f[c] + (signs[c] * 0.5 * time_step) * q[c]
            mid[c, j] = m
            top, bottom = m[:REACH], m[planes - REACH :]
            if paired:
                a, b = jnp.where(even, top, bottom), jnp.where(even, bottom, top)
            else:
                a, b = top, bottom
            first_send[j, c * REACH : (c + 1) * REACH, :] = a
            second_send[j, c * REACH : (c + 1) * REACH, :] = b


def inner_kernel(planes, *refs):
    psi1, kin1, mid, fields_flat, w_ref, part_ref, pad, hi, lo, xy = refs
    tall = up16(planes)
    zero = jnp.zeros((8, LANES), jnp.float32)
    for c in range(4):
        for j in range(8):
            value = mid[c, j]
            pad[c, j, 0:8, :] = zero
            pad[c, j, 8 : 8 + planes, :] = value
            pad[c, j, 8 + planes : 16 + planes, :] = zero
            put_split(value, c, j, 0, hi, lo)

    for j in in_plane_steps(tall, w_ref, hi, lo, xy):
        for r, count in chunks(planes):
            pot, pr, pi = [fields_flat[j // 2, j % 2, i, pl.ds(r, count), :] for i in range(3)]
            f = [psi1[c, j, pl.ds(r, count), :] for c in range(4)]
            q1 = slope(f, [kin1[c, j, pl.ds(r, count), :] + pot * f[c] for c in range(4)], pr, pi)
            m = [pad[c, j, pl.ds(8 + r, count), :] for c in range(4)]
            pot = pot + centre_coef
            near = [neighbours(pad, xy, c, j, 8 + r, r, count) for c in range(4)]
            q2 = slope(m, [unit_coef * near[c] + pot * m[c] for c in range(4)], pr, pi)
            for c in range(4):
                part_ref[c, j, pl.ds(r, count), :] = f[c] + (signs[c] * time_step / 6.0) * (
                    q1[c] + 2.0 * q2[c]
                )


def edge_kernel(paired, planes, *refs):
    part, first, second, u_ref, v_ref = refs
    even = lax.rem(lax.axis_index("grid"), 2) == 0
    scale = -0.5 * alpha_coef * 2.0 * time_step / 6.0
    terms = ((0, 1, 1.0), (1, 0, -1.0), (2, 3, -1.0), (3, 2, 1.0))
    for j in range(8):
        a, b = first[j], second[j]
        if paired:
            before, after = jnp.where(even, a, b), jnp.where(even, b, a)
        else:
            before, after = b, a
        for out, src, sign in terms:
            lo_rows = before[src * REACH : (src + 1) * REACH]
            hi_rows = after[src * REACH : (src + 1) * REACH]
            lead, tail = [], []
            for r in range(REACH):
                lead.append(
                    sum(
                        stencil_coef[k] * lo_rows[r - k + REACH : r - k + REACH + 1]
                        for k in range(r + 1, REACH + 1)
                    )
                )
                tail.append(
                    sum(
                        stencil_coef[k] * hi_rows[r + k - REACH : r + k - REACH + 1]
                        for k in range(REACH - r, REACH + 1)
                    )
                )
            value = part[out, j]
            parts = [value[:REACH] + (sign * scale) * jnp.concatenate(lead, axis=0)]
            if planes > 2 * REACH:
                parts.append(value[REACH : planes - REACH])
            parts.append(value[planes - REACH :] + (sign * scale) * jnp.concatenate(tail, axis=0))
            ref = u_ref if out < 2 else v_ref
            ref[0, out % 2, :, j * LANES : (j + 1) * LANES] = jnp.concatenate(parts, axis=0)


def potentials(raw, modes_total):
    density = 2.0 * raw[:, :, 0] / modes_total
    kinetic = (-2.0 / kinetic_coef) * raw[:, :, 1] / modes_total
    anomal_re = raw[:, :, 2] / modes_total
    anomal_im = raw[:, :, 3] / modes_total
    dense_safe = density + epsilon
    fermi = 0.5 * jnp.power(3.0 * jnp.pi**2 * dense_safe, 2.0 / 3.0)
    anomal_sq = anomal_re * anomal_re + anomal_im * anomal_im
    third_root = jnp.power(dense_safe, -1.0 / 3.0)
    field_pot = beta_coef * fermi - gamma_coef / 3.0 * anomal_sq * third_root / dense_safe
    pair_re = -gamma_coef * anomal_re * third_root
    pair_im = -gamma_coef * anomal_im * third_root
    energy = (
        alpha_coef * kinetic / 2.0
        + 0.6 * beta_coef * dense_safe * fermi
        + gamma_coef * anomal_sq * third_root
    )
    return jnp.stack([field_pot, pair_re, pair_im, energy], axis=2)


def call(kernel, outs, scratch, args, aliases=None):
    vmem = pl.BlockSpec(memory_space=pltpu.VMEM)
    shapes = [o if isinstance(o[0], tuple) else (o, jnp.float32) for o in outs]
    flops = 2 * sum(int(np.prod(s)) for s, d in shapes)
    return pl.pallas_call(
        kernel,
        out_shape=tuple(jax.ShapeDtypeStruct(s, d) for s, d in shapes),
        in_specs=[vmem] * len(args),
        out_specs=tuple([vmem] * len(outs)),
        scratch_shapes=[pltpu.VMEM(s, d) for s, d in scratch],
        input_output_aliases=aliases or {},
        compiler_params=pltpu.CompilerParams(vmem_limit_bytes=32 << 20),
        cost_estimate=pl.CostEstimate(flops=1000 * flops, bytes_accessed=4 * flops, transcendentals=0),
    )(*args)


def exchange_xor(x, axis, bits, count):
    return lax.ppermute(x, axis, [(i, i ^ bits) for i in range(count)])


def local(u_modes, v_modes, potential, pairing):
    planes = u_modes.shape[2]
    slabs = lax.axis_size("grid")
    modes = lax.axis_size("modes")
    low_bits = 4 if modes % 4 == 0 else 1
    paired = slabs == 4 and planes == 16 and low_bits == 4
    f32, bf16 = jnp.float32, jnp.bfloat16
    weights = jnp.asarray(in_plane_matrix())
    frozen = jnp.concatenate([potential[None], pairing], axis=0)
    psi = (u_modes[0], v_modes[0])

    cross = [(i, (i - 1 if i % 2 == 0 else i + 1) % slabs) for i in range(slabs)]
    up = [(i, (i + 1) % slabs) for i in range(slabs)]
    down = [(j, i) for i, j in up]
    pieces = [(0, 2, planes, 16, 16, None), (2, 2, planes, 16, 16, None), (4, 3, planes, 16, 16, None)]
    arrays = [*psi, frozen]
    if paired:
        part = planes // 2
        upper = lax.rem(lax.axis_index("modes"), 2) == 1
        mine = lax.ppermute(jnp.where(upper, frozen[:, part:], frozen[:, :part]), "grid", cross)
        far_u, far_v = [lax.ppermute(x, "grid", cross) for x in psi]
        near_u, near_v, near_f = [
            exchange_xor(x, "grid", 1, slabs) for x in (*psi, frozen)
        ]
        other = exchange_xor(mine, "modes", 1, modes)
        far_u, far_v, other = lax.optimization_barrier((far_u, far_v, other))
        lead, tail = 16 - planes, 16 + planes
        pieces += [
            (0, 2, planes, tail, lead, None),
            (2, 2, planes, tail, lead, None),
            (4, 3, planes, tail, lead, None),
            (4, 3, part, lead, tail, 0),
            (4, 3, part, lead, tail, 1),
            (0, 2, planes, lead, tail, None),
            (2, 2, planes, lead, tail, None),
        ]
        arrays += [near_u, near_v, near_f, mine, other, far_u, far_v]
        both = jnp.concatenate(
            [
                jnp.concatenate([x[:, :REACH], x[:, planes - REACH :]], axis=1)
                for x in (far_u, far_v)
            ],
            axis=0,
        )
        lead_far = tail_far = exchange_xor(both, "grid", 1, slabs)
        far = (REACH, 0)
    else:
        own = jnp.concatenate([*psi, frozen], axis=0)
        reach, step = 0, 0
        while reach < 5 * REACH:
            step += 1
            count = min(planes, 5 * REACH - reach)
            wide = 7 if reach < 4 * REACH else 4
            before = lax.ppermute(
                own[:wide, planes - count :], "grid", [(i, (i + step) % slabs) for i in range(slabs)]
            )
            after = lax.ppermute(
                own[:wide, :count], "grid", [((i + step) % slabs, i) for i in range(slabs)]
            )
            lead, tail = 16 - reach - count, 16 + planes + reach
            if wide == 7:
                pieces += [(0, 7, count, lead, lead, None), (0, 7, count, tail, tail, None)]
                arrays += [before, after]
            else:
                lead_far, tail_far, far = before, after, (0, 0)
            reach += count

    tall = up16(planes + 32)
    state = (4, 8, planes, LANES)
    split = ((4, 4, tall, WINDOW), bf16)
    b0, pd, b1, hi, lo = call(
        functools.partial(first_kernel, pieces, planes),
        [
            (4, 8, tall + 16, LANES),
            (3, 8, tall, LANES),
            (4, 8, tall + 8, LANES),
            split,
            split,
        ],
        [split, split, ((4, 4, 2, tall, LANES), f32)],
        arrays + [weights],
    )
    inputs = [lead_far, tail_far, b0, pd, b1, hi, lo, weights]
    psi1, kin1, sums, *rest = call(
        functools.partial(stages_kernel, far, planes, low_bits),
        [state, state, (4, 2, 4, planes, LANES), b1.shape, split, split],
        [
            ((4, 8, tall + 8, LANES), f32),
            ((4, 8, tall + 8, LANES), f32),
            ((4, 8, tall + 8, LANES), f32),
            split,
            split,
            ((4, 4, 2, tall, LANES), f32),
            ((4, 8, 32, LANES), f32),
        ],
        inputs,
        {4: 3, 5: 4, 6: 5},
    )

    if low_bits == 4:
        total = sums[0:1]
        for k in (1, 2, 3):
            total = total + exchange_xor(sums[k : k + 1], "modes", k, modes)
    else:
        total = sums
    bits = low_bits
    while bits < modes:
        total = total + exchange_xor(total, "modes", bits, modes)
        bits *= 2
    quarter = potentials(total, float(u_modes.shape[0] * modes))
    got = [quarter] + [exchange_xor(quarter, "modes", k, modes) for k in range(1, low_bits)]

    edge = (8, 4 * REACH, LANES)
    mid, first, second, fields, fields_flat = call(
        functools.partial(middle_kernel, paired, planes, low_bits),
        [state, edge, edge, (4, planes, NX * NY), (4, 2, 4, planes, LANES)],
        [],
        got + [psi1, kin1],
    )
    if paired:
        first = lax.ppermute(first, "grid", cross)
        second = exchange_xor(second, "grid", 1, slabs)
    else:
        first = lax.ppermute(first, "grid", down)
        second = lax.ppermute(second, "grid", up)
    flat = up16(planes)
    (part,) = call(
        functools.partial(inner_kernel, planes),
        [state],
        [
            ((4, 8, flat + 16, LANES), f32),
            ((4, 4, flat, WINDOW), bf16),
            ((4, 4, flat, WINDOW), bf16),
            ((4, 4, 2, flat, LANES), f32),
        ],
        [psi1, kin1, mid, fields_flat, weights],
    )
    u_next, v_next = call(
        functools.partial(edge_kernel, paired, planes),
        [u_modes.shape, v_modes.shape],
        [],
        [part, first, second],
    )
    return u_next, v_next, fields


def solution(mesh):
    wide = P("modes", None, "grid", None)
    return jax.shard_map(
        local,
        mesh=mesh,
        in_specs=(wide, wide, P("grid", None), P(None, "grid", None)),
        out_specs=(wide, wide, P(None, "grid", None)),
        check_vma=False,
    )
```

```python
import functools

import jax
import jax.numpy as jnp
import numpy as np
from jax import lax
from jax.experimental import pallas as pl
from jax.experimental.pallas import tpu as pltpu
from jax.sharding import PartitionSpec as P


NX = 32
NY = 32

stencil_coef = (-205.0 / 72.0, 8.0 / 5.0, -1.0 / 5.0, 8.0 / 315.0, -1.0 / 560.0)
alpha_coef = 1.14
beta_coef = -0.553
gamma_coef = -11.11
time_step = 0.18
epsilon = 1e-06

REACH = 4
LANES = 128
BLOCK = 256
WINDOW = BLOCK + 2 * LANES
kinetic_coef = -0.5 * alpha_coef
unit = stencil_coef[1]
near_coef = tuple(c / unit for c in stencil_coef)
unit_coef = kinetic_coef * unit
centre_coef = 3.0 * kinetic_coef * stencil_coef[0]


def in_plane_matrix():
    rows_out = BLOCK // NX
    mat = np.zeros((WINDOW, BLOCK), np.float64)
    for y in range(rows_out):
        for x in range(NX):
            out = y * NX + x
            for k in range(1, REACH + 1):
                for sign in (-1, 1):
                    mat[(y + REACH) * NX + (x + sign * k) % NX, out] += near_coef[k]
                    mat[(y + REACH + sign * k) * NX + x, out] += near_coef[k]
    mat = mat.astype(jnp.bfloat16)
    return np.concatenate([mat, mat], axis=0)


def up16(n):
    return -(-n // 16) * 16


def put_split(value, c, j, row, hi_ref, lo_ref):
    count = value.shape[0]
    high = value.astype(jnp.bfloat16)
    low = (value - high.astype(jnp.float32)).astype(jnp.bfloat16)
    if j % 2 == 0:
        places = ((j // 2, 1), ((j // 2 + 3) % 4, 3))
    else:
        places = ((j // 2, 2), ((j // 2 + 1) % 4, 0))
    for big, part in places:
        hi_ref[big, c, pl.ds(row, count), part * LANES : (part + 1) * LANES] = high
        lo_ref[big, c, pl.ds(row, count), part * LANES : (part + 1) * LANES] = low


GROUP = 2


def in_plane(group, rows, w_ref, hi_ref, lo_ref, xy_ref):
    span = slice(group * GROUP, (group + 1) * GROUP)
    high = hi_ref[span, :, :rows, :].reshape(GROUP * 4 * rows, WINDOW)
    low = lo_ref[span, :, :rows, :].reshape(GROUP * 4 * rows, WINDOW)
    total = jnp.dot(
        jnp.concatenate([high, low], axis=1), w_ref[...], preferred_element_type=jnp.float32
    )
    for half in range(2):
        xy_ref[span, :, half, :rows, :] = total[:, half * LANES : (half + 1) * LANES].reshape(
            GROUP, 4, rows, LANES
        )


def in_plane_steps(rows, w_ref, hi_ref, lo_ref, xy_ref):
    groups = 4 // GROUP
    in_plane(0, rows, w_ref, hi_ref, lo_ref, xy_ref)
    for group in range(groups):
        if group + 1 < groups:
            in_plane(group + 1, rows, w_ref, hi_ref, lo_ref, xy_ref)
        for j in range(group * GROUP * 2, (group + 1) * GROUP * 2):
            yield j


def neighbours(ref, xy, c, j, start, xy_start, count):
    total = xy[j // 2, c, j % 2, pl.ds(xy_start, count), :]
    for k in range(1, REACH + 1):
        pair = ref[c, j, pl.ds(start + k, count), :] + ref[c, j, pl.ds(start - k, count), :]
        total = total + (pair if k == 1 else near_coef[k] * pair)
    return total


def slope(f, kin, pr, pi):
    upper_re = kin[0] + pr * f[2] - pi * f[3]
    upper_im = kin[1] + pr * f[3] + pi * f[2]
    lower_re = pr * f[0] + pi * f[1] - kin[2]
    lower_im = pr * f[1] - pi * f[0] - kin[3]
    return upper_im, upper_re, lower_im, lower_re


signs = (1.0, -1.0, 1.0, -1.0)


def chunks(rows, size=16):
    return [(r, min(size, rows - r)) for r in range(0, rows, size)]


def laplace_rows(src, start, xy_start, rows, planes, refs, store):
    w_ref, hi, lo, xy = refs
    tall = up16(rows + 2 * xy_start)
    margin = (planes + 32 - rows) // 2
    for j in in_plane_steps(tall, w_ref, hi, lo, xy):
        for r, count in chunks(rows):
            f = [src[c, j, pl.ds(start + r, count), :] for c in range(4)]
            near = [neighbours(src, xy, c, j, start + r, xy_start + r, count) for c in range(4)]
            store(j, r, count, margin + r, f, near)


def derivative(pd, j, row, count, f, near):
    pot, pr, pi = [pd[i, j, pl.ds(row, count), :] for i in range(3)]
    return slope(f, [unit_coef * near[c] + pot * f[c] for c in range(4)], pr, pi)


def stage_store(b0, pd, dst, factor, hi, lo):
    def store(j, r, count, row, f, near):
        k = derivative(pd, j, row, count, f, near)
        for c in range(4):
            value = b0[c, j, pl.ds(row + 8, count), :] + (signs[c] * factor) * k[c]
            dst[c, j, pl.ds(r, count), :] = value
            put_split(value, c, j, r, hi, lo)

    return store


def first_kernel(pieces, planes, *refs):
    n = len(pieces)
    parts, w_ref = refs[:n], refs[n]
    b0, pd, b1, hi_b, lo_b, hi_a, lo_a, xy = refs[n + 1 :]
    odd = lax.rem(lax.axis_index("grid"), 2)
    half = lax.rem(lax.axis_index("modes"), 2)
    zero = jnp.zeros((8, LANES), jnp.float32)
    for c in range(4):
        for j in range(8):
            b0[c, j, 0:8, :] = zero
            b0[c, j, planes + 40 : planes + 48, :] = zero

    for ref, (first, channels, count, row_even, row_odd, flip) in zip(parts, pieces):
        row = row_even
        if row_odd != row_even:
            row = pl.multiple_of(row_even + odd * (row_odd - row_even), 16)
        if flip is not None:
            row = pl.multiple_of(row + (half if flip == 0 else 1 - half) * count, 8)
        for i in range(channels):
            c = first + i
            for j in range(8):
                value = ref[i, :, j * LANES : (j + 1) * LANES]
                if c < 4:
                    b0[c, j, pl.ds(row + 8, count), :] = value
                    put_split(value, c, j, row, hi_a, lo_a)
                else:
                    pd[c - 4, j, pl.ds(row, count), :] = value + centre_coef if c == 4 else value

    store = stage_store(b0, pd, b1, 0.5 * time_step, hi_b, lo_b)
    laplace_rows(b0, 8, 0, planes + 32, planes, (w_ref, hi_a, lo_a, xy), store)


def stages_kernel(far, planes, low_bits, *refs):
    lead_ref, tail_ref, b0, pd = refs[:4]
    w_ref = refs[7]
    psi1_ref, kin1_ref, sums_ref, b1, hi_b, lo_b = refs[8:14]
    b2, b3, b4, hi_a, lo_a, xy, past = refs[14:]
    quarter = lax.rem(lax.axis_index("modes"), low_bits)

    zero = jnp.zeros((8, LANES), jnp.float32)
    for c in range(4):
        for j in range(8):
            lanes = slice(j * LANES, (j + 1) * LANES)
            past[c, j, 4:12, :] = zero
            past[c, j, 16:24, :] = zero
            past[c, j, 0:REACH, :] = lead_ref[c, far[0] : far[0] + REACH, lanes]
            past[c, j, 24 : 24 + REACH, :] = tail_ref[c, far[1] : far[1] + REACH, lanes]
    scale = 0.5 * time_step * unit_coef
    for j in range(8):
        for row, begin, sign in ((0, 4, -1), (planes + 24, 16, 1)):
            change = []
            for c in range(4):
                total = past[c, j, pl.ds(begin + sign, 8), :]
                for k in range(2, REACH + 1):
                    total = total + near_coef[k] * past[c, j, pl.ds(begin + sign * k, 8), :]
                change.append(scale * total)
            for c, delta in enumerate((change[1], -change[0], -change[3], change[2])):
                value = b1[c, j, row : row + 8, :] + delta
                b1[c, j, row : row + 8, :] = value
                put_split(value, c, j, row, hi_b, lo_b)

    def run(src, start, xy_start, rows, hi, lo, store):
        laplace_rows(src, start, xy_start, rows, planes, (w_ref, hi, lo, xy), store)

    store = stage_store(b0, pd, b2, 0.5 * time_step, hi_a, lo_a)
    run(b1, 4, 4, planes + 24, hi_b, lo_b, store)
    store = stage_store(b0, pd, b3, time_step, hi_b, lo_b)
    run(b2, 4, 4, planes + 16, hi_a, lo_a, store)

    def last(j, r, count, row, f, near):
        k = derivative(pd, j, row, count, f, near)
        for c in range(4):
            early = (
                b1[c, j, pl.ds(r + 12, count), :]
                - b0[c, j, pl.ds(r + 20, count), :]
                + 2.0 * b2[c, j, pl.ds(r + 8, count), :]
                + f[c]
            )
            value = early * (1.0 / 3.0) + (signs[c] * time_step / 6.0) * k[c]
            b4[c, j, pl.ds(r, count), :] = value
            put_split(value, c, j, r, hi_a, lo_a)

    run(b3, 4, 4, planes + 8, hi_b, lo_b, last)

    def finish(j, r, count, row, f, near):
        full = [unit_coef * near[c] + centre_coef * f[c] for c in range(4)]
        for c in range(4):
            psi1_ref[c, j, pl.ds(r, count), :] = f[c]
            kin1_ref[c, j, pl.ds(r, count), :] = full[c]
        sums = (
            f[2] * f[2] + f[3] * f[3],
            f[2] * full[2] + f[3] * full[3],
            f[0] * f[2] + f[1] * f[3],
            f[1] * f[2] - f[0] * f[3],
        )
        place = lax.bitwise_xor(jnp.int32(j // 2), quarter) if low_bits == 4 else j // 2
        for s in range(4):
            sums_ref[place, j % 2, s, pl.ds(r, count), :] = sums[s]

    run(b4, 4, 4, planes, hi_a, lo_a, finish)


def middle_kernel(paired, planes, low_bits, *refs):
    pieces = refs[:low_bits]
    psi1, kin1 = refs[low_bits : low_bits + 2]
    mid, first_send, second_send, fields_flat = refs[low_bits + 2 :]
    even = lax.rem(lax.axis_index("grid"), 2) == 0
    quarter = lax.rem(lax.axis_index("modes"), low_bits)
    per = 4 // low_bits
    for k in range(low_bits):
        for t in range(per):
            place = lax.bitwise_xor(quarter, k) * per + t
            for half in range(2):
                for i in range(4):
                    fields_flat[place, half, i] = pieces[k][t, half, i]

    for j in range(8):
        big, half = j // 2, j % 2
        now = [fields_flat[big, half, i] for i in range(3)]
        f = [psi1[c, j] for c in range(4)]
        q = slope(f, [kin1[c, j] + now[0] * f[c] for c in range(4)], now[1], now[2])
        for c in range(4):
            m = f[c] + (signs[c] * 0.5 * time_step) * q[c]
            mid[c, j] = m
            top, bottom = m[:REACH], m[planes - REACH :]
            if paired:
                a, b = jnp.where(even, top, bottom), jnp.where(even, bottom, top)
            else:
                a, b = top, bottom
            first_send[j, c * REACH : (c + 1) * REACH, :] = a
            second_send[j, c * REACH : (c + 1) * REACH, :] = b


def inner_kernel(planes, *refs):
    psi1, kin1, mid, fields_flat, w_ref, part_ref, fields_out, pad, hi, lo, xy = refs
    tall = up16(planes)
    zero = jnp.zeros((8, LANES), jnp.float32)
    for j in range(8):
        for i in range(4):
            fields_out[i, :, j * LANES : (j + 1) * LANES] = fields_flat[j // 2, j % 2, i]
    for c in range(4):
        for j in range(8):
            value = mid[c, j]
            pad[c, j, 0:8, :] = zero
            pad[c, j, 8 : 8 + planes, :] = value
            pad[c, j, 8 + planes : 16 + planes, :] = zero
            put_split(value, c, j, 0, hi, lo)

    for j in in_plane_steps(tall, w_ref, hi, lo, xy):
        for r, count in chunks(planes):
            pot, pr, pi = [fields_flat[j // 2, j % 2, i, pl.ds(r, count), :] for i in range(3)]
            f = [psi1[c, j, pl.ds(r, count), :] for c in range(4)]
            q1 = slope(f, [kin1[c, j, pl.ds(r, count), :] + pot * f[c] for c in range(4)], pr, pi)
            m = [pad[c, j, pl.ds(8 + r, count), :] for c in range(4)]
            pot = pot + centre_coef
            near = [neighbours(pad, xy, c, j, 8 + r, r, count) for c in range(4)]
            q2 = slope(m, [unit_coef * near[c] + pot * m[c] for c in range(4)], pr, pi)
            for c in range(4):
                part_ref[c, j, pl.ds(r, count), :] = f[c] + (signs[c] * time_step / 6.0) * (
                    q1[c] + 2.0 * q2[c]
                )


def edge_kernel(paired, planes, *refs):
    part, first, second, u_ref, v_ref = refs
    even = lax.rem(lax.axis_index("grid"), 2) == 0
    scale = -0.5 * alpha_coef * 2.0 * time_step / 6.0
    terms = ((0, 1, 1.0), (1, 0, -1.0), (2, 3, -1.0), (3, 2, 1.0))
    for j in range(8):
        a, b = first[j], second[j]
        if paired:
            before, after = jnp.where(even, a, b), jnp.where(even, b, a)
        else:
            before, after = b, a
        for out, src, sign in terms:
            lo_rows = before[src * REACH : (src + 1) * REACH]
            hi_rows = after[src * REACH : (src + 1) * REACH]
            lead, tail = [], []
            for r in range(REACH):
                lead.append(
                    sum(
                        stencil_coef[k] * lo_rows[r - k + REACH : r - k + REACH + 1]
                        for k in range(r + 1, REACH + 1)
                    )
                )
                tail.append(
                    sum(
                        stencil_coef[k] * hi_rows[r + k - REACH : r + k - REACH + 1]
                        for k in range(REACH - r, REACH + 1)
                    )
                )
            value = part[out, j]
            parts = [value[:REACH] + (sign * scale) * jnp.concatenate(lead, axis=0)]
            if planes > 2 * REACH:
                parts.append(value[REACH : planes - REACH])
            parts.append(value[planes - REACH :] + (sign * scale) * jnp.concatenate(tail, axis=0))
            ref = u_ref if out < 2 else v_ref
            ref[0, out % 2, :, j * LANES : (j + 1) * LANES] = jnp.concatenate(parts, axis=0)


def potentials(raw, modes_total):
    density = 2.0 * raw[:, :, 0] / modes_total
    kinetic = (-2.0 / kinetic_coef) * raw[:, :, 1] / modes_total
    anomal_re = raw[:, :, 2] / modes_total
    anomal_im = raw[:, :, 3] / modes_total
    dense_safe = density + epsilon
    fermi = 0.5 * jnp.power(3.0 * jnp.pi**2 * dense_safe, 2.0 / 3.0)
    anomal_sq = anomal_re * anomal_re + anomal_im * anomal_im
    third_root = jnp.power(dense_safe, -1.0 / 3.0)
    field_pot = beta_coef * fermi - gamma_coef / 3.0 * anomal_sq * third_root / dense_safe
    pair_re = -gamma_coef * anomal_re * third_root
    pair_im = -gamma_coef * anomal_im * third_root
    energy = (
        alpha_coef * kinetic / 2.0
        + 0.6 * beta_coef * dense_safe * fermi
        + gamma_coef * anomal_sq * third_root
    )
    return jnp.stack([field_pot, pair_re, pair_im, energy], axis=2)


def call(kernel, outs, scratch, args, aliases=None):
    vmem = pl.BlockSpec(memory_space=pltpu.VMEM)
    shapes = [o if isinstance(o[0], tuple) else (o, jnp.float32) for o in outs]
    flops = 2 * sum(int(np.prod(s)) for s, d in shapes)
    return pl.pallas_call(
        kernel,
        out_shape=tuple(jax.ShapeDtypeStruct(s, d) for s, d in shapes),
        in_specs=[vmem] * len(args),
        out_specs=tuple([vmem] * len(outs)),
        scratch_shapes=[pltpu.VMEM(s, d) for s, d in scratch],
        input_output_aliases=aliases or {},
        compiler_params=pltpu.CompilerParams(vmem_limit_bytes=32 << 20),
        cost_estimate=pl.CostEstimate(flops=1000 * flops, bytes_accessed=4 * flops, transcendentals=0),
    )(*args)


def exchange_xor(x, axis, bits, count):
    return lax.ppermute(x, axis, [(i, i ^ bits) for i in range(count)])


def local(u_modes, v_modes, potential, pairing):
    planes = u_modes.shape[2]
    slabs = lax.axis_size("grid")
    modes = lax.axis_size("modes")
    low_bits = 4 if modes % 4 == 0 else 1
    paired = slabs == 4 and planes == 16 and low_bits == 4
    f32, bf16 = jnp.float32, jnp.bfloat16
    weights = jnp.asarray(in_plane_matrix())
    frozen = jnp.concatenate([potential[None], pairing], axis=0)
    psi = (u_modes[0], v_modes[0])

    cross = [(i, (i - 1 if i % 2 == 0 else i + 1) % slabs) for i in range(slabs)]
    up = [(i, (i + 1) % slabs) for i in range(slabs)]
    down = [(j, i) for i, j in up]
    pieces = [(0, 2, planes, 16, 16, None), (2, 2, planes, 16, 16, None), (4, 3, planes, 16, 16, None)]
    arrays = [*psi, frozen]
    if paired:
        part = planes // 2
        upper = lax.rem(lax.axis_index("modes"), 2) == 1
        mine = lax.ppermute(jnp.where(upper, frozen[:, part:], frozen[:, :part]), "grid", cross)
        far_u, far_v = [lax.ppermute(x, "grid", cross) for x in psi]
        near_u, near_v, near_f = [
            exchange_xor(x, "grid", 1, slabs) for x in (*psi, frozen)
        ]
        other = exchange_xor(mine, "modes", 1, modes)
        far_u, far_v, other = lax.optimization_barrier((far_u, far_v, other))
        lead, tail = 16 - planes, 16 + planes
        pieces += [
            (0, 2, planes, tail, lead, None),
            (2, 2, planes, tail, lead, None),
            (4, 3, planes, tail, lead, None),
            (4, 3, part, lead, tail, 0),
            (4, 3, part, lead, tail, 1),
            (0, 2, planes, lead, tail, None),
            (2, 2, planes, lead, tail, None),
        ]
        arrays += [near_u, near_v, near_f, mine, other, far_u, far_v]
        both = jnp.concatenate(
            [
                jnp.concatenate([x[:, :REACH], x[:, planes - REACH :]], axis=1)
                for x in (far_u, far_v)
            ],
            axis=0,
        )
        lead_far = tail_far = exchange_xor(both, "grid", 1, slabs)
        far = (REACH, 0)
    else:
        own = jnp.concatenate([*psi, frozen], axis=0)
        reach, step = 0, 0
        while reach < 5 * REACH:
            step += 1
            count = min(planes, 5 * REACH - reach)
            wide = 7 if reach < 4 * REACH else 4
            before = lax.ppermute(
                own[:wide, planes - count :], "grid", [(i, (i + step) % slabs) for i in range(slabs)]
            )
            after = lax.ppermute(
                own[:wide, :count], "grid", [((i + step) % slabs, i) for i in range(slabs)]
            )
            lead, tail = 16 - reach - count, 16 + planes + reach
            if wide == 7:
                pieces += [(0, 7, count, lead, lead, None), (0, 7, count, tail, tail, None)]
                arrays += [before, after]
            else:
                lead_far, tail_far, far = before, after, (0, 0)
            reach += count

    tall = up16(planes + 32)
    state = (4, 8, planes, LANES)
    split = ((4, 4, tall, WINDOW), bf16)
    b0, pd, b1, hi, lo = call(
        functools.partial(first_kernel, pieces, planes),
        [
            (4, 8, tall + 16, LANES),
            (3, 8, tall, LANES),
            (4, 8, tall + 8, LANES),
            split,
            split,
        ],
        [split, split, ((4, 4, 2, tall, LANES), f32)],
        arrays + [weights],
    )
    inputs = [lead_far, tail_far, b0, pd, b1, hi, lo, weights]
    psi1, kin1, sums, *rest = call(
        functools.partial(stages_kernel, far, planes, low_bits),
        [state, state, (4, 2, 4, planes, LANES), b1.shape, split, split],
        [
            ((4, 8, tall + 8, LANES), f32),
            ((4, 8, tall + 8, LANES), f32),
            ((4, 8, tall + 8, LANES), f32),
            split,
            split,
            ((4, 4, 2, tall, LANES), f32),
            ((4, 8, 32, LANES), f32),
        ],
        inputs,
        {4: 3, 5: 4, 6: 5},
    )

    if low_bits == 4:
        total = sums[0:1]
        for k in (1, 2, 3):
            total = total + exchange_xor(sums[k : k + 1], "modes", k, modes)
    else:
        total = sums
    bits = low_bits
    while bits < modes:
        total = total + exchange_xor(total, "modes", bits, modes)
        bits *= 2
    quarter = potentials(total, float(u_modes.shape[0] * modes))
    got = [quarter] + [exchange_xor(quarter, "modes", k, modes) for k in range(1, low_bits)]

    edge = (8, 4 * REACH, LANES)
    mid, first, second, fields_flat = call(
        functools.partial(middle_kernel, paired, planes, low_bits),
        [state, edge, edge, (4, 2, 4, planes, LANES)],
        [],
        got + [psi1, kin1],
    )
    if paired:
        first = lax.ppermute(first, "grid", cross)
        second = exchange_xor(second, "grid", 1, slabs)
    else:
        first = lax.ppermute(first, "grid", down)
        second = lax.ppermute(second, "grid", up)
    flat = up16(planes)
    part, fields = call(
        functools.partial(inner_kernel, planes),
        [state, (4, planes, NX * NY)],
        [
            ((4, 8, flat + 16, LANES), f32),
            ((4, 4, flat, WINDOW), bf16),
            ((4, 4, flat, WINDOW), bf16),
            ((4, 4, 2, flat, LANES), f32),
        ],
        [psi1, kin1, mid, fields_flat, weights],
    )
    u_next, v_next = call(
        functools.partial(edge_kernel, paired, planes),
        [u_modes.shape, v_modes.shape],
        [],
        [part, first, second],
    )
    return u_next, v_next, fields


def solution(mesh):
    wide = P("modes", None, "grid", None)
    return jax.shard_map(
        local,
        mesh=mesh,
        in_specs=(wide, wide, P("grid", None), P(None, "grid", None)),
        out_specs=(wide, wide, P(None, "grid", None)),
        check_vma=False,
    )
```

```python
import functools

import jax
import jax.numpy as jnp
import numpy as np
from jax import lax
from jax.experimental import pallas as pl
from jax.experimental.pallas import tpu as pltpu
from jax.sharding import PartitionSpec as P


NX = 32
NY = 32

stencil_coef = (-205.0 / 72.0, 8.0 / 5.0, -1.0 / 5.0, 8.0 / 315.0, -1.0 / 560.0)
alpha_coef = 1.14
beta_coef = -0.553
gamma_coef = -11.11
time_step = 0.18
epsilon = 1e-06

REACH = 4
LANES = 128
BLOCK = 256
WINDOW = BLOCK + 2 * LANES
kinetic_coef = -0.5 * alpha_coef
unit = stencil_coef[1]
near_coef = tuple(c / unit for c in stencil_coef)
unit_coef = kinetic_coef * unit
centre_coef = 3.0 * kinetic_coef * stencil_coef[0]


def in_plane_matrix():
    rows_out = BLOCK // NX
    mat = np.zeros((WINDOW, BLOCK), np.float64)
    for y in range(rows_out):
        for x in range(NX):
            out = y * NX + x
            for k in range(1, REACH + 1):
                for sign in (-1, 1):
                    mat[(y + REACH) * NX + (x + sign * k) % NX, out] += near_coef[k]
                    mat[(y + REACH + sign * k) * NX + x, out] += near_coef[k]
    mat = mat.astype(jnp.bfloat16)
    return np.concatenate([mat, mat], axis=0)


def up16(n):
    return -(-n // 16) * 16


def put_split(value, c, j, row, hi_ref, lo_ref):
    count = value.shape[0]
    high = value.astype(jnp.bfloat16)
    low = (value - high.astype(jnp.float32)).astype(jnp.bfloat16)
    if j % 2 == 0:
        places = ((j // 2, 1), ((j // 2 + 3) % 4, 3))
    else:
        places = ((j // 2, 2), ((j // 2 + 1) % 4, 0))
    for big, part in places:
        hi_ref[big, c, pl.ds(row, count), part * LANES : (part + 1) * LANES] = high
        lo_ref[big, c, pl.ds(row, count), part * LANES : (part + 1) * LANES] = low


def in_plane(first, number, rows, w_ref, hi_ref, lo_ref, xy_ref):
    span = slice(first, first + number)
    high = hi_ref[span, :, :rows, :].reshape(number * 4 * rows, WINDOW)
    low = lo_ref[span, :, :rows, :].reshape(number * 4 * rows, WINDOW)
    total = jnp.dot(
        jnp.concatenate([high, low], axis=1), w_ref[...], preferred_element_type=jnp.float32
    )
    for half in range(2):
        xy_ref[span, :, half, :rows, :] = total[:, half * LANES : (half + 1) * LANES].reshape(
            number, 4, rows, LANES
        )


def neighbours(ref, xy, c, j, start, xy_start, count):
    total = xy[j // 2, c, j % 2, pl.ds(xy_start, count), :]
    for k in range(1, REACH + 1):
        pair = ref[c, j, pl.ds(start + k, count), :] + ref[c, j, pl.ds(start - k, count), :]
        total = total + (pair if k == 1 else near_coef[k] * pair)
    return total


def slope(f, kin, pr, pi):
    upper_re = kin[0] + pr * f[2] - pi * f[3]
    upper_im = kin[1] + pr * f[3] + pi * f[2]
    lower_re = pr * f[0] + pi * f[1] - kin[2]
    lower_im = pr * f[1] - pi * f[0] - kin[3]
    return upper_im, upper_re, lower_im, lower_re


signs = (1.0, -1.0, 1.0, -1.0)


def chunks(rows, size=16):
    return [(r, min(size, rows - r)) for r in range(0, rows, size)]


def pipeline(steps, planes, w_ref, xys):
    def product(s, big):
        _, _, xy_start, rows, hi, lo, _ = steps[s]
        in_plane(big % 4, 1, up16(rows + 2 * xy_start), w_ref, hi, lo, xys[s % 2])

    product(0, 0)
    for s, (src, start, xy_start, rows, hi, lo, store) in enumerate(steps):
        margin = (planes + 32 - rows) // 2
        for i in range(8):
            if s == 0 and i in (0, 2, 4):
                product(0, i // 2 + 1)
            j = (2 * s + i) % 8
            for r, count in chunks(rows):
                f = [src[c, j, pl.ds(start + r, count), :] for c in range(4)]
                near = [
                    neighbours(src, xys[s % 2], c, j, start + r, xy_start + r, count)
                    for c in range(4)
                ]
                store(j, r, count, margin + r, f, near)
            if s + 1 < len(steps):
                for ahead in {4: (1,), 6: (2,), 7: (3, 4)}.get(i, ()):
                    product(s + 1, s + ahead)


def derivative(pd, j, row, count, f, near):
    pot, pr, pi = [pd[i, j, pl.ds(row, count), :] for i in range(3)]
    return slope(f, [unit_coef * near[c] + pot * f[c] for c in range(4)], pr, pi)


def stage_store(b0, pd, dst, factor, hi, lo, base=None):
    def store(j, r, count, row, f, near):
        if base is not None:
            row = pl.multiple_of(base + r, 8)
        k = derivative(pd, j, row, count, f, near)
        for c in range(4):
            value = b0[c, j, pl.ds(row + 8, count), :] + (signs[c] * factor) * k[c]
            place = r if base is None else row
            dst[c, j, pl.ds(place, count), :] = value
            put_split(value, c, j, place, hi, lo)

    return store


def place_rows(ref, channel, row, b0, pd, hi, lo, split_row):
    for i in range(ref.shape[0]):
        c = channel + i
        for j in range(8):
            value = ref[i, :, j * LANES : (j + 1) * LANES]
            if c < 4:
                b0[c, j, pl.ds(pl.multiple_of(row + 8, 8), ref.shape[1]), :] = value
                put_split(value, c, j, split_row, hi, lo)
            else:
                value = value + centre_coef if c == 4 else value
                pd[c - 4, j, pl.ds(row, ref.shape[1]), :] = value


def clear_rows(b0, row):
    for c in range(4):
        for j in range(8):
            b0[c, j, pl.ds(row, 8), :] = jnp.zeros((8, LANES), jnp.float32)


def add_share(past, b1, hi, lo, row, terms):
    scale = 0.5 * time_step * unit_coef
    for j in range(8):
        change = []
        for c in range(4):
            total = None
            for begin, sign in terms:
                for k in range(1, REACH + 1):
                    value = past[c, j, pl.ds(begin + sign * k, 8), :]
                    value = value if k == 1 else near_coef[k] * value
                    total = value if total is None else total + value
            change.append(scale * total)
        for c, delta in enumerate((change[1], -change[0], -change[3], change[2])):
            value = b1[c, j, pl.ds(row, 8), :] + delta
            b1[c, j, pl.ds(row, 8), :] = value
            put_split(value, c, j, row, hi, lo)


LEAD, TAIL = (4, -1), (16, 1)


def clear_past(past):
    zero = jnp.zeros((8, LANES), jnp.float32)
    for c in range(4):
        for j in range(8):
            past[c, j, 4:12, :] = zero
            past[c, j, 16:24, :] = zero


def first_kernel(pieces, planes, *refs):
    n = len(pieces)
    parts, w_ref = refs[:n], refs[n]
    b0, pd, b1, hi_b, lo_b, hi_a, lo_a, *xys = refs[n + 1 :]
    clear_rows(b0, 0)
    clear_rows(b0, planes + 40)
    for ref, row in zip(parts, pieces):
        place_rows(ref, 0, row, b0, pd, hi_a, lo_a, row)
    store = stage_store(b0, pd, b1, 0.5 * time_step, hi_b, lo_b)
    pipeline([(b0, 8, 0, planes + 32, hi_a, lo_a, store)], planes, w_ref, xys)


def early_kernel(planes, *refs):
    parts, w_ref = refs[:8], refs[8]
    b0, pd, b1, hi_b, lo_b, hi_a, lo_a, *xys = refs[9:]
    odd = lax.rem(lax.axis_index("grid"), 2)
    base = pl.multiple_of((1 - odd) * planes, 16)
    clear_rows(b0, base)
    clear_rows(b0, pl.multiple_of(base + 2 * planes + 8, 8))
    for i, ref in enumerate(parts):
        inner = pl.multiple_of((odd if i < 4 else 1 - odd) * planes, 16)
        channel = (0, 2, 4, 5)[i % 4]
        place_rows(ref, channel, pl.multiple_of(base + inner, 16), b0, pd, hi_a, lo_a, inner)
    store = stage_store(b0, pd, b1, 0.5 * time_step, hi_b, lo_b, base)
    pipeline([(b0, base + 8, 0, 2 * planes, hi_a, lo_a, store)], planes, w_ref, xys)


def late_kernel(planes, *refs):
    far_u, far_v, mine, other = refs[:4]
    w_ref = refs[9]
    b0, pd, b1, hi_b, lo_b, hi_a, lo_a, past, *xys = refs[10:]
    odd = lax.rem(lax.axis_index("grid"), 2)
    half = lax.rem(lax.axis_index("modes"), 2)
    base = pl.multiple_of(odd * (2 * planes), 16)
    clear_rows(b0, pl.multiple_of(odd * (3 * planes + 8), 8))
    for ref, channel in ((far_u, 0), (far_v, 2)):
        place_rows(ref, channel, base, b0, pd, hi_a, lo_a, 0)
    for ref, which in ((mine, half), (other, 1 - half)):
        row = pl.multiple_of(base + which * (planes // 2), 8)
        place_rows(ref, 4, row, b0, pd, hi_a, lo_a, 0)
    store = stage_store(b0, pd, b1, 0.5 * time_step, hi_b, lo_b, base)
    pipeline([(b0, base + 8, 0, planes, hi_a, lo_a, store)], planes, w_ref, xys)

    clear_past(past)
    none = jnp.zeros((REACH, LANES), jnp.float32)
    for c in range(4):
        ref = far_u if c < 2 else far_v
        for j in range(8):
            lanes = slice(j * LANES, (j + 1) * LANES)
            ahead, behind = ref[c % 2, planes - REACH :, lanes], ref[c % 2, :REACH, lanes]
            past[c, j, 0:REACH, :] = jnp.where(odd == 0, ahead, none)
            past[c, j, 24 : 24 + REACH, :] = jnp.where(odd == 0, none, behind)
    row = pl.multiple_of(planes + odd * (planes - 8), 8)
    add_share(past, b1, hi_b, lo_b, row, (LEAD, TAIL))


def stages_kernel(far, planes, low_bits, *refs):
    lead_ref, tail_ref, b0, pd = refs[:4]
    w_ref = refs[7]
    psi1_ref, kin1_ref, sums_ref, b1, hi_b, lo_b = refs[8:14]
    b2, b3, b4, hi_a, lo_a, past, *xys = refs[14:]
    quarter = lax.rem(lax.axis_index("modes"), low_bits)

    clear_past(past)
    for c in range(4):
        for j in range(8):
            lanes = slice(j * LANES, (j + 1) * LANES)
            past[c, j, 0:REACH, :] = lead_ref[c, far[0] : far[0] + REACH, lanes]
            past[c, j, 24 : 24 + REACH, :] = tail_ref[c, far[1] : far[1] + REACH, lanes]
    add_share(past, b1, hi_b, lo_b, 0, (LEAD,))
    add_share(past, b1, hi_b, lo_b, planes + 24, (TAIL,))

    def last(j, r, count, row, f, near):
        k = derivative(pd, j, row, count, f, near)
        for c in range(4):
            early = (
                b1[c, j, pl.ds(r + 12, count), :]
                - b0[c, j, pl.ds(r + 20, count), :]
                + 2.0 * b2[c, j, pl.ds(r + 8, count), :]
                + f[c]
            )
            value = early * (1.0 / 3.0) + (signs[c] * time_step / 6.0) * k[c]
            b4[c, j, pl.ds(r, count), :] = value
            put_split(value, c, j, r, hi_a, lo_a)

    def finish(j, r, count, row, f, near):
        full = [unit_coef * near[c] + centre_coef * f[c] for c in range(4)]
        for c in range(4):
            psi1_ref[c, j, pl.ds(r, count), :] = f[c]
            kin1_ref[c, j, pl.ds(r, count), :] = full[c]
        sums = (
            f[2] * f[2] + f[3] * f[3],
            f[2] * full[2] + f[3] * full[3],
            f[0] * f[2] + f[1] * f[3],
            f[1] * f[2] - f[0] * f[3],
        )
        place = lax.bitwise_xor(jnp.int32(j // 2), quarter) if low_bits == 4 else j // 2
        for s in range(4):
            sums_ref[place, j % 2, s, pl.ds(r, count), :] = sums[s]

    second = stage_store(b0, pd, b2, 0.5 * time_step, hi_a, lo_a)
    third = stage_store(b0, pd, b3, time_step, hi_b, lo_b)
    steps = [
        (b1, 4, 4, planes + 24, hi_b, lo_b, second),
        (b2, 4, 4, planes + 16, hi_a, lo_a, third),
        (b3, 4, 4, planes + 8, hi_b, lo_b, last),
        (b4, 4, 4, planes, hi_a, lo_a, finish),
    ]
    pipeline(steps, planes, w_ref, xys)


def middle_kernel(paired, planes, low_bits, *refs):
    pieces = refs[:low_bits]
    psi1, kin1 = refs[low_bits : low_bits + 2]
    mid, first_send, second_send, fields_flat = refs[low_bits + 2 :]
    even = lax.rem(lax.axis_index("grid"), 2) == 0
    quarter = lax.rem(lax.axis_index("modes"), low_bits)
    per = 4 // low_bits
    for k in range(low_bits):
        for t in range(per):
            place = lax.bitwise_xor(quarter, k) * per + t
            for half in range(2):
                for i in range(4):
                    fields_flat[place, half, i] = pieces[k][t, half, i]

    for j in range(8):
        big, half = j // 2, j % 2
        now = [fields_flat[big, half, i] for i in range(3)]
        f = [psi1[c, j] for c in range(4)]
        q = slope(f, [kin1[c, j] + now[0] * f[c] for c in range(4)], now[1], now[2])
        for c in range(4):
            m = f[c] + (signs[c] * 0.5 * time_step) * q[c]
            mid[c, j] = m
            top, bottom = m[:REACH], m[planes - REACH :]
            if paired:
                a, b = jnp.where(even, top, bottom), jnp.where(even, bottom, top)
            else:
                a, b = top, bottom
            first_send[j, c * REACH : (c + 1) * REACH, :] = a
            second_send[j, c * REACH : (c + 1) * REACH, :] = b


def inner_kernel(planes, *refs):
    psi1, kin1, mid, fields_flat, w_ref, part_ref, fields_out, pad, hi, lo, xy = refs
    zero = jnp.zeros((8, LANES), jnp.float32)
    for j in range(8):
        for i in range(4):
            fields_out[i, :, j * LANES : (j + 1) * LANES] = fields_flat[j // 2, j % 2, i]
    for c in range(4):
        for j in range(8):
            value = mid[c, j]
            pad[c, j, 0:8, :] = zero
            pad[c, j, 8 : 8 + planes, :] = value
            pad[c, j, 8 + planes : 16 + planes, :] = zero
            put_split(value, c, j, 0, hi, lo)

    def store(j, r, count, row, m, near):
        pot, pr, pi = [fields_flat[j // 2, j % 2, i, pl.ds(r, count), :] for i in range(3)]
        f = [psi1[c, j, pl.ds(r, count), :] for c in range(4)]
        q1 = slope(f, [kin1[c, j, pl.ds(r, count), :] + pot * f[c] for c in range(4)], pr, pi)
        pot = pot + centre_coef
        q2 = slope(m, [unit_coef * near[c] + pot * m[c] for c in range(4)], pr, pi)
        for c in range(4):
            part_ref[c, j, pl.ds(r, count), :] = f[c] + (signs[c] * time_step / 6.0) * (
                q1[c] + 2.0 * q2[c]
            )

    pipeline([(pad, 8, 0, planes, hi, lo, store)], planes, w_ref, [xy])


def edge_kernel(paired, planes, *refs):
    part, first, second, u_ref, v_ref = refs
    even = lax.rem(lax.axis_index("grid"), 2) == 0
    scale = -0.5 * alpha_coef * 2.0 * time_step / 6.0
    terms = ((0, 1, 1.0), (1, 0, -1.0), (2, 3, -1.0), (3, 2, 1.0))
    for j in range(8):
        a, b = first[j], second[j]
        if paired:
            before, after = jnp.where(even, a, b), jnp.where(even, b, a)
        else:
            before, after = b, a
        for out, src, sign in terms:
            lo_rows = before[src * REACH : (src + 1) * REACH]
            hi_rows = after[src * REACH : (src + 1) * REACH]
            lead, tail = [], []
            for r in range(REACH):
                lead.append(
                    sum(
                        stencil_coef[k] * lo_rows[r - k + REACH : r - k + REACH + 1]
                        for k in range(r + 1, REACH + 1)
                    )
                )
                tail.append(
                    sum(
                        stencil_coef[k] * hi_rows[r + k - REACH : r + k - REACH + 1]
                        for k in range(REACH - r, REACH + 1)
                    )
                )
            value = part[out, j]
            parts = [value[:REACH] + (sign * scale) * jnp.concatenate(lead, axis=0)]
            if planes > 2 * REACH:
                parts.append(value[REACH : planes - REACH])
            parts.append(value[planes - REACH :] + (sign * scale) * jnp.concatenate(tail, axis=0))
            ref = u_ref if out < 2 else v_ref
            ref[0, out % 2, :, j * LANES : (j + 1) * LANES] = jnp.concatenate(parts, axis=0)


def potentials(raw, modes_total):
    density = 2.0 * raw[:, :, 0] / modes_total
    kinetic = (-2.0 / kinetic_coef) * raw[:, :, 1] / modes_total
    anomal_re = raw[:, :, 2] / modes_total
    anomal_im = raw[:, :, 3] / modes_total
    dense_safe = density + epsilon
    fermi = 0.5 * jnp.power(3.0 * jnp.pi**2 * dense_safe, 2.0 / 3.0)
    anomal_sq = anomal_re * anomal_re + anomal_im * anomal_im
    third_root = jnp.power(dense_safe, -1.0 / 3.0)
    field_pot = beta_coef * fermi - gamma_coef / 3.0 * anomal_sq * third_root / dense_safe
    pair_re = -gamma_coef * anomal_re * third_root
    pair_im = -gamma_coef * anomal_im * third_root
    energy = (
        alpha_coef * kinetic / 2.0
        + 0.6 * beta_coef * dense_safe * fermi
        + gamma_coef * anomal_sq * third_root
    )
    return jnp.stack([field_pot, pair_re, pair_im, energy], axis=2)


def call(kernel, outs, scratch, args, aliases=None):
    vmem = pl.BlockSpec(memory_space=pltpu.VMEM)
    shapes = [o if isinstance(o[0], tuple) else (o, jnp.float32) for o in outs]
    flops = 2 * sum(int(np.prod(s)) for s, d in shapes)
    return pl.pallas_call(
        kernel,
        out_shape=tuple(jax.ShapeDtypeStruct(s, d) for s, d in shapes),
        in_specs=[vmem] * len(args),
        out_specs=tuple([vmem] * len(outs)),
        scratch_shapes=[pltpu.VMEM(s, d) for s, d in scratch],
        input_output_aliases=aliases or {},
        compiler_params=pltpu.CompilerParams(vmem_limit_bytes=32 << 20),
        cost_estimate=pl.CostEstimate(flops=1000 * flops, bytes_accessed=4 * flops, transcendentals=0),
    )(*args)


def exchange_xor(x, axis, bits, count):
    return lax.ppermute(x, axis, [(i, i ^ bits) for i in range(count)])


def local(u_modes, v_modes, potential, pairing):
    planes = u_modes.shape[2]
    slabs = lax.axis_size("grid")
    modes = lax.axis_size("modes")
    low_bits = 4 if modes % 4 == 0 else 1
    paired = slabs == 4 and planes == 16 and low_bits == 4
    f32, bf16 = jnp.float32, jnp.bfloat16
    weights = jnp.asarray(in_plane_matrix())
    psi = (u_modes[0], v_modes[0])
    tall = up16(planes + 32)
    state = (4, 8, planes, LANES)
    split = ((4, 4, tall, WINDOW), bf16)
    product = ((4, 4, 2, tall, LANES), f32)
    past = ((4, 8, 32, LANES), f32)
    buffers = [
        (4, 8, tall + 16, LANES),
        (3, 8, tall, LANES),
        (4, 8, tall + 8, LANES),
        split,
        split,
    ]

    cross = [(i, (i - 1 if i % 2 == 0 else i + 1) % slabs) for i in range(slabs)]
    up = [(i, (i + 1) % slabs) for i in range(slabs)]
    down = [(j, i) for i, j in up]
    if paired:
        part = planes // 2
        upper = lax.rem(lax.axis_index("modes"), 2) == 1
        frozen = (potential[None], pairing)
        both = jnp.concatenate(frozen, axis=0)
        mine = lax.ppermute(
            jnp.where(upper, both[:, part:], both[:, :part]), "grid", cross
        )
        far_u, far_v = [lax.ppermute(x, "grid", cross) for x in psi]
        near = [exchange_xor(x, "grid", 1, slabs) for x in (*psi, *frozen)]
        other = exchange_xor(mine, "modes", 1, modes)
        ready = call(
            functools.partial(early_kernel, planes), buffers, [split, split, product], [*psi, *frozen, *near, weights]
        )
        far_u, far_v, other = lax.optimization_barrier((far_u, far_v, other))
        both = jnp.concatenate(
            [
                jnp.concatenate([x[:, :REACH], x[:, planes - REACH :]], axis=1)
                for x in (far_u, far_v)
            ],
            axis=0,
        )
        lead_far = tail_far = exchange_xor(both, "grid", 1, slabs)
        far = (REACH, 0)
        b0, pd, b1, hi, lo = call(
            functools.partial(late_kernel, planes),
            buffers,
            [split, split, past, product],
            [far_u, far_v, mine, other, *ready, weights],
            {4 + i: i for i in range(5)},
        )
    else:
        own = jnp.concatenate([*psi, potential[None], pairing], axis=0)
        pieces, arrays = [16], [own]
        reach, step = 0, 0
        while reach < 5 * REACH:
            step += 1
            count = min(planes, 5 * REACH - reach)
            wide = 7 if reach < 4 * REACH else 4
            before = lax.ppermute(
                own[:wide, planes - count :], "grid", [(i, (i + step) % slabs) for i in range(slabs)]
            )
            after = lax.ppermute(
                own[:wide, :count], "grid", [((i + step) % slabs, i) for i in range(slabs)]
            )
            if wide == 7:
                pieces += [16 - reach - count, 16 + planes + reach]
                arrays += [before, after]
            else:
                lead_far, tail_far, far = before, after, (0, 0)
            reach += count
        b0, pd, b1, hi, lo = call(
            functools.partial(first_kernel, pieces, planes), buffers, [split, split, product], arrays + [weights]
        )

    inputs = [lead_far, tail_far, b0, pd, b1, hi, lo, weights]
    psi1, kin1, sums, *rest = call(
        functools.partial(stages_kernel, far, planes, low_bits),
        [state, state, (4, 2, 4, planes, LANES), b1.shape, split, split],
        [
            ((4, 8, tall + 8, LANES), f32),
            ((4, 8, tall + 8, LANES), f32),
            ((4, 8, tall + 8, LANES), f32),
            split,
            split,
            past,
            product,
            product,
        ],
        inputs,
        {4: 3, 5: 4, 6: 5},
    )

    if low_bits == 4:
        total = sums[0:1]
        for k in (1, 2, 3):
            total = total + exchange_xor(sums[k : k + 1], "modes", k, modes)
    else:
        total = sums
    bits = low_bits
    while bits < modes:
        total = total + exchange_xor(total, "modes", bits, modes)
        bits *= 2
    quarter = potentials(total, float(u_modes.shape[0] * modes))
    got = [quarter] + [exchange_xor(quarter, "modes", k, modes) for k in range(1, low_bits)]

    edge = (8, 4 * REACH, LANES)
    mid, first, second, fields_flat = call(
        functools.partial(middle_kernel, paired, planes, low_bits),
        [state, edge, edge, (4, 2, 4, planes, LANES)],
        [],
        got + [psi1, kin1],
    )
    if paired:
        first = lax.ppermute(first, "grid", cross)
        second = exchange_xor(second, "grid", 1, slabs)
    else:
        first = lax.ppermute(first, "grid", down)
        second = lax.ppermute(second, "grid", up)
    flat = up16(planes)
    part, fields = call(
        functools.partial(inner_kernel, planes),
        [state, (4, planes, NX * NY)],
        [
            ((4, 8, flat + 16, LANES), f32),
            ((4, 4, flat, WINDOW), bf16),
            ((4, 4, flat, WINDOW), bf16),
            ((4, 4, 2, flat, LANES), f32),
        ],
        [psi1, kin1, mid, fields_flat, weights],
    )
    u_next, v_next = call(
        functools.partial(edge_kernel, paired, planes), [u_modes.shape, v_modes.shape], [], [part, first, second]
    )
    return u_next, v_next, fields


def solution(mesh):
    wide = P("modes", None, "grid", None)
    return jax.shard_map(
        local,
        mesh=mesh,
        in_specs=(wide, wide, P("grid", None), P(None, "grid", None)),
        out_specs=(wide, wide, P(None, "grid", None)),
        check_vma=False,
    )
```

```python
import functools

import jax
import jax.numpy as jnp
import numpy as np
from jax import lax
from jax.experimental import pallas as pl
from jax.experimental.pallas import tpu as pltpu
from jax.sharding import PartitionSpec as P


NX = 32
NY = 32

stencil_coef = (-205.0 / 72.0, 8.0 / 5.0, -1.0 / 5.0, 8.0 / 315.0, -1.0 / 560.0)
alpha_coef = 1.14
beta_coef = -0.553
gamma_coef = -11.11
time_step = 0.18
epsilon = 1e-06

REACH = 4
LANES = 128
BLOCK = 256
WINDOW = BLOCK + 2 * LANES
kinetic_coef = -0.5 * alpha_coef
unit = stencil_coef[1]
near_coef = tuple(c / unit for c in stencil_coef)
unit_coef = kinetic_coef * unit
centre_coef = 3.0 * kinetic_coef * stencil_coef[0]


def in_plane_matrix():
    rows_out = BLOCK // NX
    mat = np.zeros((WINDOW, BLOCK), np.float64)
    for y in range(rows_out):
        for x in range(NX):
            out = y * NX + x
            for k in range(1, REACH + 1):
                for sign in (-1, 1):
                    mat[(y + REACH) * NX + (x + sign * k) % NX, out] += near_coef[k]
                    mat[(y + REACH + sign * k) * NX + x, out] += near_coef[k]
    mat = mat.astype(jnp.bfloat16)
    return np.concatenate([mat, mat], axis=0)


def up16(n):
    return -(-n // 16) * 16


def put_split(value, c, j, row, hi_ref, lo_ref):
    count = value.shape[0]
    high = value.astype(jnp.bfloat16)
    low = (value - high.astype(jnp.float32)).astype(jnp.bfloat16)
    if j % 2 == 0:
        places = ((j // 2, 1), ((j // 2 + 3) % 4, 3))
    else:
        places = ((j // 2, 2), ((j // 2 + 1) % 4, 0))
    for big, part in places:
        hi_ref[big, c, pl.ds(row, count), part * LANES : (part + 1) * LANES] = high
        lo_ref[big, c, pl.ds(row, count), part * LANES : (part + 1) * LANES] = low


def in_plane(first, number, rows, w_ref, hi_ref, lo_ref, xy_ref):
    span = slice(first, first + number)
    high = hi_ref[span, :, :rows, :].reshape(number * 4 * rows, WINDOW)
    low = lo_ref[span, :, :rows, :].reshape(number * 4 * rows, WINDOW)
    total = jnp.dot(
        jnp.concatenate([high, low], axis=1), w_ref[...], preferred_element_type=jnp.float32
    )
    for half in range(2):
        xy_ref[span, :, half, :rows, :] = total[:, half * LANES : (half + 1) * LANES].reshape(
            number, 4, rows, LANES
        )


def neighbours(ref, xy, c, j, start, xy_start, count):
    total = xy[j // 2, c, j % 2, pl.ds(xy_start, count), :]
    for k in range(1, REACH + 1):
        pair = ref[c, j, pl.ds(start + k, count), :] + ref[c, j, pl.ds(start - k, count), :]
        total = total + (pair if k == 1 else near_coef[k] * pair)
    return total


def slope(f, kin, pr, pi):
    upper_re = kin[0] + pr * f[2] - pi * f[3]
    upper_im = kin[1] + pr * f[3] + pi * f[2]
    lower_re = pr * f[0] + pi * f[1] - kin[2]
    lower_im = pr * f[1] - pi * f[0] - kin[3]
    return upper_im, upper_re, lower_im, lower_re


signs = (1.0, -1.0, 1.0, -1.0)


def chunks(rows, size=16):
    return [(r, min(size, rows - r)) for r in range(0, rows, size)]


def pipeline(steps, planes, w_ref, xys, together=False):
    def product(s, big):
        _, _, xy_start, rows, hi, lo, _ = steps[s]
        in_plane(big % 4, 1, up16(rows + 2 * xy_start), w_ref, hi, lo, xys[s % 2])

    if together:
        src, start, xy_start, rows, hi, lo, store = steps[0]
        in_plane(0, 4, up16(rows), w_ref, hi, lo, xys[0])
    else:
        product(0, 0)
    for s, (src, start, xy_start, rows, hi, lo, store) in enumerate(steps):
        margin = (planes + 32 - rows) // 2
        for i in range(8):
            if s == 0 and i in (0, 2, 4) and not together:
                product(0, i // 2 + 1)
            j = (2 * s + i) % 8
            for r, count in chunks(rows):
                f = [src[c, j, pl.ds(start + r, count), :] for c in range(4)]
                near = [
                    neighbours(src, xys[s % 2], c, j, start + r, xy_start + r, count)
                    for c in range(4)
                ]
                store(j, r, count, margin + r, f, near)
            if s + 1 < len(steps):
                for ahead in {4: (1,), 6: (2,), 7: (3, 4)}.get(i, ()):
                    product(s + 1, s + ahead)


def derivative(pd, j, row, count, f, near):
    pot, pr, pi = [pd[i, j, pl.ds(row, count), :] for i in range(3)]
    return slope(f, [unit_coef * near[c] + pot * f[c] for c in range(4)], pr, pi)


def stage_store(b0, pd, dst, factor, hi, lo, base=None):
    def store(j, r, count, row, f, near):
        if base is not None:
            row = pl.multiple_of(base + r, 8)
        k = derivative(pd, j, row, count, f, near)
        for c in range(4):
            value = b0[c, j, pl.ds(row + 8, count), :] + (signs[c] * factor) * k[c]
            place = r if base is None else row
            dst[c, j, pl.ds(place, count), :] = value
            put_split(value, c, j, place, hi, lo)

    return store


def place_rows(ref, channel, row, b0, pd, hi, lo, split_row):
    for i in range(ref.shape[0]):
        c = channel + i
        for j in range(8):
            value = ref[i, :, j * LANES : (j + 1) * LANES]
            if c < 4:
                b0[c, j, pl.ds(pl.multiple_of(row + 8, 8), ref.shape[1]), :] = value
                put_split(value, c, j, split_row, hi, lo)
            else:
                value = value + centre_coef if c == 4 else value
                pd[c - 4, j, pl.ds(row, ref.shape[1]), :] = value


def clear_rows(b0, row):
    for c in range(4):
        for j in range(8):
            b0[c, j, pl.ds(row, 8), :] = jnp.zeros((8, LANES), jnp.float32)


def add_share(past, b1, hi, lo, row, terms):
    scale = 0.5 * time_step * unit_coef
    for j in range(8):
        change = []
        for c in range(4):
            total = None
            for begin, sign in terms:
                for k in range(1, REACH + 1):
                    value = past[c, j, pl.ds(begin + sign * k, 8), :]
                    value = value if k == 1 else near_coef[k] * value
                    total = value if total is None else total + value
            change.append(scale * total)
        for c, delta in enumerate((change[1], -change[0], -change[3], change[2])):
            value = b1[c, j, pl.ds(row, 8), :] + delta
            b1[c, j, pl.ds(row, 8), :] = value
            put_split(value, c, j, row, hi, lo)


LEAD, TAIL = (4, -1), (16, 1)


def clear_past(past):
    zero = jnp.zeros((8, LANES), jnp.float32)
    for c in range(4):
        for j in range(8):
            past[c, j, 4:12, :] = zero
            past[c, j, 16:24, :] = zero


def first_kernel(pieces, planes, *refs):
    n = len(pieces)
    parts, w_ref = refs[:n], refs[n]
    b0, pd, b1, hi_b, lo_b, hi_a, lo_a, *xys = refs[n + 1 :]
    clear_rows(b0, 0)
    clear_rows(b0, planes + 40)
    for ref, row in zip(parts, pieces):
        place_rows(ref, 0, row, b0, pd, hi_a, lo_a, row)
    store = stage_store(b0, pd, b1, 0.5 * time_step, hi_b, lo_b)
    pipeline([(b0, 8, 0, planes + 32, hi_a, lo_a, store)], planes, w_ref, xys, True)


def early_kernel(planes, *refs):
    own, near, w_ref = refs[:3]
    b0, pd, b1, hi_b, lo_b, hi_a, lo_a, xy = refs[3:]
    odd = lax.rem(lax.axis_index("grid"), 2)
    base = pl.multiple_of((1 - odd) * planes, 16)
    clear_rows(b0, base)
    clear_rows(b0, pl.multiple_of(base + 2 * planes + 8, 8))
    for ref, side in ((own, odd), (near, 1 - odd)):
        inner = pl.multiple_of(side * planes, 16)
        place_rows(ref, 0, pl.multiple_of(base + inner, 16), b0, pd, hi_a, lo_a, inner)
    store = stage_store(b0, pd, b1, 0.5 * time_step, hi_b, lo_b, base)
    pipeline([(b0, base + 8, 0, 2 * planes, hi_a, lo_a, store)], planes, w_ref, [xy], True)


def late_kernel(planes, *refs):
    far, mine, other = refs[:3]
    w_ref = refs[8]
    b0, pd, b1, hi_b, lo_b, hi_a, lo_a, past, *xys = refs[9:]
    odd = lax.rem(lax.axis_index("grid"), 2)
    half = lax.rem(lax.axis_index("modes"), 2)
    base = pl.multiple_of(odd * (2 * planes), 16)
    clear_rows(b0, pl.multiple_of(odd * (3 * planes + 8), 8))
    place_rows(far, 0, base, b0, pd, hi_a, lo_a, 0)
    for ref, which in ((mine, half), (other, 1 - half)):
        row = pl.multiple_of(base + which * (planes // 2), 8)
        place_rows(ref, 4, row, b0, pd, hi_a, lo_a, 0)
    store = stage_store(b0, pd, b1, 0.5 * time_step, hi_b, lo_b, base)
    pipeline([(b0, base + 8, 0, planes, hi_a, lo_a, store)], planes, w_ref, xys, True)

    clear_past(past)
    none = jnp.zeros((REACH, LANES), jnp.float32)
    for c in range(4):
        for j in range(8):
            lanes = slice(j * LANES, (j + 1) * LANES)
            ahead, behind = far[c, planes - REACH :, lanes], far[c, :REACH, lanes]
            past[c, j, 0:REACH, :] = jnp.where(odd == 0, ahead, none)
            past[c, j, 24 : 24 + REACH, :] = jnp.where(odd == 0, none, behind)
    row = pl.multiple_of(planes + odd * (planes - 8), 8)
    add_share(past, b1, hi_b, lo_b, row, (LEAD, TAIL))


def stages_kernel(far, planes, low_bits, *refs):
    lead_ref, tail_ref, b0, pd = refs[:4]
    w_ref = refs[7]
    psi1_ref, kin1_ref, sums_ref, b1, hi_b, lo_b = refs[8:14]
    b2, b3, b4, hi_a, lo_a, past, *xys = refs[14:]
    quarter = lax.rem(lax.axis_index("modes"), low_bits)

    clear_past(past)
    for c in range(4):
        for j in range(8):
            lanes = slice(j * LANES, (j + 1) * LANES)
            past[c, j, 0:REACH, :] = lead_ref[c, far[0] : far[0] + REACH, lanes]
            past[c, j, 24 : 24 + REACH, :] = tail_ref[c, far[1] : far[1] + REACH, lanes]
    add_share(past, b1, hi_b, lo_b, 0, (LEAD,))
    add_share(past, b1, hi_b, lo_b, planes + 24, (TAIL,))

    def last(j, r, count, row, f, near):
        k = derivative(pd, j, row, count, f, near)
        for c in range(4):
            early = (
                b1[c, j, pl.ds(r + 12, count), :]
                - b0[c, j, pl.ds(r + 20, count), :]
                + 2.0 * b2[c, j, pl.ds(r + 8, count), :]
                + f[c]
            )
            value = early * (1.0 / 3.0) + (signs[c] * time_step / 6.0) * k[c]
            b4[c, j, pl.ds(r, count), :] = value
            put_split(value, c, j, r, hi_a, lo_a)

    def finish(j, r, count, row, f, near):
        full = [unit_coef * near[c] + centre_coef * f[c] for c in range(4)]
        for c in range(4):
            psi1_ref[c, j, pl.ds(r, count), :] = f[c]
            kin1_ref[c, j, pl.ds(r, count), :] = full[c]
        sums = (
            f[2] * f[2] + f[3] * f[3],
            f[2] * full[2] + f[3] * full[3],
            f[0] * f[2] + f[1] * f[3],
            f[1] * f[2] - f[0] * f[3],
        )
        place = lax.bitwise_xor(jnp.int32(j // 2), quarter) if low_bits == 4 else j // 2
        for s in range(4):
            sums_ref[place, j % 2, s, pl.ds(r, count), :] = sums[s]

    second = stage_store(b0, pd, b2, 0.5 * time_step, hi_a, lo_a)
    third = stage_store(b0, pd, b3, time_step, hi_b, lo_b)
    steps = [
        (b1, 4, 4, planes + 24, hi_b, lo_b, second),
        (b2, 4, 4, planes + 16, hi_a, lo_a, third),
        (b3, 4, 4, planes + 8, hi_b, lo_b, last),
        (b4, 4, 4, planes, hi_a, lo_a, finish),
    ]
    pipeline(steps, planes, w_ref, xys)


def middle_kernel(paired, planes, low_bits, *refs):
    pieces = refs[:low_bits]
    psi1, kin1 = refs[low_bits : low_bits + 2]
    mid, first_send, second_send, fields_flat = refs[low_bits + 2 :]
    even = lax.rem(lax.axis_index("grid"), 2) == 0
    quarter = lax.rem(lax.axis_index("modes"), low_bits)
    per = 4 // low_bits
    for k in range(low_bits):
        for t in range(per):
            place = lax.bitwise_xor(quarter, k) * per + t
            for half in range(2):
                for i in range(4):
                    fields_flat[place, half, i] = pieces[k][t, half, i]

    for j in range(8):
        big, half = j // 2, j % 2
        now = [fields_flat[big, half, i] for i in range(3)]
        f = [psi1[c, j] for c in range(4)]
        q = slope(f, [kin1[c, j] + now[0] * f[c] for c in range(4)], now[1], now[2])
        for c in range(4):
            m = f[c] + (signs[c] * 0.5 * time_step) * q[c]
            mid[c, j] = m
            top, bottom = m[:REACH], m[planes - REACH :]
            if paired:
                a, b = jnp.where(even, top, bottom), jnp.where(even, bottom, top)
            else:
                a, b = top, bottom
            first_send[j, c * REACH : (c + 1) * REACH, :] = a
            second_send[j, c * REACH : (c + 1) * REACH, :] = b


def inner_kernel(planes, *refs):
    psi1, kin1, mid, fields_flat, w_ref, part_ref, fields_out, pad, hi, lo, xy = refs
    zero = jnp.zeros((8, LANES), jnp.float32)
    for j in range(8):
        for i in range(4):
            fields_out[i, :, j * LANES : (j + 1) * LANES] = fields_flat[j // 2, j % 2, i]
    for c in range(4):
        for j in range(8):
            value = mid[c, j]
            pad[c, j, 0:8, :] = zero
            pad[c, j, 8 : 8 + planes, :] = value
            pad[c, j, 8 + planes : 16 + planes, :] = zero
            put_split(value, c, j, 0, hi, lo)

    def store(j, r, count, row, m, near):
        pot, pr, pi = [fields_flat[j // 2, j % 2, i, pl.ds(r, count), :] for i in range(3)]
        f = [psi1[c, j, pl.ds(r, count), :] for c in range(4)]
        q1 = slope(f, [kin1[c, j, pl.ds(r, count), :] + pot * f[c] for c in range(4)], pr, pi)
        pot = pot + centre_coef
        q2 = slope(m, [unit_coef * near[c] + pot * m[c] for c in range(4)], pr, pi)
        for c in range(4):
            part_ref[c, j, pl.ds(r, count), :] = f[c] + (signs[c] * time_step / 6.0) * (
                q1[c] + 2.0 * q2[c]
            )

    pipeline([(pad, 8, 0, planes, hi, lo, store)], planes, w_ref, [xy])


def edge_kernel(paired, planes, *refs):
    part, first, second, u_ref, v_ref = refs
    even = lax.rem(lax.axis_index("grid"), 2) == 0
    scale = -0.5 * alpha_coef * 2.0 * time_step / 6.0
    terms = ((0, 1, 1.0), (1, 0, -1.0), (2, 3, -1.0), (3, 2, 1.0))
    for j in range(8):
        a, b = first[j], second[j]
        if paired:
            before, after = jnp.where(even, a, b), jnp.where(even, b, a)
        else:
            before, after = b, a
        for out, src, sign in terms:
            lo_rows = before[src * REACH : (src + 1) * REACH]
            hi_rows = after[src * REACH : (src + 1) * REACH]
            lead, tail = [], []
            for r in range(REACH):
                lead.append(
                    sum(
                        stencil_coef[k] * lo_rows[r - k + REACH : r - k + REACH + 1]
                        for k in range(r + 1, REACH + 1)
                    )
                )
                tail.append(
                    sum(
                        stencil_coef[k] * hi_rows[r + k - REACH : r + k - REACH + 1]
                        for k in range(REACH - r, REACH + 1)
                    )
                )
            value = part[out, j]
            parts = [value[:REACH] + (sign * scale) * jnp.concatenate(lead, axis=0)]
            if planes > 2 * REACH:
                parts.append(value[REACH : planes - REACH])
            parts.append(value[planes - REACH :] + (sign * scale) * jnp.concatenate(tail, axis=0))
            ref = u_ref if out < 2 else v_ref
            ref[0, out % 2, :, j * LANES : (j + 1) * LANES] = jnp.concatenate(parts, axis=0)


def potentials(raw, modes_total):
    density = 2.0 * raw[:, :, 0] / modes_total
    kinetic = (-2.0 / kinetic_coef) * raw[:, :, 1] / modes_total
    anomal_re = raw[:, :, 2] / modes_total
    anomal_im = raw[:, :, 3] / modes_total
    dense_safe = density + epsilon
    fermi = 0.5 * jnp.power(3.0 * jnp.pi**2 * dense_safe, 2.0 / 3.0)
    anomal_sq = anomal_re * anomal_re + anomal_im * anomal_im
    third_root = jnp.power(dense_safe, -1.0 / 3.0)
    field_pot = beta_coef * fermi - gamma_coef / 3.0 * anomal_sq * third_root / dense_safe
    pair_re = -gamma_coef * anomal_re * third_root
    pair_im = -gamma_coef * anomal_im * third_root
    energy = (
        alpha_coef * kinetic / 2.0
        + 0.6 * beta_coef * dense_safe * fermi
        + gamma_coef * anomal_sq * third_root
    )
    return jnp.stack([field_pot, pair_re, pair_im, energy], axis=2)


def call(kernel, outs, scratch, args, aliases=None):
    vmem = pl.BlockSpec(memory_space=pltpu.VMEM)
    shapes = [o if isinstance(o[0], tuple) else (o, jnp.float32) for o in outs]
    flops = 2 * sum(int(np.prod(s)) for s, d in shapes)
    return pl.pallas_call(
        kernel,
        out_shape=tuple(jax.ShapeDtypeStruct(s, d) for s, d in shapes),
        in_specs=[vmem] * len(args),
        out_specs=tuple([vmem] * len(outs)),
        scratch_shapes=[pltpu.VMEM(s, d) for s, d in scratch],
        input_output_aliases=aliases or {},
        compiler_params=pltpu.CompilerParams(vmem_limit_bytes=32 << 20),
        cost_estimate=pl.CostEstimate(flops=1000 * flops, bytes_accessed=4 * flops, transcendentals=0),
    )(*args)


def exchange_xor(x, axis, bits, count):
    return lax.ppermute(x, axis, [(i, i ^ bits) for i in range(count)])


def local(u_modes, v_modes, potential, pairing):
    planes = u_modes.shape[2]
    slabs = lax.axis_size("grid")
    modes = lax.axis_size("modes")
    low_bits = 4 if modes % 4 == 0 else 1
    paired = slabs == 4 and planes == 16 and low_bits == 4
    f32, bf16 = jnp.float32, jnp.bfloat16
    weights = jnp.asarray(in_plane_matrix())
    own = jnp.concatenate([u_modes[0], v_modes[0], potential[None], pairing], axis=0)
    own = lax.optimization_barrier(own)
    tall = up16(planes + 32)
    state = (4, 8, planes, LANES)
    split = ((4, 4, tall, WINDOW), bf16)
    product = ((4, 4, 2, tall, LANES), f32)
    past = ((4, 8, 32, LANES), f32)
    buffers = [
        (4, 8, tall + 16, LANES),
        (3, 8, tall, LANES),
        (4, 8, tall + 8, LANES),
        split,
        split,
    ]

    cross = [(i, (i - 1 if i % 2 == 0 else i + 1) % slabs) for i in range(slabs)]
    up = [(i, (i + 1) % slabs) for i in range(slabs)]
    down = [(j, i) for i, j in up]
    if paired:
        part = planes // 2
        upper = lax.rem(lax.axis_index("modes"), 2) == 1
        picked = jnp.where(upper, own[4:, part:], own[4:, :part])
        mine = lax.ppermute(picked, "grid", cross)
        far = lax.ppermute(own[:4], "grid", cross)
        near = exchange_xor(own, "grid", 1, slabs)
        other = exchange_xor(mine, "modes", 1, modes)
        ready = call(functools.partial(early_kernel, planes), buffers, [split, split, product], [own, near, weights])
        far, other = lax.optimization_barrier((far, other))
        both = jnp.concatenate([far[:, :REACH], far[:, planes - REACH :]], axis=1)
        lead_far = tail_far = exchange_xor(both, "grid", 1, slabs)
        past_rows = (REACH, 0)
        b0, pd, b1, hi, lo = call(
            functools.partial(late_kernel, planes),
            buffers,
            [split, split, past, product],
            [far, mine, other, *ready, weights],
            {3 + i: i for i in range(5)},
        )
    else:
        pieces, arrays = [16], [own]
        reach, step = 0, 0
        while reach < 5 * REACH:
            step += 1
            count = min(planes, 5 * REACH - reach)
            wide = 7 if reach < 4 * REACH else 4
            before = lax.ppermute(
                own[:wide, planes - count :], "grid", [(i, (i + step) % slabs) for i in range(slabs)]
            )
            after = lax.ppermute(
                own[:wide, :count], "grid", [((i + step) % slabs, i) for i in range(slabs)]
            )
            if wide == 7:
                pieces += [16 - reach - count, 16 + planes + reach]
                arrays += [before, after]
            else:
                lead_far, tail_far, past_rows = before, after, (0, 0)
            reach += count
        b0, pd, b1, hi, lo = call(
            functools.partial(first_kernel, pieces, planes), buffers, [split, split, product], arrays + [weights]
        )

    inputs = [lead_far, tail_far, b0, pd, b1, hi, lo, weights]
    psi1, kin1, sums, *rest = call(
        functools.partial(stages_kernel, past_rows, planes, low_bits),
        [state, state, (4, 2, 4, planes, LANES), b1.shape, split, split],
        [
            ((4, 8, tall + 8, LANES), f32),
            ((4, 8, tall + 8, LANES), f32),
            ((4, 8, tall + 8, LANES), f32),
            split,
            split,
            past,
            product,
            product,
        ],
        inputs,
        {4: 3, 5: 4, 6: 5},
    )

    if low_bits == 4:
        total = sums[0:1]
        for k in (1, 2, 3):
            total = total + exchange_xor(sums[k : k + 1], "modes", k, modes)
    else:
        total = sums
    bits = low_bits
    while bits < modes:
        total = total + exchange_xor(total, "modes", bits, modes)
        bits *= 2
    quarter = potentials(total, float(u_modes.shape[0] * modes))
    got = [quarter] + [exchange_xor(quarter, "modes", k, modes) for k in range(1, low_bits)]

    edge = (8, 4 * REACH, LANES)
    mid, first, second, fields_flat = call(
        functools.partial(middle_kernel, paired, planes, low_bits),
        [state, edge, edge, (4, 2, 4, planes, LANES)],
        [],
        got + [psi1, kin1],
    )
    if paired:
        first = lax.ppermute(first, "grid", cross)
        second = exchange_xor(second, "grid", 1, slabs)
    else:
        first = lax.ppermute(first, "grid", down)
        second = lax.ppermute(second, "grid", up)
    flat = up16(planes)
    part, fields = call(
        functools.partial(inner_kernel, planes),
        [state, (4, planes, NX * NY)],
        [
            ((4, 8, flat + 16, LANES), f32),
            ((4, 4, flat, WINDOW), bf16),
            ((4, 4, flat, WINDOW), bf16),
            ((4, 4, 2, flat, LANES), f32),
        ],
        [psi1, kin1, mid, fields_flat, weights],
    )
    u_next, v_next = call(
        functools.partial(edge_kernel, paired, planes), [u_modes.shape, v_modes.shape], [], [part, first, second]
    )
    return u_next, v_next, fields


def solution(mesh):
    wide = P("modes", None, "grid", None)
    return jax.shard_map(
        local,
        mesh=mesh,
        in_specs=(wide, wide, P("grid", None), P(None, "grid", None)),
        out_specs=(wide, wide, P(None, "grid", None)),
        check_vma=False,
    )
```

```python
import functools

import jax
import jax.numpy as jnp
import numpy as np
from jax import lax
from jax.experimental import pallas as pl
from jax.experimental.pallas import tpu as pltpu
from jax.sharding import PartitionSpec as P


NX = 32
NY = 32

stencil_coef = (-205.0 / 72.0, 8.0 / 5.0, -1.0 / 5.0, 8.0 / 315.0, -1.0 / 560.0)
alpha_coef = 1.14
beta_coef = -0.553
gamma_coef = -11.11
time_step = 0.18
epsilon = 1e-06

REACH = 4
LANES = 128
BLOCK = 256
WINDOW = BLOCK + 2 * LANES
kinetic_coef = -0.5 * alpha_coef
unit = stencil_coef[1]
near_coef = tuple(c / unit for c in stencil_coef)
unit_coef = kinetic_coef * unit
centre_coef = 3.0 * kinetic_coef * stencil_coef[0]


def in_plane_matrix():
    rows_out = BLOCK // NX
    mat = np.zeros((WINDOW, BLOCK), np.float64)
    for y in range(rows_out):
        for x in range(NX):
            out = y * NX + x
            for k in range(1, REACH + 1):
                for sign in (-1, 1):
                    mat[(y + REACH) * NX + (x + sign * k) % NX, out] += near_coef[k]
                    mat[(y + REACH + sign * k) * NX + x, out] += near_coef[k]
    mat = mat.astype(jnp.bfloat16)
    return np.concatenate([mat, mat], axis=0)


def up16(n):
    return -(-n // 16) * 16


def put_split(value, c, j, row, hi_ref, lo_ref):
    count = value.shape[0]
    high = value.astype(jnp.bfloat16)
    low = (value - high.astype(jnp.float32)).astype(jnp.bfloat16)
    if j % 2 == 0:
        places = ((j // 2, 1), ((j // 2 + 3) % 4, 3))
    else:
        places = ((j // 2, 2), ((j // 2 + 1) % 4, 0))
    for big, part in places:
        hi_ref[big, c, pl.ds(row, count), part * LANES : (part + 1) * LANES] = high
        lo_ref[big, c, pl.ds(row, count), part * LANES : (part + 1) * LANES] = low


def in_plane(first, number, rows, w_ref, hi_ref, lo_ref, xy_ref):
    span = slice(first, first + number)
    high = hi_ref[span, :, :rows, :].reshape(number * 4 * rows, WINDOW)
    low = lo_ref[span, :, :rows, :].reshape(number * 4 * rows, WINDOW)
    total = jnp.dot(
        jnp.concatenate([high, low], axis=1), w_ref[...], preferred_element_type=jnp.float32
    )
    for half in range(2):
        xy_ref[span, :, half, :rows, :] = total[:, half * LANES : (half + 1) * LANES].reshape(
            number, 4, rows, LANES
        )


def neighbours(ref, xy, c, j, start, xy_start, count):
    total = xy[j // 2, c, j % 2, pl.ds(xy_start, count), :]
    for k in range(1, REACH + 1):
        pair = ref[c, j, pl.ds(start + k, count), :] + ref[c, j, pl.ds(start - k, count), :]
        total = total + (pair if k == 1 else near_coef[k] * pair)
    return total


def slope(f, kin, pr, pi):
    upper_re = kin[0] + pr * f[2] - pi * f[3]
    upper_im = kin[1] + pr * f[3] + pi * f[2]
    lower_re = pr * f[0] + pi * f[1] - kin[2]
    lower_im = pr * f[1] - pi * f[0] - kin[3]
    return upper_im, upper_re, lower_im, lower_re


signs = (1.0, -1.0, 1.0, -1.0)


def chunks(rows, size=16):
    return [(r, min(size, rows - r)) for r in range(0, rows, size)]


def pipeline(steps, planes, w_ref, xys, together=False):
    def product(s, big):
        _, _, xy_start, rows, hi, lo, _ = steps[s]
        in_plane(big % 4, 1, up16(rows + 2 * xy_start), w_ref, hi, lo, xys[s % 2])

    if together:
        src, start, xy_start, rows, hi, lo, store = steps[0]
        in_plane(0, 4, up16(rows), w_ref, hi, lo, xys[0])
    else:
        product(0, 0)
    for s, (src, start, xy_start, rows, hi, lo, store) in enumerate(steps):
        margin = (planes + 32 - rows) // 2
        for i in range(8):
            if s == 0 and i in (0, 2, 4) and not together:
                product(0, i // 2 + 1)
            j = (2 * s + i) % 8
            for r, count in chunks(rows):
                f = [src[c, j, pl.ds(start + r, count), :] for c in range(4)]
                near = [
                    neighbours(src, xys[s % 2], c, j, start + r, xy_start + r, count)
                    for c in range(4)
                ]
                store(j, r, count, margin + r, f, near)
            if s + 1 < len(steps):
                for ahead in {4: (1,), 6: (2,), 7: (3, 4)}.get(i, ()):
                    product(s + 1, s + ahead)


def derivative(pd, j, row, count, f, near):
    pot, pr, pi = [pd[i, j, pl.ds(row, count), :] for i in range(3)]
    return slope(f, [unit_coef * near[c] + pot * f[c] for c in range(4)], pr, pi)


def stage_store(b0, pd, dst, factor, hi, lo, base=None):
    def store(j, r, count, row, f, near):
        if base is not None:
            row = pl.multiple_of(base + r, 8)
        k = derivative(pd, j, row, count, f, near)
        for c in range(4):
            value = b0[c, j, pl.ds(row + 8, count), :] + (signs[c] * factor) * k[c]
            place = r if base is None else row
            dst[c, j, pl.ds(place, count), :] = value
            put_split(value, c, j, place, hi, lo)

    return store


def place_rows(ref, channel, row, b0, pd, hi, lo, split_row):
    for i in range(ref.shape[0]):
        c = channel + i
        for j in range(8):
            value = ref[i, :, j * LANES : (j + 1) * LANES]
            if c < 4:
                b0[c, j, pl.ds(pl.multiple_of(row + 8, 8), ref.shape[1]), :] = value
                put_split(value, c, j, split_row, hi, lo)
            else:
                value = value + centre_coef if c == 4 else value
                pd[c - 4, j, pl.ds(row, ref.shape[1]), :] = value


def clear_rows(b0, row):
    for c in range(4):
        for j in range(8):
            b0[c, j, pl.ds(row, 8), :] = jnp.zeros((8, LANES), jnp.float32)


def add_share(past, b1, hi, lo, row, terms):
    scale = 0.5 * time_step * unit_coef
    for j in range(8):
        change = []
        for c in range(4):
            total = None
            for begin, sign in terms:
                for k in range(1, REACH + 1):
                    value = past[c, j, pl.ds(begin + sign * k, 8), :]
                    value = value if k == 1 else near_coef[k] * value
                    total = value if total is None else total + value
            change.append(scale * total)
        for c, delta in enumerate((change[1], -change[0], -change[3], change[2])):
            value = b1[c, j, pl.ds(row, 8), :] + delta
            b1[c, j, pl.ds(row, 8), :] = value
            put_split(value, c, j, row, hi, lo)


LEAD, TAIL = (4, -1), (16, 1)


def clear_past(past):
    zero = jnp.zeros((8, LANES), jnp.float32)
    for c in range(4):
        for j in range(8):
            past[c, j, 4:12, :] = zero
            past[c, j, 16:24, :] = zero


def first_kernel(pieces, planes, *refs):
    n = len(pieces)
    parts, w_ref = refs[:n], refs[n]
    b0, pd, b1, hi_b, lo_b, hi_a, lo_a, *xys = refs[n + 1 :]
    clear_rows(b0, 0)
    clear_rows(b0, planes + 40)
    for ref, row in zip(parts, pieces):
        place_rows(ref, 0, row, b0, pd, hi_a, lo_a, row)
    store = stage_store(b0, pd, b1, 0.5 * time_step, hi_b, lo_b)
    pipeline([(b0, 8, 0, planes + 32, hi_a, lo_a, store)], planes, w_ref, xys, True)


def early_kernel(planes, *refs):
    own, near, w_ref = refs[:3]
    b0, pd, b1, hi_b, lo_b, hi_a, lo_a, xy = refs[3:]
    odd = lax.rem(lax.axis_index("grid"), 2)
    base = pl.multiple_of((1 - odd) * planes, 16)
    clear_rows(b0, base)
    clear_rows(b0, pl.multiple_of(base + 2 * planes + 8, 8))
    for ref, side in ((own, odd), (near, 1 - odd)):
        inner = pl.multiple_of(side * planes, 16)
        place_rows(ref, 0, pl.multiple_of(base + inner, 16), b0, pd, hi_a, lo_a, inner)
    store = stage_store(b0, pd, b1, 0.5 * time_step, hi_b, lo_b, base)
    pipeline([(b0, base + 8, 0, 2 * planes, hi_a, lo_a, store)], planes, w_ref, [xy], True)


def late_kernel(planes, *refs):
    rims, far, mine, other, relayed = refs[:5]
    w_ref = refs[10]
    b0, pd, b1, hi_b, lo_b, hi_a, lo_a, past, *xys = refs[11:]
    odd = lax.rem(lax.axis_index("grid"), 2)
    half = lax.rem(lax.axis_index("modes"), 2)
    base = pl.multiple_of(odd * (2 * planes), 16)
    clear_rows(b0, pl.multiple_of(odd * (3 * planes + 8), 8))
    for c in range(4):
        for j in range(8):
            lanes = slice(j * LANES, (j + 1) * LANES)
            value = jnp.concatenate(
                [rims[c, :REACH, lanes], far[c, :, lanes], rims[c, REACH:, lanes]], axis=0
            )
            b0[c, j, pl.ds(pl.multiple_of(base + 8, 8), planes), :] = value
            put_split(value, c, j, 0, hi_a, lo_a)
    for ref, which in ((mine, half), (other, 1 - half)):
        row = pl.multiple_of(base + which * (planes // 2), 8)
        place_rows(ref, 4, row, b0, pd, hi_a, lo_a, 0)
    store = stage_store(b0, pd, b1, 0.5 * time_step, hi_b, lo_b, base)
    pipeline([(b0, base + 8, 0, planes, hi_a, lo_a, store)], planes, w_ref, xys, True)

    clear_past(past)
    none = jnp.zeros((REACH, LANES), jnp.float32)
    for c in range(4):
        for j in range(8):
            lanes = slice(j * LANES, (j + 1) * LANES)
            ahead, behind = rims[c, REACH:, lanes], rims[c, :REACH, lanes]
            past[c, j, 0:REACH, :] = jnp.where(odd == 0, ahead, none)
            past[c, j, 24 : 24 + REACH, :] = jnp.where(odd == 0, none, behind)
    row = pl.multiple_of(planes + odd * (planes - 8), 8)
    add_share(past, b1, hi_b, lo_b, row, (LEAD, TAIL))
    add_far_share(past, b1, hi_b, lo_b, planes, relayed, REACH, relayed, 0)


def add_far_share(past, b1, hi, lo, planes, lead_ref, lead, tail_ref, tail):
    clear_past(past)
    for c in range(4):
        for j in range(8):
            lanes = slice(j * LANES, (j + 1) * LANES)
            past[c, j, 0:REACH, :] = lead_ref[c, lead : lead + REACH, lanes]
            past[c, j, 24 : 24 + REACH, :] = tail_ref[c, tail : tail + REACH, lanes]
    add_share(past, b1, hi, lo, 0, (LEAD,))
    add_share(past, b1, hi, lo, planes + 24, (TAIL,))


def stages_kernel(ends, planes, low_bits, *refs):
    n = 2 if ends else 0
    b0, pd = refs[n : n + 2]
    w_ref = refs[n + 5]
    psi1_ref, kin1_ref, sums_ref, b1, hi_b, lo_b = refs[n + 6 : n + 12]
    b2, b3, b4, hi_a, lo_a, past, *xys = refs[n + 12 :]
    quarter = lax.rem(lax.axis_index("modes"), low_bits)
    if ends:
        add_far_share(past, b1, hi_b, lo_b, planes, refs[0], 0, refs[1], 0)

    def last(j, r, count, row, f, near):
        k = derivative(pd, j, row, count, f, near)
        for c in range(4):
            early = (
                b1[c, j, pl.ds(r + 12, count), :]
                - b0[c, j, pl.ds(r + 20, count), :]
                + 2.0 * b2[c, j, pl.ds(r + 8, count), :]
                + f[c]
            )
            value = early * (1.0 / 3.0) + (signs[c] * time_step / 6.0) * k[c]
            b4[c, j, pl.ds(r, count), :] = value
            put_split(value, c, j, r, hi_a, lo_a)

    def finish(j, r, count, row, f, near):
        full = [unit_coef * near[c] + centre_coef * f[c] for c in range(4)]
        for c in range(4):
            psi1_ref[c, j, pl.ds(r, count), :] = f[c]
            kin1_ref[c, j, pl.ds(r, count), :] = full[c]
        sums = (
            f[2] * f[2] + f[3] * f[3],
            f[2] * full[2] + f[3] * full[3],
            f[0] * f[2] + f[1] * f[3],
            f[1] * f[2] - f[0] * f[3],
        )
        place = lax.bitwise_xor(jnp.int32(j // 2), quarter) if low_bits == 4 else j // 2
        for s in range(4):
            sums_ref[place, j % 2, s, pl.ds(r, count), :] = sums[s]

    second = stage_store(b0, pd, b2, 0.5 * time_step, hi_a, lo_a)
    third = stage_store(b0, pd, b3, time_step, hi_b, lo_b)
    steps = [
        (b1, 4, 4, planes + 24, hi_b, lo_b, second),
        (b2, 4, 4, planes + 16, hi_a, lo_a, third),
        (b3, 4, 4, planes + 8, hi_b, lo_b, last),
        (b4, 4, 4, planes, hi_a, lo_a, finish),
    ]
    pipeline(steps, planes, w_ref, xys)


def middle_kernel(paired, planes, low_bits, *refs):
    pieces = refs[:low_bits]
    psi1, kin1 = refs[low_bits : low_bits + 2]
    mid, first_send, second_send, fields_flat = refs[low_bits + 2 :]
    even = lax.rem(lax.axis_index("grid"), 2) == 0
    quarter = lax.rem(lax.axis_index("modes"), low_bits)
    per = 4 // low_bits
    for k in range(low_bits):
        for t in range(per):
            place = lax.bitwise_xor(quarter, k) * per + t
            for half in range(2):
                for i in range(4):
                    fields_flat[place, half, i] = pieces[k][t, half, i]

    for j in range(8):
        big, half = j // 2, j % 2
        now = [fields_flat[big, half, i] for i in range(3)]
        f = [psi1[c, j] for c in range(4)]
        q = slope(f, [kin1[c, j] + now[0] * f[c] for c in range(4)], now[1], now[2])
        for c in range(4):
            m = f[c] + (signs[c] * 0.5 * time_step) * q[c]
            mid[c, j] = m
            top, bottom = m[:REACH], m[planes - REACH :]
            if paired:
                a, b = jnp.where(even, top, bottom), jnp.where(even, bottom, top)
            else:
                a, b = top, bottom
            first_send[j, c * REACH : (c + 1) * REACH, :] = a
            second_send[j, c * REACH : (c + 1) * REACH, :] = b


def inner_kernel(planes, *refs):
    psi1, kin1, mid, fields_flat, w_ref, part_ref, fields_out, pad, hi, lo, xy = refs
    zero = jnp.zeros((8, LANES), jnp.float32)
    for j in range(8):
        for i in range(4):
            fields_out[i, :, j * LANES : (j + 1) * LANES] = fields_flat[j // 2, j % 2, i]
    for c in range(4):
        for j in range(8):
            value = mid[c, j]
            pad[c, j, 0:8, :] = zero
            pad[c, j, 8 : 8 + planes, :] = value
            pad[c, j, 8 + planes : 16 + planes, :] = zero
            put_split(value, c, j, 0, hi, lo)

    def store(j, r, count, row, m, near):
        pot, pr, pi = [fields_flat[j // 2, j % 2, i, pl.ds(r, count), :] for i in range(3)]
        f = [psi1[c, j, pl.ds(r, count), :] for c in range(4)]
        q1 = slope(f, [kin1[c, j, pl.ds(r, count), :] + pot * f[c] for c in range(4)], pr, pi)
        pot = pot + centre_coef
        q2 = slope(m, [unit_coef * near[c] + pot * m[c] for c in range(4)], pr, pi)
        for c in range(4):
            part_ref[c, j, pl.ds(r, count), :] = f[c] + (signs[c] * time_step / 6.0) * (
                q1[c] + 2.0 * q2[c]
            )

    pipeline([(pad, 8, 0, planes, hi, lo, store)], planes, w_ref, [xy])


def edge_kernel(paired, planes, *refs):
    part, first, second, u_ref, v_ref = refs
    even = lax.rem(lax.axis_index("grid"), 2) == 0
    scale = -0.5 * alpha_coef * 2.0 * time_step / 6.0
    terms = ((0, 1, 1.0), (1, 0, -1.0), (2, 3, -1.0), (3, 2, 1.0))
    for j in range(8):
        a, b = first[j], second[j]
        if paired:
            before, after = jnp.where(even, a, b), jnp.where(even, b, a)
        else:
            before, after = b, a
        for out, src, sign in terms:
            lo_rows = before[src * REACH : (src + 1) * REACH]
            hi_rows = after[src * REACH : (src + 1) * REACH]
            lead, tail = [], []
            for r in range(REACH):
                lead.append(
                    sum(
                        stencil_coef[k] * lo_rows[r - k + REACH : r - k + REACH + 1]
                        for k in range(r + 1, REACH + 1)
                    )
                )
                tail.append(
                    sum(
                        stencil_coef[k] * hi_rows[r + k - REACH : r + k - REACH + 1]
                        for k in range(REACH - r, REACH + 1)
                    )
                )
            value = part[out, j]
            parts = [value[:REACH] + (sign * scale) * jnp.concatenate(lead, axis=0)]
            if planes > 2 * REACH:
                parts.append(value[REACH : planes - REACH])
            parts.append(value[planes - REACH :] + (sign * scale) * jnp.concatenate(tail, axis=0))
            ref = u_ref if out < 2 else v_ref
            ref[0, out % 2, :, j * LANES : (j + 1) * LANES] = jnp.concatenate(parts, axis=0)


def potentials(raw, modes_total):
    density = 2.0 * raw[:, :, 0] / modes_total
    kinetic = (-2.0 / kinetic_coef) * raw[:, :, 1] / modes_total
    anomal_re = raw[:, :, 2] / modes_total
    anomal_im = raw[:, :, 3] / modes_total
    dense_safe = density + epsilon
    fermi = 0.5 * jnp.power(3.0 * jnp.pi**2 * dense_safe, 2.0 / 3.0)
    anomal_sq = anomal_re * anomal_re + anomal_im * anomal_im
    third_root = jnp.power(dense_safe, -1.0 / 3.0)
    field_pot = beta_coef * fermi - gamma_coef / 3.0 * anomal_sq * third_root / dense_safe
    pair_re = -gamma_coef * anomal_re * third_root
    pair_im = -gamma_coef * anomal_im * third_root
    energy = (
        alpha_coef * kinetic / 2.0
        + 0.6 * beta_coef * dense_safe * fermi
        + gamma_coef * anomal_sq * third_root
    )
    return jnp.stack([field_pot, pair_re, pair_im, energy], axis=2)


def call(kernel, outs, scratch, args, aliases=None):
    vmem = pl.BlockSpec(memory_space=pltpu.VMEM)
    shapes = [o if isinstance(o[0], tuple) else (o, jnp.float32) for o in outs]
    flops = 2 * sum(int(np.prod(s)) for s, d in shapes)
    return pl.pallas_call(
        kernel,
        out_shape=tuple(jax.ShapeDtypeStruct(s, d) for s, d in shapes),
        in_specs=[vmem] * len(args),
        out_specs=tuple([vmem] * len(outs)),
        scratch_shapes=[pltpu.VMEM(s, d) for s, d in scratch],
        input_output_aliases=aliases or {},
        compiler_params=pltpu.CompilerParams(vmem_limit_bytes=32 << 20),
        cost_estimate=pl.CostEstimate(flops=1000 * flops, bytes_accessed=4 * flops, transcendentals=0),
    )(*args)


def exchange_xor(x, axis, bits, count):
    return lax.ppermute(x, axis, [(i, i ^ bits) for i in range(count)])


def local(u_modes, v_modes, potential, pairing):
    planes = u_modes.shape[2]
    slabs = lax.axis_size("grid")
    modes = lax.axis_size("modes")
    low_bits = 4 if modes % 4 == 0 else 1
    paired = slabs == 4 and planes == 16 and low_bits == 4
    f32, bf16 = jnp.float32, jnp.bfloat16
    weights = jnp.asarray(in_plane_matrix())
    own = jnp.concatenate([u_modes[0], v_modes[0], potential[None], pairing], axis=0)
    own = lax.optimization_barrier(own)
    tall = up16(planes + 32)
    state = (4, 8, planes, LANES)
    split = ((4, 4, tall, WINDOW), bf16)
    product = ((4, 4, 2, tall, LANES), f32)
    past = ((4, 8, 32, LANES), f32)
    buffers = [
        (4, 8, tall + 16, LANES),
        (3, 8, tall, LANES),
        (4, 8, tall + 8, LANES),
        split,
        split,
    ]

    cross = [(i, (i - 1 if i % 2 == 0 else i + 1) % slabs) for i in range(slabs)]
    up = [(i, (i + 1) % slabs) for i in range(slabs)]
    down = [(j, i) for i, j in up]
    if paired:
        part = planes // 2
        upper = lax.rem(lax.axis_index("modes"), 2) == 1
        picked = jnp.where(upper, own[4:, part:], own[4:, :part])
        mine = lax.ppermute(picked, "grid", cross)
        rims = jnp.concatenate([own[:4, :REACH], own[:4, planes - REACH :]], axis=1)
        rims = lax.ppermute(rims, "grid", cross)
        far = lax.ppermute(own[:4, REACH : planes - REACH], "grid", cross)
        near = exchange_xor(own, "grid", 1, slabs)
        other = exchange_xor(mine, "modes", 1, modes)
        ready = call(functools.partial(early_kernel, planes), buffers, [split, split, product], [own, near, weights])
        relayed = exchange_xor(rims, "grid", 1, slabs)
        far, other, relayed = lax.optimization_barrier((far, other, relayed))
        ends = []
        b0, pd, b1, hi, lo = call(
            functools.partial(late_kernel, planes),
            buffers,
            [split, split, past, product],
            [rims, far, mine, other, relayed, *ready, weights],
            {5 + i: i for i in range(5)},
        )
    else:
        pieces, arrays = [16], [own]
        reach, step = 0, 0
        while reach < 5 * REACH:
            step += 1
            count = min(planes, 5 * REACH - reach)
            wide = 7 if reach < 4 * REACH else 4
            before = lax.ppermute(
                own[:wide, planes - count :], "grid", [(i, (i + step) % slabs) for i in range(slabs)]
            )
            after = lax.ppermute(
                own[:wide, :count], "grid", [((i + step) % slabs, i) for i in range(slabs)]
            )
            if wide == 7:
                pieces += [16 - reach - count, 16 + planes + reach]
                arrays += [before, after]
            else:
                ends = [before, after]
            reach += count
        b0, pd, b1, hi, lo = call(
            functools.partial(first_kernel, pieces, planes), buffers, [split, split, product], arrays + [weights]
        )

    inputs = [*ends, b0, pd, b1, hi, lo, weights]
    psi1, kin1, sums, *rest = call(
        functools.partial(stages_kernel, bool(ends), planes, low_bits),
        [state, state, (4, 2, 4, planes, LANES), b1.shape, split, split],
        [
            ((4, 8, tall + 8, LANES), f32),
            ((4, 8, tall + 8, LANES), f32),
            ((4, 8, tall + 8, LANES), f32),
            split,
            split,
            past,
            product,
            product,
        ],
        inputs,
        {len(ends) + 2 + i: 3 + i for i in range(3)},
    )

    if low_bits == 4:
        total = sums[0:1]
        for k in (1, 2, 3):
            total = total + exchange_xor(sums[k : k + 1], "modes", k, modes)
    else:
        total = sums
    bits = low_bits
    while bits < modes:
        total = total + exchange_xor(total, "modes", bits, modes)
        bits *= 2
    quarter = potentials(total, float(u_modes.shape[0] * modes))
    got = [quarter] + [exchange_xor(quarter, "modes", k, modes) for k in range(1, low_bits)]

    edge = (8, 4 * REACH, LANES)
    mid, first, second, fields_flat = call(
        functools.partial(middle_kernel, paired, planes, low_bits),
        [state, edge, edge, (4, 2, 4, planes, LANES)],
        [],
        got + [psi1, kin1],
    )
    if paired:
        first = lax.ppermute(first, "grid", cross)
        second = exchange_xor(second, "grid", 1, slabs)
    else:
        first = lax.ppermute(first, "grid", down)
        second = lax.ppermute(second, "grid", up)
    flat = up16(planes)
    part, fields = call(
        functools.partial(inner_kernel, planes),
        [state, (4, planes, NX * NY)],
        [
            ((4, 8, flat + 16, LANES), f32),
            ((4, 4, flat, WINDOW), bf16),
            ((4, 4, flat, WINDOW), bf16),
            ((4, 4, 2, flat, LANES), f32),
        ],
        [psi1, kin1, mid, fields_flat, weights],
    )
    u_next, v_next = call(
        functools.partial(edge_kernel, paired, planes), [u_modes.shape, v_modes.shape], [], [part, first, second]
    )
    return u_next, v_next, fields


def solution(mesh):
    wide = P("modes", None, "grid", None)
    return jax.shard_map(
        local,
        mesh=mesh,
        in_specs=(wide, wide, P("grid", None), P(None, "grid", None)),
        out_specs=(wide, wide, P(None, "grid", None)),
        check_vma=False,
    )
```

```python
import functools

import jax
import jax.numpy as jnp
import numpy as np
from jax import lax
from jax.experimental import pallas as pl
from jax.experimental.pallas import tpu as pltpu
from jax.sharding import PartitionSpec as P


NX = 32
NY = 32

stencil_coef = (-205.0 / 72.0, 8.0 / 5.0, -1.0 / 5.0, 8.0 / 315.0, -1.0 / 560.0)
alpha_coef = 1.14
beta_coef = -0.553
gamma_coef = -11.11
time_step = 0.18
epsilon = 1e-06

REACH = 4
LANES = 128
BLOCK = 256
WINDOW = BLOCK + 2 * LANES
kinetic_coef = -0.5 * alpha_coef
unit = stencil_coef[1]
near_coef = tuple(c / unit for c in stencil_coef)
unit_coef = kinetic_coef * unit
centre_coef = 3.0 * kinetic_coef * stencil_coef[0]


def in_plane_matrix():
    rows_out = BLOCK // NX
    mat = np.zeros((WINDOW, BLOCK), np.float64)
    for y in range(rows_out):
        for x in range(NX):
            out = y * NX + x
            for k in range(1, REACH + 1):
                for sign in (-1, 1):
                    mat[(y + REACH) * NX + (x + sign * k) % NX, out] += near_coef[k]
                    mat[(y + REACH + sign * k) * NX + x, out] += near_coef[k]
    mat = mat.astype(jnp.bfloat16)
    return np.concatenate([mat, mat], axis=0)


def up16(n):
    return -(-n // 16) * 16


def put_split(value, c, j, row, hi_ref, lo_ref):
    count = value.shape[0]
    high = value.astype(jnp.bfloat16)
    low = (value - high.astype(jnp.float32)).astype(jnp.bfloat16)
    if j % 2 == 0:
        places = ((j // 2, 1), ((j // 2 + 3) % 4, 3))
    else:
        places = ((j // 2, 2), ((j // 2 + 1) % 4, 0))
    for big, part in places:
        hi_ref[big, c, pl.ds(row, count), part * LANES : (part + 1) * LANES] = high
        lo_ref[big, c, pl.ds(row, count), part * LANES : (part + 1) * LANES] = low


def in_plane(first, number, rows, w_ref, hi_ref, lo_ref, xy_ref):
    span = slice(first, first + number)
    high = hi_ref[span, :, :rows, :].reshape(number * 4 * rows, WINDOW)
    low = lo_ref[span, :, :rows, :].reshape(number * 4 * rows, WINDOW)
    total = jnp.dot(
        jnp.concatenate([high, low], axis=1), w_ref[...], preferred_element_type=jnp.float32
    )
    for half in range(2):
        xy_ref[span, :, half, :rows, :] = total[:, half * LANES : (half + 1) * LANES].reshape(
            number, 4, rows, LANES
        )


def neighbours(ref, xy, c, j, start, xy_start, count):
    total = xy[j // 2, c, j % 2, pl.ds(xy_start, count), :]
    for k in range(1, REACH + 1):
        pair = ref[c, j, pl.ds(start + k, count), :] + ref[c, j, pl.ds(start - k, count), :]
        total = total + (pair if k == 1 else near_coef[k] * pair)
    return total


def slope(f, kin, pr, pi):
    upper_re = kin[0] + pr * f[2] - pi * f[3]
    upper_im = kin[1] + pr * f[3] + pi * f[2]
    lower_re = pr * f[0] + pi * f[1] - kin[2]
    lower_im = pr * f[1] - pi * f[0] - kin[3]
    return upper_im, upper_re, lower_im, lower_re


signs = (1.0, -1.0, 1.0, -1.0)


def chunks(rows, size=16):
    return [(r, min(size, rows - r)) for r in range(0, rows, size)]


def pipeline(steps, planes, w_ref, xys, together=False):
    def product(s, big):
        _, _, xy_start, rows, hi, lo, _ = steps[s]
        in_plane(big % 4, 1, up16(rows + 2 * xy_start), w_ref, hi, lo, xys[s % 2])

    if together:
        src, start, xy_start, rows, hi, lo, store = steps[0]
        in_plane(0, 4, up16(rows), w_ref, hi, lo, xys[0])
    else:
        product(0, 0)
    for s, (src, start, xy_start, rows, hi, lo, store) in enumerate(steps):
        margin = (planes + 32 - rows) // 2
        for i in range(8):
            if s == 0 and i in (0, 2, 4) and not together:
                product(0, i // 2 + 1)
            j = (2 * s + i) % 8
            for r, count in chunks(rows):
                f = [src[c, j, pl.ds(start + r, count), :] for c in range(4)]
                near = [
                    neighbours(src, xys[s % 2], c, j, start + r, xy_start + r, count)
                    for c in range(4)
                ]
                store(j, r, count, margin + r, f, near)
            if s + 1 < len(steps):
                for ahead in {4: (1,), 6: (2,), 7: (3, 4)}.get(i, ()):
                    product(s + 1, s + ahead)


def derivative(pd, j, row, count, f, near):
    pot, pr, pi = [pd[i, j, pl.ds(row, count), :] for i in range(3)]
    return slope(f, [unit_coef * near[c] + pot * f[c] for c in range(4)], pr, pi)


def stage_store(b0, pd, dst, factor, hi, lo, base=None):
    def store(j, r, count, row, f, near):
        if base is not None:
            row = pl.multiple_of(base + r, 8)
        k = derivative(pd, j, row, count, f, near)
        for c in range(4):
            value = b0[c, j, pl.ds(row + 8, count), :] + (signs[c] * factor) * k[c]
            place = r if base is None else row
            dst[c, j, pl.ds(place, count), :] = value
            put_split(value, c, j, place, hi, lo)

    return store


def place_rows(ref, channel, row, b0, pd, hi, lo, split_row):
    for i in range(ref.shape[0]):
        c = channel + i
        for j in range(8):
            value = ref[i, :, j * LANES : (j + 1) * LANES]
            if c < 4:
                b0[c, j, pl.ds(pl.multiple_of(row + 8, 8), ref.shape[1]), :] = value
                put_split(value, c, j, split_row, hi, lo)
            else:
                value = value + centre_coef if c == 4 else value
                pd[c - 4, j, pl.ds(row, ref.shape[1]), :] = value


def clear_rows(b0, row):
    for c in range(4):
        for j in range(8):
            b0[c, j, pl.ds(row, 8), :] = jnp.zeros((8, LANES), jnp.float32)


def add_share(past, b1, hi, lo, row, terms):
    scale = 0.5 * time_step * unit_coef
    for j in range(8):
        change = []
        for c in range(4):
            total = None
            for begin, sign in terms:
                for k in range(1, REACH + 1):
                    value = past[c, j, pl.ds(begin + sign * k, 8), :]
                    value = value if k == 1 else near_coef[k] * value
                    total = value if total is None else total + value
            change.append(scale * total)
        for c, delta in enumerate((change[1], -change[0], -change[3], change[2])):
            value = b1[c, j, pl.ds(row, 8), :] + delta
            b1[c, j, pl.ds(row, 8), :] = value
            put_split(value, c, j, row, hi, lo)


LEAD, TAIL = (4, -1), (16, 1)


def clear_past(past):
    zero = jnp.zeros((8, LANES), jnp.float32)
    for c in range(4):
        for j in range(8):
            past[c, j, 4:12, :] = zero
            past[c, j, 16:24, :] = zero


def first_kernel(pieces, planes, *refs):
    n = len(pieces)
    parts, w_ref = refs[:n], refs[n]
    b0, pd, b1, hi_b, lo_b, hi_a, lo_a, *xys = refs[n + 1 :]
    clear_rows(b0, 0)
    clear_rows(b0, planes + 40)
    for ref, row in zip(parts, pieces):
        place_rows(ref, 0, row, b0, pd, hi_a, lo_a, row)
    store = stage_store(b0, pd, b1, 0.5 * time_step, hi_b, lo_b)
    pipeline([(b0, 8, 0, planes + 32, hi_a, lo_a, store)], planes, w_ref, xys, True)


def early_kernel(planes, *refs):
    own, near, w_ref = refs[:3]
    b0, pd, b1, hi_b, lo_b, hi_a, lo_a, xy = refs[3:]
    odd = lax.rem(lax.axis_index("grid"), 2)
    base = pl.multiple_of((1 - odd) * planes, 16)
    clear_rows(b0, base)
    clear_rows(b0, pl.multiple_of(base + 2 * planes + 8, 8))
    for ref, side in ((own, odd), (near, 1 - odd)):
        inner = pl.multiple_of(side * planes, 16)
        place_rows(ref, 0, pl.multiple_of(base + inner, 16), b0, pd, hi_a, lo_a, inner)
    store = stage_store(b0, pd, b1, 0.5 * time_step, hi_b, lo_b, base)
    pipeline([(b0, base + 8, 0, 2 * planes, hi_a, lo_a, store)], planes, w_ref, [xy], True)


def late_kernel(planes, *refs):
    rims, far, mine, other, relayed = refs[:5]
    w_ref = refs[10]
    b0, pd, b1, hi_b, lo_b, hi_a, lo_a, past, *xys = refs[11:]
    odd = lax.rem(lax.axis_index("grid"), 2)
    half = lax.rem(lax.axis_index("modes"), 2)
    base = pl.multiple_of(odd * (2 * planes), 16)
    clear_rows(b0, pl.multiple_of(odd * (3 * planes + 8), 8))
    for c in range(4):
        for j in range(8):
            lanes = slice(j * LANES, (j + 1) * LANES)
            value = jnp.concatenate(
                [rims[c, :REACH, lanes], far[c, :, lanes], rims[c, REACH:, lanes]], axis=0
            )
            b0[c, j, pl.ds(pl.multiple_of(base + 8, 8), planes), :] = value
            put_split(value, c, j, 0, hi_a, lo_a)
    for ref, which in ((mine, half), (other, 1 - half)):
        row = pl.multiple_of(base + which * (planes // 2), 8)
        place_rows(ref, 4, row, b0, pd, hi_a, lo_a, 0)
    store = stage_store(b0, pd, b1, 0.5 * time_step, hi_b, lo_b, base)
    pipeline([(b0, base + 8, 0, planes, hi_a, lo_a, store)], planes, w_ref, xys, True)

    clear_past(past)
    none = jnp.zeros((REACH, LANES), jnp.float32)
    for c in range(4):
        for j in range(8):
            lanes = slice(j * LANES, (j + 1) * LANES)
            ahead, behind = rims[c, REACH:, lanes], rims[c, :REACH, lanes]
            past[c, j, 0:REACH, :] = jnp.where(odd == 0, ahead, none)
            past[c, j, 24 : 24 + REACH, :] = jnp.where(odd == 0, none, behind)
    row = pl.multiple_of(planes + odd * (planes - 8), 8)
    add_share(past, b1, hi_b, lo_b, row, (LEAD, TAIL))
    add_far_share(past, b1, hi_b, lo_b, planes, relayed, REACH, relayed, 0)


def add_far_share(past, b1, hi, lo, planes, lead_ref, lead, tail_ref, tail):
    clear_past(past)
    for c in range(4):
        for j in range(8):
            lanes = slice(j * LANES, (j + 1) * LANES)
            past[c, j, 0:REACH, :] = lead_ref[c, lead : lead + REACH, lanes]
            past[c, j, 24 : 24 + REACH, :] = tail_ref[c, tail : tail + REACH, lanes]
    add_share(past, b1, hi, lo, 0, (LEAD,))
    add_share(past, b1, hi, lo, planes + 24, (TAIL,))


def stages_kernel(ends, planes, low_bits, *refs):
    n = 2 if ends else 0
    b0, pd = refs[n : n + 2]
    w_ref = refs[n + 5]
    psi1_ref, kin1_ref, sums_ref, b1, hi_b, lo_b = refs[n + 6 : n + 12]
    b2, b3, b4, hi_a, lo_a, past, *xys = refs[n + 12 :]
    quarter = lax.rem(lax.axis_index("modes"), low_bits)
    if ends:
        add_far_share(past, b1, hi_b, lo_b, planes, refs[0], 0, refs[1], 0)

    def last(j, r, count, row, f, near):
        k = derivative(pd, j, row, count, f, near)
        for c in range(4):
            early = (
                b1[c, j, pl.ds(r + 12, count), :]
                - b0[c, j, pl.ds(r + 20, count), :]
                + 2.0 * b2[c, j, pl.ds(r + 8, count), :]
                + f[c]
            )
            value = early * (1.0 / 3.0) + (signs[c] * time_step / 6.0) * k[c]
            b4[c, j, pl.ds(r, count), :] = value
            put_split(value, c, j, r, hi_a, lo_a)

    def finish(j, r, count, row, f, near):
        full = [unit_coef * near[c] + centre_coef * f[c] for c in range(4)]
        for c in range(4):
            psi1_ref[c, j, pl.ds(r, count), :] = f[c]
            kin1_ref[c, j, pl.ds(r, count), :] = full[c]
        sums = (
            f[2] * f[2] + f[3] * f[3],
            f[2] * full[2] + f[3] * full[3],
            f[0] * f[2] + f[1] * f[3],
            f[1] * f[2] - f[0] * f[3],
        )
        place = lax.bitwise_xor(jnp.int32(j // 2), quarter) if low_bits == 4 else j // 2
        for s in range(4):
            sums_ref[place, j % 2, s, pl.ds(r, count), :] = sums[s]

    second = stage_store(b0, pd, b2, 0.5 * time_step, hi_a, lo_a)
    third = stage_store(b0, pd, b3, time_step, hi_b, lo_b)
    steps = [
        (b1, 4, 4, planes + 24, hi_b, lo_b, second),
        (b2, 4, 4, planes + 16, hi_a, lo_a, third),
        (b3, 4, 4, planes + 8, hi_b, lo_b, last),
        (b4, 4, 4, planes, hi_a, lo_a, finish),
    ]
    pipeline(steps, planes, w_ref, xys)


def middle_kernel(paired, planes, low_bits, *refs):
    pieces = refs[:low_bits]
    psi1, kin1 = refs[low_bits : low_bits + 2]
    mid, first_send, second_send, fields_flat = refs[low_bits + 2 :]
    even = lax.rem(lax.axis_index("grid"), 2) == 0
    quarter = lax.rem(lax.axis_index("modes"), low_bits)
    per = 4 // low_bits
    for k in range(low_bits):
        for t in range(per):
            place = lax.bitwise_xor(quarter, k) * per + t
            for half in range(2):
                for i in range(4):
                    fields_flat[place, half, i] = pieces[k][t, half, i]

    for j in range(8):
        big, half = j // 2, j % 2
        now = [fields_flat[big, half, i] for i in range(3)]
        f = [psi1[c, j] for c in range(4)]
        q = slope(f, [kin1[c, j] + now[0] * f[c] for c in range(4)], now[1], now[2])
        for c in range(4):
            m = f[c] + (signs[c] * 0.5 * time_step) * q[c]
            mid[c, j] = m
            top, bottom = m[:REACH], m[planes - REACH :]
            if paired:
                a, b = jnp.where(even, top, bottom), jnp.where(even, bottom, top)
            else:
                a, b = top, bottom
            first_send[j, c * REACH : (c + 1) * REACH, :] = a
            second_send[j, c * REACH : (c + 1) * REACH, :] = b


def inner_kernel(planes, *refs):
    psi1, kin1, mid, fields_flat, w_ref, part_ref, fields_out, pad, hi, lo, xy = refs
    zero = jnp.zeros((8, LANES), jnp.float32)
    for j in range(8):
        for i in range(4):
            fields_out[i, :, j * LANES : (j + 1) * LANES] = fields_flat[j // 2, j % 2, i]
    for c in range(4):
        for j in range(8):
            value = mid[c, j]
            pad[c, j, 0:8, :] = zero
            pad[c, j, 8 : 8 + planes, :] = value
            pad[c, j, 8 + planes : 16 + planes, :] = zero
            put_split(value, c, j, 0, hi, lo)

    def store(j, r, count, row, m, near):
        pot, pr, pi = [fields_flat[j // 2, j % 2, i, pl.ds(r, count), :] for i in range(3)]
        f = [psi1[c, j, pl.ds(r, count), :] for c in range(4)]
        q1 = slope(f, [kin1[c, j, pl.ds(r, count), :] + pot * f[c] for c in range(4)], pr, pi)
        pot = pot + centre_coef
        q2 = slope(m, [unit_coef * near[c] + pot * m[c] for c in range(4)], pr, pi)
        for c in range(4):
            part_ref[c, j, pl.ds(r, count), :] = f[c] + (signs[c] * time_step / 6.0) * (
                q1[c] + 2.0 * q2[c]
            )

    pipeline([(pad, 8, 0, planes, hi, lo, store)], planes, w_ref, [xy])


def edge_kernel(paired, planes, *refs):
    part, first, second, u_ref, v_ref = refs
    even = lax.rem(lax.axis_index("grid"), 2) == 0
    scale = -0.5 * alpha_coef * 2.0 * time_step / 6.0
    terms = ((0, 1, 1.0), (1, 0, -1.0), (2, 3, -1.0), (3, 2, 1.0))
    for j in range(8):
        a, b = first[j], second[j]
        if paired:
            before, after = jnp.where(even, a, b), jnp.where(even, b, a)
        else:
            before, after = b, a
        for out, src, sign in terms:
            lo_rows = before[src * REACH : (src + 1) * REACH]
            hi_rows = after[src * REACH : (src + 1) * REACH]
            lead, tail = [], []
            for r in range(REACH):
                lead.append(
                    sum(
                        stencil_coef[k] * lo_rows[r - k + REACH : r - k + REACH + 1]
                        for k in range(r + 1, REACH + 1)
                    )
                )
                tail.append(
                    sum(
                        stencil_coef[k] * hi_rows[r + k - REACH : r + k - REACH + 1]
                        for k in range(REACH - r, REACH + 1)
                    )
                )
            value = part[out, j]
            parts = [value[:REACH] + (sign * scale) * jnp.concatenate(lead, axis=0)]
            if planes > 2 * REACH:
                parts.append(value[REACH : planes - REACH])
            parts.append(value[planes - REACH :] + (sign * scale) * jnp.concatenate(tail, axis=0))
            ref = u_ref if out < 2 else v_ref
            ref[0, out % 2, :, j * LANES : (j + 1) * LANES] = jnp.concatenate(parts, axis=0)


def potentials(raw, modes_total):
    density = 2.0 * raw[:, :, 0] / modes_total
    kinetic = (-2.0 / kinetic_coef) * raw[:, :, 1] / modes_total
    anomal_re = raw[:, :, 2] / modes_total
    anomal_im = raw[:, :, 3] / modes_total
    dense_safe = density + epsilon
    fermi = 0.5 * jnp.power(3.0 * jnp.pi**2 * dense_safe, 2.0 / 3.0)
    anomal_sq = anomal_re * anomal_re + anomal_im * anomal_im
    third_root = jnp.power(dense_safe, -1.0 / 3.0)
    field_pot = beta_coef * fermi - gamma_coef / 3.0 * anomal_sq * third_root / dense_safe
    pair_re = -gamma_coef * anomal_re * third_root
    pair_im = -gamma_coef * anomal_im * third_root
    energy = (
        alpha_coef * kinetic / 2.0
        + 0.6 * beta_coef * dense_safe * fermi
        + gamma_coef * anomal_sq * third_root
    )
    return jnp.stack([field_pot, pair_re, pair_im, energy], axis=2)


def call(kernel, outs, scratch, args, aliases=None):
    vmem = pl.BlockSpec(memory_space=pltpu.VMEM)
    shapes = [o if isinstance(o[0], tuple) else (o, jnp.float32) for o in outs]
    flops = 2 * sum(int(np.prod(s)) for s, d in shapes)
    return pl.pallas_call(
        kernel,
        out_shape=tuple(jax.ShapeDtypeStruct(s, d) for s, d in shapes),
        in_specs=[vmem] * len(args),
        out_specs=tuple([vmem] * len(outs)),
        scratch_shapes=[pltpu.VMEM(s, d) for s, d in scratch],
        input_output_aliases=aliases or {},
        compiler_params=pltpu.CompilerParams(vmem_limit_bytes=32 << 20),
        cost_estimate=pl.CostEstimate(flops=1000 * flops, bytes_accessed=4 * flops, transcendentals=0),
    )(*args)


def exchange_xor(x, axis, bits, count):
    return lax.ppermute(x, axis, [(i, i ^ bits) for i in range(count)])


def local(u_modes, v_modes, potential, pairing):
    planes = u_modes.shape[2]
    slabs = lax.axis_size("grid")
    modes = lax.axis_size("modes")
    low_bits = 4 if modes % 4 == 0 else 1
    paired = slabs == 4 and planes == 16 and low_bits == 4
    f32, bf16 = jnp.float32, jnp.bfloat16
    weights = jnp.asarray(in_plane_matrix())
    own = jnp.concatenate([u_modes[0], v_modes[0], potential[None], pairing], axis=0)
    own = lax.optimization_barrier(own)
    tall = up16(planes + 32)
    state = (4, 8, planes, LANES)
    split = ((4, 4, tall, WINDOW), bf16)
    product = ((4, 4, 2, tall, LANES), f32)
    past = ((4, 8, 32, LANES), f32)
    buffers = [
        (4, 8, tall + 16, LANES),
        (3, 8, tall, LANES),
        (4, 8, tall + 8, LANES),
        split,
        split,
    ]

    cross = [(i, (i - 1 if i % 2 == 0 else i + 1) % slabs) for i in range(slabs)]
    up = [(i, (i + 1) % slabs) for i in range(slabs)]
    down = [(j, i) for i, j in up]
    if paired:
        part = planes // 2
        upper = lax.rem(lax.axis_index("modes"), 2) == 1
        picked = jnp.where(upper, own[4:, part:], own[4:, :part])
        mine = lax.ppermute(picked, "grid", cross)
        rims = jnp.concatenate([own[:4, :REACH], own[:4, planes - REACH :]], axis=1)
        rims = lax.ppermute(rims, "grid", cross)
        far = lax.ppermute(own[:4, REACH : planes - REACH], "grid", cross)
        near = exchange_xor(own, "grid", 1, slabs)
        other = exchange_xor(mine, "modes", 1, modes)
        ready = call(functools.partial(early_kernel, planes), buffers, [split, split, product], [own, near, weights])
        relayed = exchange_xor(rims, "grid", 1, slabs)
        far, other, relayed = lax.optimization_barrier((far, other, relayed))
        ends = []
        b0, pd, b1, hi, lo = call(
            functools.partial(late_kernel, planes),
            buffers,
            [split, split, past, product],
            [rims, far, mine, other, relayed, *ready, weights],
            {5 + i: i for i in range(5)},
        )
    else:
        pieces, arrays = [16], [own]
        reach, step = 0, 0
        while reach < 5 * REACH:
            step += 1
            count = min(planes, 5 * REACH - reach)
            wide = 7 if reach < 4 * REACH else 4
            before = lax.ppermute(
                own[:wide, planes - count :], "grid", [(i, (i + step) % slabs) for i in range(slabs)]
            )
            after = lax.ppermute(
                own[:wide, :count], "grid", [((i + step) % slabs, i) for i in range(slabs)]
            )
            if wide == 7:
                pieces += [16 - reach - count, 16 + planes + reach]
                arrays += [before, after]
            else:
                ends = [before, after]
            reach += count
        b0, pd, b1, hi, lo = call(
            functools.partial(first_kernel, pieces, planes), buffers, [split, split, product], arrays + [weights]
        )

    inputs = [*ends, b0, pd, b1, hi, lo, weights]
    psi1, kin1, sums, *rest = call(
        functools.partial(stages_kernel, bool(ends), planes, low_bits),
        [state, state, (4, 2, 4, planes, LANES), b1.shape, split, split],
        [
            ((4, 8, tall + 8, LANES), f32),
            ((4, 8, tall + 8, LANES), f32),
            ((4, 8, tall + 8, LANES), f32),
            split,
            split,
            past,
            product,
            product,
        ],
        inputs,
        {len(ends) + 2 + i: 3 + i for i in range(3)},
    )

    if low_bits == 4:
        total = sums[0:1]
        for k in (1, 2, 3):
            got = exchange_xor(sums[k : k + 1], "modes", k, modes)
            total = total + got
    else:
        total = sums
    bits = low_bits
    while bits < modes:
        total = total + exchange_xor(total, "modes", bits, modes)
        bits *= 2
    quarter = potentials(total, float(u_modes.shape[0] * modes))
    got = [quarter]
    for k in range(1, low_bits):
        got.append(exchange_xor(quarter, "modes", k, modes))

    edge = (8, 4 * REACH, LANES)
    mid, first, second, fields_flat = call(
        functools.partial(middle_kernel, paired, planes, low_bits),
        [state, edge, edge, (4, 2, 4, planes, LANES)],
        [],
        got + [psi1, kin1],
    )
    if paired:
        first = lax.ppermute(first, "grid", cross)
        second = exchange_xor(second, "grid", 1, slabs)
    else:
        first = lax.ppermute(first, "grid", down)
        second = lax.ppermute(second, "grid", up)
    flat = up16(planes)
    part, fields = call(
        functools.partial(inner_kernel, planes),
        [state, (4, planes, NX * NY)],
        [
            ((4, 8, flat + 16, LANES), f32),
            ((4, 4, flat, WINDOW), bf16),
            ((4, 4, flat, WINDOW), bf16),
            ((4, 4, 2, flat, LANES), f32),
        ],
        [psi1, kin1, mid, fields_flat, weights],
    )
    u_next, v_next = call(
        functools.partial(edge_kernel, paired, planes), [u_modes.shape, v_modes.shape], [], [part, first, second]
    )
    return u_next, v_next, fields


def solution(mesh):
    wide = P("modes", None, "grid", None)
    return jax.shard_map(
        local,
        mesh=mesh,
        in_specs=(wide, wide, P("grid", None), P(None, "grid", None)),
        out_specs=(wide, wide, P(None, "grid", None)),
        check_vma=False,
    )
```

```python
import functools

import jax
import jax.numpy as jnp
import numpy as np
from jax import lax
from jax.experimental import pallas as pl
from jax.experimental.pallas import tpu as pltpu
from jax.sharding import PartitionSpec as P


NX = 32
NY = 32

stencil_coef = (-205.0 / 72.0, 8.0 / 5.0, -1.0 / 5.0, 8.0 / 315.0, -1.0 / 560.0)
alpha_coef = 1.14
beta_coef = -0.553
gamma_coef = -11.11
time_step = 0.18
epsilon = 1e-06

REACH = 4
LANES = 128
BLOCK = 256
WINDOW = BLOCK + 2 * LANES
kinetic_coef = -0.5 * alpha_coef
unit = stencil_coef[1]
near_coef = tuple(c / unit for c in stencil_coef)
unit_coef = kinetic_coef * unit
centre_coef = 3.0 * kinetic_coef * stencil_coef[0]


def in_plane_matrix():
    rows_out = BLOCK // NX
    mat = np.zeros((WINDOW, BLOCK), np.float64)
    for y in range(rows_out):
        for x in range(NX):
            out = y * NX + x
            for k in range(1, REACH + 1):
                for sign in (-1, 1):
                    mat[(y + REACH) * NX + (x + sign * k) % NX, out] += near_coef[k]
                    mat[(y + REACH + sign * k) * NX + x, out] += near_coef[k]
    mat = mat.astype(jnp.bfloat16)
    return np.concatenate([mat, mat], axis=0)


def up16(n):
    return -(-n // 16) * 16


def put_split(value, c, j, row, hi_ref, lo_ref):
    count = value.shape[0]
    high = value.astype(jnp.bfloat16)
    low = (value - high.astype(jnp.float32)).astype(jnp.bfloat16)
    if j % 2 == 0:
        places = ((j // 2, 1), ((j // 2 + 3) % 4, 3))
    else:
        places = ((j // 2, 2), ((j // 2 + 1) % 4, 0))
    for big, part in places:
        hi_ref[big, c, pl.ds(row, count), part * LANES : (part + 1) * LANES] = high
        lo_ref[big, c, pl.ds(row, count), part * LANES : (part + 1) * LANES] = low


def in_plane(first, number, rows, w_ref, hi_ref, lo_ref, xy_ref):
    span = slice(first, first + number)
    high = hi_ref[span, :, :rows, :].reshape(number * 4 * rows, WINDOW)
    low = lo_ref[span, :, :rows, :].reshape(number * 4 * rows, WINDOW)
    total = jnp.dot(
        jnp.concatenate([high, low], axis=1), w_ref[...], preferred_element_type=jnp.float32
    )
    for half in range(2):
        xy_ref[span, :, half, :rows, :] = total[:, half * LANES : (half + 1) * LANES].reshape(
            number, 4, rows, LANES
        )


def neighbours(ref, xy, c, j, start, xy_start, count):
    total = xy[j // 2, c, j % 2, pl.ds(xy_start, count), :]
    for k in range(1, REACH + 1):
        pair = ref[c, j, pl.ds(start + k, count), :] + ref[c, j, pl.ds(start - k, count), :]
        total = total + (pair if k == 1 else near_coef[k] * pair)
    return total


def slope(f, kin, pr, pi):
    upper_re = kin[0] + pr * f[2] - pi * f[3]
    upper_im = kin[1] + pr * f[3] + pi * f[2]
    lower_re = pr * f[0] + pi * f[1] - kin[2]
    lower_im = pr * f[1] - pi * f[0] - kin[3]
    return upper_im, upper_re, lower_im, lower_re


signs = (1.0, -1.0, 1.0, -1.0)


def chunks(rows, size=16):
    return [(r, min(size, rows - r)) for r in range(0, rows, size)]


def pipeline(steps, planes, w_ref, xys, together=False):
    def product(s, big):
        _, _, xy_start, rows, hi, lo, _ = steps[s]
        in_plane(big % 4, 1, up16(rows + 2 * xy_start), w_ref, hi, lo, xys[s % 2])

    if together:
        src, start, xy_start, rows, hi, lo, store = steps[0]
        in_plane(0, 4, up16(rows), w_ref, hi, lo, xys[0])
    else:
        product(0, 0)
    for s, (src, start, xy_start, rows, hi, lo, store) in enumerate(steps):
        margin = (planes + 32 - rows) // 2
        for i in range(8):
            if s == 0 and i in (0, 2, 4) and not together:
                product(0, i // 2 + 1)
            j = (2 * s + i) % 8
            for r, count in chunks(rows):
                f = [src[c, j, pl.ds(start + r, count), :] for c in range(4)]
                near = [
                    neighbours(src, xys[s % 2], c, j, start + r, xy_start + r, count)
                    for c in range(4)
                ]
                store(j, r, count, margin + r, f, near)
            if s + 1 < len(steps):
                for ahead in {4: (1,), 6: (2,), 7: (3, 4)}.get(i, ()):
                    product(s + 1, s + ahead)


def derivative(pd, j, row, count, f, near):
    pot, pr, pi = [pd[i, j, pl.ds(row, count), :] for i in range(3)]
    return slope(f, [unit_coef * near[c] + pot * f[c] for c in range(4)], pr, pi)


def stage_store(b0, pd, dst, factor, hi, lo, base=None):
    def store(j, r, count, row, f, near):
        if base is not None:
            row = pl.multiple_of(base + r, 8)
        k = derivative(pd, j, row, count, f, near)
        for c in range(4):
            value = b0[c, j, pl.ds(row + 8, count), :] + (signs[c] * factor) * k[c]
            place = r if base is None else row
            dst[c, j, pl.ds(place, count), :] = value
            put_split(value, c, j, place, hi, lo)

    return store


def place_rows(ref, channel, row, b0, pd, hi, lo, split_row):
    for i in range(ref.shape[0]):
        c = channel + i
        for j in range(8):
            value = ref[i, :, j * LANES : (j + 1) * LANES]
            if c < 4:
                b0[c, j, pl.ds(pl.multiple_of(row + 8, 8), ref.shape[1]), :] = value
                put_split(value, c, j, split_row, hi, lo)
            else:
                value = value + centre_coef if c == 4 else value
                pd[c - 4, j, pl.ds(row, ref.shape[1]), :] = value


def clear_rows(b0, row):
    for c in range(4):
        for j in range(8):
            b0[c, j, pl.ds(row, 8), :] = jnp.zeros((8, LANES), jnp.float32)


def add_share(past, b1, hi, lo, row, terms):
    scale = 0.5 * time_step * unit_coef
    for j in range(8):
        change = []
        for c in range(4):
            total = None
            for begin, sign in terms:
                for k in range(1, REACH + 1):
                    value = past[c, j, pl.ds(begin + sign * k, 8), :]
                    value = value if k == 1 else near_coef[k] * value
                    total = value if total is None else total + value
            change.append(scale * total)
        for c, delta in enumerate((change[1], -change[0], -change[3], change[2])):
            value = b1[c, j, pl.ds(row, 8), :] + delta
            b1[c, j, pl.ds(row, 8), :] = value
            put_split(value, c, j, row, hi, lo)


LEAD, TAIL = (4, -1), (16, 1)


def clear_past(past):
    zero = jnp.zeros((8, LANES), jnp.float32)
    for c in range(4):
        for j in range(8):
            past[c, j, 4:12, :] = zero
            past[c, j, 16:24, :] = zero


def first_kernel(pieces, planes, *refs):
    n = len(pieces)
    parts, w_ref = refs[:n], refs[n]
    b0, pd, b1, hi_b, lo_b, hi_a, lo_a, *xys = refs[n + 1 :]
    clear_rows(b0, 0)
    clear_rows(b0, planes + 40)
    for ref, row in zip(parts, pieces):
        place_rows(ref, 0, row, b0, pd, hi_a, lo_a, row)
    store = stage_store(b0, pd, b1, 0.5 * time_step, hi_b, lo_b)
    pipeline([(b0, 8, 0, planes + 32, hi_a, lo_a, store)], planes, w_ref, xys, True)


def early_kernel(planes, *refs):
    own, near, w_ref = refs[:3]
    b0, pd, b1, hi_b, lo_b, hi_a, lo_a, xy = refs[3:]
    odd = lax.rem(lax.axis_index("grid"), 2)
    base = pl.multiple_of((1 - odd) * planes, 16)
    clear_rows(b0, base)
    clear_rows(b0, pl.multiple_of(base + 2 * planes + 8, 8))
    for ref, side in ((own, odd), (near, 1 - odd)):
        inner = pl.multiple_of(side * planes, 16)
        place_rows(ref, 0, pl.multiple_of(base + inner, 16), b0, pd, hi_a, lo_a, inner)
    store = stage_store(b0, pd, b1, 0.5 * time_step, hi_b, lo_b, base)
    pipeline([(b0, base + 8, 0, 2 * planes, hi_a, lo_a, store)], planes, w_ref, [xy], True)


def late_kernel(planes, *refs):
    rims, far, mine, other, relayed = refs[:5]
    w_ref = refs[10]
    b0, pd, b1, hi_b, lo_b, hi_a, lo_a, past, *xys = refs[11:]
    odd = lax.rem(lax.axis_index("grid"), 2)
    half = lax.rem(lax.axis_index("modes"), 2)
    base = pl.multiple_of(odd * (2 * planes), 16)
    clear_rows(b0, pl.multiple_of(odd * (3 * planes + 8), 8))
    for c in range(4):
        for j in range(8):
            lanes = slice(j * LANES, (j + 1) * LANES)
            value = jnp.concatenate(
                [rims[c, :REACH, lanes], far[c, :, lanes], rims[c, REACH:, lanes]], axis=0
            )
            b0[c, j, pl.ds(pl.multiple_of(base + 8, 8), planes), :] = value
            put_split(value, c, j, 0, hi_a, lo_a)
    for ref, which in ((mine, half), (other, 1 - half)):
        row = pl.multiple_of(base + which * (planes // 2), 8)
        place_rows(ref, 4, row, b0, pd, hi_a, lo_a, 0)
    store = stage_store(b0, pd, b1, 0.5 * time_step, hi_b, lo_b, base)
    pipeline([(b0, base + 8, 0, planes, hi_a, lo_a, store)], planes, w_ref, xys, True)

    clear_past(past)
    for c in range(4):
        for j in range(8):
            lanes = slice(j * LANES, (j + 1) * LANES)
            ahead, behind = rims[c, REACH:, lanes], rims[c, :REACH, lanes]
            past[c, j, 0:REACH, :] = ahead
            past[c, j, 24 : 24 + REACH, :] = behind
    row = pl.multiple_of(planes + odd * (planes - 8), 8)
    side = (LEAD[0] + odd * (TAIL[0] - LEAD[0]), 2 * odd - 1)
    add_share(past, b1, hi_b, lo_b, row, (side,))
    add_far_share(past, b1, hi_b, lo_b, planes, relayed, REACH, relayed, 0)


def add_far_share(past, b1, hi, lo, planes, lead_ref, lead, tail_ref, tail):
    clear_past(past)
    for c in range(4):
        for j in range(8):
            lanes = slice(j * LANES, (j + 1) * LANES)
            past[c, j, 0:REACH, :] = lead_ref[c, lead : lead + REACH, lanes]
            past[c, j, 24 : 24 + REACH, :] = tail_ref[c, tail : tail + REACH, lanes]
    add_share(past, b1, hi, lo, 0, (LEAD,))
    add_share(past, b1, hi, lo, planes + 24, (TAIL,))


def stages_kernel(ends, planes, low_bits, *refs):
    n = 2 if ends else 0
    b0, pd = refs[n : n + 2]
    w_ref = refs[n + 5]
    psi1_ref, kin1_ref, sums_ref, b1, hi_b, lo_b = refs[n + 6 : n + 12]
    b2, b3, b4, hi_a, lo_a, past, *xys = refs[n + 12 :]
    quarter = lax.rem(lax.axis_index("modes"), low_bits)
    if ends:
        add_far_share(past, b1, hi_b, lo_b, planes, refs[0], 0, refs[1], 0)

    def last(j, r, count, row, f, near):
        k = derivative(pd, j, row, count, f, near)
        for c in range(4):
            early = (
                b1[c, j, pl.ds(r + 12, count), :]
                - b0[c, j, pl.ds(r + 20, count), :]
                + 2.0 * b2[c, j, pl.ds(r + 8, count), :]
                + f[c]
            )
            value = early * (1.0 / 3.0) + (signs[c] * time_step / 6.0) * k[c]
            b4[c, j, pl.ds(r, count), :] = value
            put_split(value, c, j, r, hi_a, lo_a)

    def finish(j, r, count, row, f, near):
        full = [unit_coef * near[c] + centre_coef * f[c] for c in range(4)]
        for c in range(4):
            psi1_ref[c, j, pl.ds(r, count), :] = f[c]
            kin1_ref[c, j, pl.ds(r, count), :] = full[c]
        sums = (
            f[2] * f[2] + f[3] * f[3],
            f[2] * full[2] + f[3] * full[3],
            f[0] * f[2] + f[1] * f[3],
            f[1] * f[2] - f[0] * f[3],
        )
        place = lax.bitwise_xor(jnp.int32(j // 2), quarter) if low_bits == 4 else j // 2
        for s in range(4):
            sums_ref[place, j % 2, s, pl.ds(r, count), :] = sums[s]

    second = stage_store(b0, pd, b2, 0.5 * time_step, hi_a, lo_a)
    third = stage_store(b0, pd, b3, time_step, hi_b, lo_b)
    steps = [
        (b1, 4, 4, planes + 24, hi_b, lo_b, second),
        (b2, 4, 4, planes + 16, hi_a, lo_a, third),
        (b3, 4, 4, planes + 8, hi_b, lo_b, last),
        (b4, 4, 4, planes, hi_a, lo_a, finish),
    ]
    pipeline(steps, planes, w_ref, xys)


def middle_kernel(paired, planes, low_bits, *refs):
    pieces = refs[:low_bits]
    psi1, kin1 = refs[low_bits : low_bits + 2]
    mid, first_send, second_send, fields_flat = refs[low_bits + 2 :]
    even = lax.rem(lax.axis_index("grid"), 2) == 0
    quarter = lax.rem(lax.axis_index("modes"), low_bits)
    per = 4 // low_bits
    for k in range(low_bits):
        for t in range(per):
            place = lax.bitwise_xor(quarter, k) * per + t
            for half in range(2):
                for i in range(4):
                    fields_flat[place, half, i] = pieces[k][t, half, i]

    for j in range(8):
        big, half = j // 2, j % 2
        now = [fields_flat[big, half, i] for i in range(3)]
        f = [psi1[c, j] for c in range(4)]
        q = slope(f, [kin1[c, j] + now[0] * f[c] for c in range(4)], now[1], now[2])
        for c in range(4):
            m = f[c] + (signs[c] * 0.5 * time_step) * q[c]
            mid[c, j] = m
            top, bottom = m[:REACH], m[planes - REACH :]
            if paired:
                a, b = jnp.where(even, top, bottom), jnp.where(even, bottom, top)
            else:
                a, b = top, bottom
            first_send[j, c * REACH : (c + 1) * REACH, :] = a
            second_send[j, c * REACH : (c + 1) * REACH, :] = b


def inner_kernel(planes, *refs):
    psi1, kin1, mid, fields_flat, w_ref, part_ref, fields_out, pad, hi, lo, xy = refs
    zero = jnp.zeros((8, LANES), jnp.float32)
    for j in range(8):
        for i in range(4):
            fields_out[i, :, j * LANES : (j + 1) * LANES] = fields_flat[j // 2, j % 2, i]
    for c in range(4):
        for j in range(8):
            value = mid[c, j]
            pad[c, j, 0:8, :] = zero
            pad[c, j, 8 : 8 + planes, :] = value
            pad[c, j, 8 + planes : 16 + planes, :] = zero
            put_split(value, c, j, 0, hi, lo)

    def store(j, r, count, row, m, near):
        pot, pr, pi = [fields_flat[j // 2, j % 2, i, pl.ds(r, count), :] for i in range(3)]
        f = [psi1[c, j, pl.ds(r, count), :] for c in range(4)]
        q1 = slope(f, [kin1[c, j, pl.ds(r, count), :] + pot * f[c] for c in range(4)], pr, pi)
        pot = pot + centre_coef
        q2 = slope(m, [unit_coef * near[c] + pot * m[c] for c in range(4)], pr, pi)
        for c in range(4):
            part_ref[c, j, pl.ds(r, count), :] = f[c] + (signs[c] * time_step / 6.0) * (
                q1[c] + 2.0 * q2[c]
            )

    pipeline([(pad, 8, 0, planes, hi, lo, store)], planes, w_ref, [xy])


def edge_kernel(paired, planes, *refs):
    part, first, second, u_ref, v_ref = refs
    even = lax.rem(lax.axis_index("grid"), 2) == 0
    scale = -0.5 * alpha_coef * 2.0 * time_step / 6.0
    terms = ((0, 1, 1.0), (1, 0, -1.0), (2, 3, -1.0), (3, 2, 1.0))
    for j in range(8):
        a, b = first[j], second[j]
        if paired:
            before, after = jnp.where(even, a, b), jnp.where(even, b, a)
        else:
            before, after = b, a
        for out, src, sign in terms:
            lo_rows = before[src * REACH : (src + 1) * REACH]
            hi_rows = after[src * REACH : (src + 1) * REACH]
            lead, tail = [], []
            for r in range(REACH):
                lead.append(
                    sum(
                        stencil_coef[k] * lo_rows[r - k + REACH : r - k + REACH + 1]
                        for k in range(r + 1, REACH + 1)
                    )
                )
                tail.append(
                    sum(
                        stencil_coef[k] * hi_rows[r + k - REACH : r + k - REACH + 1]
                        for k in range(REACH - r, REACH + 1)
                    )
                )
            value = part[out, j]
            parts = [value[:REACH] + (sign * scale) * jnp.concatenate(lead, axis=0)]
            if planes > 2 * REACH:
                parts.append(value[REACH : planes - REACH])
            parts.append(value[planes - REACH :] + (sign * scale) * jnp.concatenate(tail, axis=0))
            ref = u_ref if out < 2 else v_ref
            ref[0, out % 2, :, j * LANES : (j + 1) * LANES] = jnp.concatenate(parts, axis=0)


def potentials(raw, modes_total):
    density = 2.0 * raw[:, :, 0] / modes_total
    kinetic = (-2.0 / kinetic_coef) * raw[:, :, 1] / modes_total
    anomal_re = raw[:, :, 2] / modes_total
    anomal_im = raw[:, :, 3] / modes_total
    dense_safe = density + epsilon
    fermi = 0.5 * jnp.power(3.0 * jnp.pi**2 * dense_safe, 2.0 / 3.0)
    anomal_sq = anomal_re * anomal_re + anomal_im * anomal_im
    third_root = jnp.power(dense_safe, -1.0 / 3.0)
    field_pot = beta_coef * fermi - gamma_coef / 3.0 * anomal_sq * third_root / dense_safe
    pair_re = -gamma_coef * anomal_re * third_root
    pair_im = -gamma_coef * anomal_im * third_root
    energy = (
        alpha_coef * kinetic / 2.0
        + 0.6 * beta_coef * dense_safe * fermi
        + gamma_coef * anomal_sq * third_root
    )
    return jnp.stack([field_pot, pair_re, pair_im, energy], axis=2)


def call(kernel, outs, scratch, args, aliases=None):
    vmem = pl.BlockSpec(memory_space=pltpu.VMEM)
    shapes = [o if isinstance(o[0], tuple) else (o, jnp.float32) for o in outs]
    flops = 2 * sum(int(np.prod(s)) for s, d in shapes)
    return pl.pallas_call(
        kernel,
        out_shape=tuple(jax.ShapeDtypeStruct(s, d) for s, d in shapes),
        in_specs=[vmem] * len(args),
        out_specs=tuple([vmem] * len(outs)),
        scratch_shapes=[pltpu.VMEM(s, d) for s, d in scratch],
        input_output_aliases=aliases or {},
        compiler_params=pltpu.CompilerParams(vmem_limit_bytes=32 << 20),
        cost_estimate=pl.CostEstimate(flops=1000 * flops, bytes_accessed=4 * flops, transcendentals=0),
    )(*args)


def exchange_xor(x, axis, bits, count):
    return lax.ppermute(x, axis, [(i, i ^ bits) for i in range(count)])


def local(u_modes, v_modes, potential, pairing):
    planes = u_modes.shape[2]
    slabs = lax.axis_size("grid")
    modes = lax.axis_size("modes")
    low_bits = 4 if modes % 4 == 0 else 1
    paired = slabs == 4 and planes == 16 and low_bits == 4
    f32, bf16 = jnp.float32, jnp.bfloat16
    weights = jnp.asarray(in_plane_matrix())
    own = jnp.concatenate([u_modes[0], v_modes[0], potential[None], pairing], axis=0)
    own = lax.optimization_barrier(own)
    tall = up16(planes + 32)
    state = (4, 8, planes, LANES)
    split = ((4, 4, tall, WINDOW), bf16)
    product = ((4, 4, 2, tall, LANES), f32)
    past = ((4, 8, 32, LANES), f32)
    buffers = [
        (4, 8, tall + 16, LANES),
        (3, 8, tall, LANES),
        (4, 8, tall + 8, LANES),
        split,
        split,
    ]

    cross = [(i, (i - 1 if i % 2 == 0 else i + 1) % slabs) for i in range(slabs)]
    up = [(i, (i + 1) % slabs) for i in range(slabs)]
    down = [(j, i) for i, j in up]
    if paired:
        part = planes // 2
        upper = lax.rem(lax.axis_index("modes"), 2) == 1
        picked = jnp.where(upper, own[4:, part:], own[4:, :part])
        mine = lax.ppermute(picked, "grid", cross)
        rims = jnp.concatenate([own[:4, :REACH], own[:4, planes - REACH :]], axis=1)
        rims = lax.ppermute(rims, "grid", cross)
        far = lax.ppermute(own[:4, REACH : planes - REACH], "grid", cross)
        near = exchange_xor(own, "grid", 1, slabs)
        other = exchange_xor(mine, "modes", 1, modes)
        ready = call(functools.partial(early_kernel, planes), buffers, [split, split, product], [own, near, weights])
        relayed = exchange_xor(rims, "grid", 1, slabs)
        far, other, relayed = lax.optimization_barrier((far, other, relayed))
        ends = []
        b0, pd, b1, hi, lo = call(
            functools.partial(late_kernel, planes),
            buffers,
            [split, split, past, product],
            [rims, far, mine, other, relayed, *ready, weights],
            {5 + i: i for i in range(5)},
        )
    else:
        pieces, arrays = [16], [own]
        reach, step = 0, 0
        while reach < 5 * REACH:
            step += 1
            count = min(planes, 5 * REACH - reach)
            wide = 7 if reach < 4 * REACH else 4
            before = lax.ppermute(
                own[:wide, planes - count :], "grid", [(i, (i + step) % slabs) for i in range(slabs)]
            )
            after = lax.ppermute(
                own[:wide, :count], "grid", [((i + step) % slabs, i) for i in range(slabs)]
            )
            if wide == 7:
                pieces += [16 - reach - count, 16 + planes + reach]
                arrays += [before, after]
            else:
                ends = [before, after]
            reach += count
        b0, pd, b1, hi, lo = call(
            functools.partial(first_kernel, pieces, planes), buffers, [split, split, product], arrays + [weights]
        )

    inputs = [*ends, b0, pd, b1, hi, lo, weights]
    psi1, kin1, sums, *rest = call(
        functools.partial(stages_kernel, bool(ends), planes, low_bits),
        [state, state, (4, 2, 4, planes, LANES), b1.shape, split, split],
        [
            ((4, 8, tall + 8, LANES), f32),
            ((4, 8, tall + 8, LANES), f32),
            ((4, 8, tall + 8, LANES), f32),
            split,
            split,
            past,
            product,
            product,
        ],
        inputs,
        {len(ends) + 2 + i: 3 + i for i in range(3)},
    )

    if low_bits == 4:
        total = sums[0:1]
        for k in (1, 2, 3):
            got = exchange_xor(sums[k : k + 1], "modes", k, modes)
            total = total + got
    else:
        total = sums
    bits = low_bits
    while bits < modes:
        total = total + exchange_xor(total, "modes", bits, modes)
        bits *= 2
    quarter = potentials(total, float(u_modes.shape[0] * modes))
    got = [quarter]
    for k in range(1, low_bits):
        got.append(exchange_xor(quarter, "modes", k, modes))

    edge = (8, 4 * REACH, LANES)
    mid, first, second, fields_flat = call(
        functools.partial(middle_kernel, paired, planes, low_bits),
        [state, edge, edge, (4, 2, 4, planes, LANES)],
        [],
        got + [psi1, kin1],
    )
    if paired:
        first = lax.ppermute(first, "grid", cross)
        second = exchange_xor(second, "grid", 1, slabs)
    else:
        first = lax.ppermute(first, "grid", down)
        second = lax.ppermute(second, "grid", up)
    flat = up16(planes)
    part, fields = call(
        functools.partial(inner_kernel, planes),
        [state, (4, planes, NX * NY)],
        [
            ((4, 8, flat + 16, LANES), f32),
            ((4, 4, flat, WINDOW), bf16),
            ((4, 4, flat, WINDOW), bf16),
            ((4, 4, 2, flat, LANES), f32),
        ],
        [psi1, kin1, mid, fields_flat, weights],
    )
    u_next, v_next = call(
        functools.partial(edge_kernel, paired, planes), [u_modes.shape, v_modes.shape], [], [part, first, second]
    )
    return u_next, v_next, fields


def solution(mesh):
    wide = P("modes", None, "grid", None)
    return jax.shard_map(
        local,
        mesh=mesh,
        in_specs=(wide, wide, P("grid", None), P(None, "grid", None)),
        out_specs=(wide, wide, P(None, "grid", None)),
        check_vma=False,
    )
```
